256 devices in a mesh: mode: 8 (over y, core), blk: 32 (over z, x).
Axes of the slice: x: 4, y: 4, z: 8, core: 2. Of those that a mesh axis runs over, the one named last changes fastest.
Arguments:
- divergence: float32 [32, 32, 128, 1024], P('blk', None, 'mode')
- neighbours: int32 [32, 2], P('blk'), may hold values from -1 to 31, as said below
- levels: int32 [32], P('blk'), may hold values from 0 to 2
- sweeps: int32 [3], replicated, may hold values from 1 to 2, as said below
Outputs:
- pressure: float32 [32, 32, 128, 1024], P('blk', None, 'mode')
The draws below stay inside these ranges and needn't reach their ends.
Inputs may be any that keep to these rules, and one draw needn't show every extreme that they name: `neighbours`: row b holds the slots of the columns west (entry 0) and east (entry 1) of the column in slot b along x, -1 beyond the two ends of the 32 columns. The lists are mutual, every slot is named, and every neighbour's slot lies within 3 of b, exactly 3 away for some. Some level has 2 sweeps.
All inputs are finite; a program needn't handle non-finite values.
Results may differ from the reference program's by a relative error of at most 0.0003.
Values sent between devices are 32-bit elements; how exact they have to be, the bound alone decides.
No kernel may reach another device: no remote copies, remote signals or barrier semaphores. Data moves between devices by JAX's collectives and lax.ppermute only.
A program may use at most 128 MiB of HBM per device.

```python
import math
import jax
import jax.numpy as jnp
from jax import lax

NY = 1024
BX = 32
NZ = 128
SWEEPS = 2
LEVELS = 3
CITERS = 8
COLS = 32
N_MODE = 8


def draw_divergence(key, part):
    shape = (COLS, BX, NZ, NY)
    return jax.random.normal(key, shape, jnp.float32)


def draw_neighbours(key, part):
    pair_count = COLS // 2
    swapped = jax.random.randint(key, (pair_count,), 0, 2).astype(jnp.int32)
    forced = jax.random.randint(jax.random.fold_in(key, 3), (), 0, pair_count - 1).astype(jnp.int32)
    group_ids = jnp.arange(pair_count, dtype=jnp.int32)
    swapped = jnp.where((group_ids == forced) | (group_ids == forced + 1), 1, swapped).astype(jnp.int32)
    positions = jnp.arange(COLS, dtype=jnp.int32)
    slot_of = 2 * (positions // 2) + (positions % 2 ^ swapped[positions // 2])
    west_pos = positions - 1
    east_pos = positions + 1
    west_slot = jnp.where(west_pos >= 0, slot_of[jnp.clip(west_pos, 0, COLS - 1)], -1)
    east_slot = jnp.where(east_pos < COLS, slot_of[jnp.clip(east_pos, 0, COLS - 1)], -1)
    table = jnp.zeros((COLS, 2), jnp.int32)
    table = table.at[slot_of, 0].set(west_slot.astype(jnp.int32))
    table = table.at[slot_of, 1].set(east_slot.astype(jnp.int32))
    return table


def draw_sweeps(key, part):
    counts = jax.random.randint(key, (LEVELS,), 1, SWEEPS + 1).astype(jnp.int32)
    chosen = jax.random.randint(jax.random.fold_in(key, 5), (), 0, LEVELS).astype(jnp.int32)
    return jnp.where(jnp.arange(LEVELS, dtype=jnp.int32) == chosen, SWEEPS, counts).astype(jnp.int32)


def with_ends(array, stream_key, least, top_value):
    longest = array.shape.index(max(array.shape))
    spots = []
    for shift in (0, 1):
        where = [jax.random.randint(jax.random.fold_in(stream_key, axis), (), 0, length) for axis, length in enumerate(array.shape)]
        where[longest] = (where[longest] + shift) % array.shape[longest]
        spots.append(tuple(where))
    return array.at[spots[0]].set(least).at[spots[1]].set(top_value)


def setup_inputs(seed: int = 0) -> dict:
    arg_keys = jax.random.split(jax.random.key(seed), 5)
    divergence = draw_divergence(jax.random.fold_in(arg_keys[4], 71), 0)
    neighbours = draw_neighbours(jax.random.fold_in(arg_keys[4], 71), 0)
    levels = with_ends(jax.random.randint(arg_keys[2], (COLS,), 0, LEVELS), jax.random.fold_in(arg_keys[2], 1), 0, LEVELS - 1).astype(jnp.int32)
    sweeps = draw_sweeps(jax.random.fold_in(arg_keys[4], 71), 0)
    return {"divergence": divergence, "neighbours": neighbours, "levels": levels, "sweeps": sweeps}


PRECISE = lax.Precision.HIGHEST
DAMPING = 0.8

def sine_table(extent):
    ordinal = jnp.arange(extent, dtype=jnp.int32) + 1
    phases = ordinal[:, None] * ordinal[None, :] % (2 * (extent + 1))
    angles = phases.astype(jnp.float32) * (math.pi / (extent + 1))
    matrix = math.sqrt(2.0 / (extent + 1)) * jnp.sin(angles)
    spectrum = 2.0 - 2.0 * jnp.cos(ordinal.astype(jnp.float32) * (math.pi / (extent + 1)))
    return (matrix.astype(jnp.float32), spectrum.astype(jnp.float32))

def fourier_table(length):
    half_len = length // 2
    row_ids = jnp.arange(length, dtype=jnp.int32)
    wavenumber = jnp.where(row_ids <= half_len, row_ids, row_ids - half_len)
    phases = wavenumber[:, None] * row_ids[None, :] % length
    angles = phases.astype(jnp.float32) * (2.0 * math.pi / length)
    fourier = jnp.where((row_ids <= half_len)[:, None], jnp.cos(angles), jnp.sin(angles)).astype(jnp.float32)
    edges = (row_ids == 0) | (row_ids == half_len)
    weights = jnp.where(edges, 1.0 / length, 2.0 / length).astype(jnp.float32)
    wave_shift = (2.0 - 2.0 * jnp.cos(wavenumber.astype(jnp.float32) * (2.0 * math.pi / length))).astype(jnp.float32)
    return (fourier, weights, wave_shift)

def stiffness_of(levels):
    return jnp.left_shift(jnp.ones_like(levels), 2 * levels).astype(jnp.float32)

def local_solve(loaded, stiffness, wave_shift, tables):
    sine_x, lambda_x, sine_z, lambda_z = tables
    transformed = jnp.einsum('bxzq,xi->bizq', loaded, sine_x, precision=PRECISE)
    transformed = jnp.einsum('bizq,zj->bijq', transformed, sine_z, precision=PRECISE)
    divisor = stiffness[:, None, None, None] * (lambda_x[None, :, None, None] + lambda_z[None, None, :, None]) + wave_shift[None, None, None, :]
    transformed = transformed / divisor
    transformed = jnp.einsum('bijq,ix->bxjq', transformed, sine_x, precision=PRECISE)
    return jnp.einsum('bxjq,jz->bxzq', transformed, sine_z, precision=PRECISE)

def apply_local(iterate, stiffness, wave_shift):
    padded_x = jnp.pad(iterate, ((0, 0), (1, 1), (0, 0), (0, 0)))
    padded_z = jnp.pad(iterate, ((0, 0), (0, 0), (1, 1), (0, 0)))
    laplace = 4.0 * iterate - padded_x[:, 2:] - padded_x[:, :-2] - padded_z[:, :, 2:] - padded_z[:, :, :-2]
    return stiffness[:, None, None, None] * laplace + wave_shift * iterate

def boundary(iterate, neighbours):
    west_slot = neighbours[:, 0]
    east_slot = neighbours[:, 1]
    west_present = (west_slot >= 0).astype(jnp.float32)[:, None, None]
    east_present = (east_slot >= 0).astype(jnp.float32)[:, None, None]
    from_west = jnp.take(iterate[:, -1], jnp.maximum(west_slot, 0), axis=0) * west_present
    from_east = jnp.take(iterate[:, 0], jnp.maximum(east_slot, 0), axis=0) * east_present
    return (from_west, from_east)

def loaded_rhs(source, from_west, from_east, stiffness):
    factor = stiffness[:, None, None]
    loaded = source.at[:, 0].add(factor * from_west)
    return loaded.at[:, -1].add(factor * from_east)

def neighbour_sum(values, neighbours):
    west_slot = neighbours[:, 0]
    east_slot = neighbours[:, 1]
    west_present = (west_slot >= 0).astype(jnp.float32)[:, None]
    east_present = (east_slot >= 0).astype(jnp.float32)[:, None]
    return jnp.take(values, jnp.maximum(west_slot, 0), axis=0) * west_present + jnp.take(values, jnp.maximum(east_slot, 0), axis=0) * east_present

def coarse_terms(stiffness, wave_shift):
    diagonal = stiffness[:, None] * float(2 * NZ + 2 * BX) + float(BX * NZ) * wave_shift[None, :]
    coupling = stiffness[:, None] * float(NZ)
    return (diagonal, coupling)

def reference(divergence, neighbours, levels, sweeps):
    fourier, weights, wave_shift = fourier_table(NY)
    tables = sine_table(BX) + sine_table(NZ)
    stiffness = stiffness_of(levels)
    allowed = jnp.take(sweeps, levels)
    spectrum = jnp.einsum('bxzy,qy->bxzq', divergence, fourier, precision=PRECISE)
    share = NY // N_MODE
    blocks = NY // share
    spectrum = jnp.moveaxis(spectrum.reshape(COLS, BX, NZ, blocks, share), 3, 0)
    shifts = wave_shift.reshape(blocks, share)

    def smooth(iterate, source, own_shift):
        for repeat in range(SWEEPS):
            from_west, from_east = boundary(iterate, neighbours)
            solved = local_solve(loaded_rhs(source, from_west, from_east, stiffness), stiffness, own_shift, tables)
            iterate = jnp.where((allowed > repeat)[:, None, None, None], solved, iterate)
        return iterate

    def cycle(block_pair):
        source, own_shift = block_pair
        iterate = smooth(jnp.zeros_like(source), source, own_shift)
        from_west, from_east = boundary(iterate, neighbours)
        remainder = loaded_rhs(source, from_west, from_east, stiffness) - apply_local(iterate, stiffness, own_shift)
        coarse_rhs = lax.optimization_barrier(jnp.sum(remainder, axis=(1, 2)))
        diagonal, coupling = coarse_terms(stiffness, own_shift)
        correction = jnp.zeros_like(coarse_rhs)
        for repeat in range(CITERS):
            beside = neighbour_sum(correction, neighbours)
            correction = correction + DAMPING * (coarse_rhs - diagonal * correction + coupling * beside) / diagonal
        iterate = iterate + correction[:, None, None, :]
        return smooth(iterate, source, own_shift)
    solved_blocks = lax.map(cycle, (spectrum, shifts))
    solution = jnp.moveaxis(solved_blocks, 0, 3).reshape(COLS, BX, NZ, NY)
    return jnp.einsum('bxzq,qy->bxzy', solution * weights, fourier, precision=PRECISE)
```

```python
import functools
import math

import jax
import jax.numpy as jnp
import numpy as np
from jax import lax
from jax.experimental import pallas as pl
from jax.experimental.pallas import tpu as pltpu
from jax.sharding import PartitionSpec as P

NY = 1024
BX = 32
NZ = 128
CITERS = 8
DAMPING = 0.8
REACH = 3
BLOCKS = 8
ROWS = NZ // BLOCKS
DEVICES = 256
F32 = jnp.float32
BF16 = jnp.bfloat16


def sine_table(extent):
    ordinal = np.arange(1, extent + 1)
    angles = np.pi * np.outer(ordinal, ordinal) / (extent + 1)
    matrix = np.sqrt(2.0 / (extent + 1)) * np.sin(angles)
    return matrix, 4.0 * np.sin(np.pi * ordinal / (2 * (extent + 1))) ** 2


def two_terms(array):
    high = np.asarray(array, np.float32).astype(BF16)
    low = (np.asarray(array, np.float64) - high.astype(np.float64)).astype(BF16)
    return high, low


def fourier_class(length, cosines, sines):
    y = np.arange(length)
    columns = []
    for waves, function in ((cosines, np.cos), (sines, np.sin)):
        for m in waves:
            weight = (1.0 if m in (0, NY // 2) else 2.0) / NY
            columns.append(math.sqrt(weight) * function(2 * np.pi * ((m * y) % NY) / NY))
    waves = np.concatenate((np.array(cosines), np.array(sines)))
    return np.stack(columns, axis=1), 4.0 * np.sin(np.pi * waves / NY) ** 2


SX, LX = sine_table(BX)
SB, LB = sine_table(ROWS)
SZ, LZ = sine_table(NZ)
IX = np.concatenate((np.arange(0, BX, 2), np.arange(1, BX, 2)))
JB = np.concatenate((np.arange(0, ROWS, 2), np.arange(1, ROWS, 2)))
T0, K0 = fourier_class(256, range(0, 513, 4), range(4, 512, 4))
T2, K2 = fourier_class(256, range(2, 512, 4), range(2, 512, 4))
T1, K1 = fourier_class(512, range(1, 512, 2), range(1, 512, 2))
KQ = np.concatenate((K0, K2, K1))


def plane_table(parity):
    ways = SX[IX[16 * parity : 16 * parity + 16], :16]
    return np.einsum("ix,jz->ijxz", ways, SB[JB]).reshape(256, 256)


PLANE = np.stack((plane_table(0), plane_table(1)))
ROW_LAMBDA = (LX[IX][:, None] + LB[JB][None, :]).reshape(512, 1)
ZBASIS = np.einsum("jmz,kz->jmk", SZ.reshape(NZ, BLOCKS, ROWS), SB[JB]).reshape(NZ, NZ)
ZSUM = SZ.sum(axis=0).reshape(NZ, 1)


def link_tables():
    scale = np.zeros((2, 4, 32, 4, 2, 16))
    lam = np.zeros((2, 4, 32, 4, 2, 16))
    for half in range(2):
        for q in range(4):
            for a in range(32):
                lam[half, q, a] = LX[IX[a]] + LB[JB][None, None, :]
                for b in range(8 * half, 8 * half + 8):
                    scale[half, q, a, q, a // 16, b] = SX[0, IX[a]] * SB[0, JB[b]]
    return scale.reshape(256, 128), lam.reshape(256, 128)


LINK_SCALE, LINK_LAMBDA = link_tables()
KQ_OWN = np.repeat(KQ.reshape(4, DEVICES).T, 32, axis=1).reshape(DEVICES, 1, 128)


def halves(value):
    high = value.astype(BF16)
    return high, (value - high.astype(F32)).astype(BF16)


def dot3(a, b, dims=(((1,), (0,)), ((), ()))):
    ah, al = a
    bh, bl = b
    mul = functools.partial(lax.dot_general, dimension_numbers=dims, preferred_element_type=F32)
    return mul(ah, bh) + mul(ah, bl) + mul(al, bh)


NT = (((1,), (1,)), ((), ()))
TN = (((0,), (0,)), ((), ()))


def stiffness_scalar(level):
    return lax.shift_left(jnp.int32(1), 2 * level).astype(F32)


def forward_kernel(
    levels, neighbours, sweeps, xa, xb, plane_h, plane_l, t0h, t0l, t2h, t2l, t1h, t1l,
    row_lambda, kq, out, w_out, yh, yl, features,
):
    step = pl.program_id(0)
    for k in range(4):
        a, b = xa[k], xb[3 - k]
        rows = pl.ds(pl.multiple_of((4 * step + k) * 16, 16), 16)
        for parity, v in ((0, a + b), (1, a - b)):
            v0, v1, v2, v3 = (v[:, 256 * n : 256 * n + 256] for n in range(4))
            e0, e1 = v0 + v2, v1 + v3
            for n, part in enumerate((e0 + e1, e0 - e1, v0 - v2, v1 - v3)):
                high, low = halves(part)
                yh[parity, rows, 256 * n : 256 * n + 256] = high
                yl[parity, rows, 256 * n : 256 * n + 256] = low

    @pl.when(step == pl.num_programs(0) - 1)
    def _():
        level = levels[0]
        stiffness = stiffness_scalar(level)
        for parity in range(2):
            plane = (plane_h[parity], plane_l[parity])
            z = []
            for n in range(4):
                cut = slice(256 * n, 256 * n + 256)
                z.append(halves(dot3(plane, (yh[parity, :, cut], yl[parity, :, cut]))))
            odd = tuple(jnp.concatenate((z[2][h], z[3][h]), axis=1) for h in range(2))
            base = stiffness * row_lambda[256 * parity : 256 * parity + 256]
            for q in range(4):
                if q == 0:
                    g = dot3(z[0], (t0h[...], t0l[...]))
                elif q == 1:
                    g = dot3(z[1], (t2h[...], t2l[...]))
                else:
                    cut = slice(256 * (q - 2), 256 * (q - 2) + 256)
                    g = dot3(odd, (t1h[:, cut], t1l[:, cut]))
                w = g / (base + kq[:, 256 * q : 256 * q + 256])
                w_out[256 * parity : 256 * parity + 256, 256 * q : 256 * q + 256] = w
                wb = w.reshape(16, 2, 8, 256)
                place = slice(32 * q + 16 * parity, 32 * q + 16 * parity + 16)
                iota = lax.broadcasted_iota(jnp.int32, (8, 256), 0)
                for half in range(2):
                    first = jnp.zeros((8, 256), F32)
                    for b in range(8):
                        first = jnp.where(iota == b, np.float32(SB[0, JB[8 * half + b]]), first)
                    features[half, place, :] = jnp.sum(wb[:, half] * first[None], axis=1)
                total = np.float32(SX[0, IX[16 * parity]]) * w[:16]
                for a in range(1, 16):
                    total = total + np.float32(SX[0, IX[16 * parity + a]]) * w[16 * a : 16 * a + 16]
                features[2, place, :] = total
        for kind in range(3):
            out[pl.ds(kind, DEVICES, stride=4), :] = features[kind].T
        lane = lax.broadcasted_iota(jnp.int32, (DEVICES, 128), 1)
        meta = jnp.zeros((DEVICES, 128), F32)
        facts = (
            stiffness,
            sweeps[level].astype(F32),
            neighbours[0, 0].astype(F32),
            neighbours[0, 1].astype(F32),
        )
        for n, fact in enumerate(facts):
            meta = jnp.where(lane == n, fact, meta)
        out[pl.ds(3, DEVICES, stride=4), :] = meta


def end_responses(shift, extent):
    half = 0.5 * shift
    ratio = 1.0 / (1.0 + half + jnp.sqrt(half * (half + 2.0)))
    square = ratio * ratio
    power = ratio
    for _ in range(extent.bit_length() - 1):
        power = power * power
    rest = power * power
    below = 1.0 / (1.0 - rest * square)
    return ratio * (1.0 - rest) * below, power * (1.0 - square) * below


def column_kernel(
    own, inbox, k_own, lam_x, lam_z, link_scale, link_lambda, zbasis_h, zbasis_l, zsum,
    out, x_links, t_faces,
):
    del own
    k_row = k_own[0]
    meta = inbox[pl.ds(3, 32, stride=4), :]
    stiff_col = meta[:, 0:1]
    easing_col = 1.0 / stiff_col

    near, far = end_responses(lam_x[...] + k_row * easing_col, ROWS)
    passing, held = [], []
    carry = jnp.zeros((32, 128), F32)
    for m in range(BLOCKS):
        held.append((carry, 1.0 / (1.0 - near * carry)))
        carry = near + far * far * carry * held[-1][1]

    def interfaces(even, odd):
        firsts, offsets = [], []
        offset = jnp.zeros((32, 128), F32)
        for m in range(BLOCKS):
            ratio, scale = held[m]
            first, last = even[m] + odd[m], even[m] - odd[m]
            pushed = (first + near * offset) * scale
            offsets.append(offset)
            firsts.append(pushed)
            offset = last + far * (offset + ratio * pushed)
        above = jnp.zeros((32, 128), F32)
        sides = [None] * BLOCKS
        for m in reversed(range(BLOCKS)):
            ratio, scale = held[m]
            head = firsts[m] + far * scale * above
            below = ratio * head + offsets[m]
            sides[m] = (below + above, below - above)
            above = head
        return sides

    def received(kind, m):
        return inbox[pl.ds(128 * m + kind, 32, stride=4), :]

    even = [received(0, m) for m in range(BLOCKS)]
    odd = [received(1, m) for m in range(BLOCKS)]
    sides = interfaces(even, odd)
    for m in range(BLOCKS):
        x_links[32 * m : 32 * m + 32, 0:128] = sides[m][0]
        x_links[32 * m : 32 * m + 32, 128:256] = sides[m][1]

    links = [
        halves(link_scale[...] / (link_lambda[...] + k_row * np.float32(0.25**level)))
        for level in range(3)
    ]
    stiff_rows = jnp.concatenate([stiff_col] * BLOCKS, axis=0)
    hits = [stiff_rows == np.float32(4.0**level) for level in range(3)]
    x_all = x_links[...]
    faces = jnp.concatenate([received(2, m) for m in range(BLOCKS)], axis=0)
    for level in range(3):
        faces = faces + dot3(halves(jnp.where(hits[level], x_all, 0.0)), links[level])

    turned = faces.T
    for m in range(BLOCKS):
        for parity in range(2):
            t_faces[16 * m : 16 * m + 16, 128 * parity : 128 * parity + 128] = jnp.concatenate(
                [
                    turned[32 * q + 16 * parity : 32 * q + 16 * parity + 16, 32 * m : 32 * m + 32]
                    for q in range(4)
                ],
                axis=1,
            )
    zbasis = (zbasis_h[...], zbasis_l[...])
    modes = dot3(zbasis, halves(t_faces[...]))
    west_end = modes[:, :128] + modes[:, 128:]
    east_end = modes[:, :128] - modes[:, 128:]

    meta_t = meta.T
    facts = jnp.concatenate([meta_t[0:8]] * 4, axis=1)
    stiff, allowed = facts[0:1], facts[1:2]
    west_slot, east_slot = facts[2:3], facts[3:4]
    lane = lax.broadcasted_iota(jnp.int32, (1, 128), 1)
    column = (lane % 32).astype(F32)
    offsets = [o for o in range(-REACH, REACH + 1) if o != 0]
    west_hits = [
        ((west_slot >= 0.0) & (column - west_slot == np.float32(o))).astype(F32) for o in offsets
    ]
    east_hits = [
        ((east_slot >= 0.0) & (column - east_slot == np.float32(o))).astype(F32) for o in offsets
    ]

    def shifted(value, hits_by_offset):
        parts = [
            pltpu.roll(value, o % 128, 1) * hit for o, hit in zip(offsets, hits_by_offset)
        ]
        return ((parts[0] + parts[1]) + (parts[2] + parts[3])) + (parts[4] + parts[5])

    def exchange(first, last):
        return shifted(last, west_hits), shifted(first, east_hits)

    face_near, face_far = end_responses(lam_z[...] + k_row / stiff, BX)
    twice = (allowed > 1.0).astype(F32)
    west1, east1 = exchange(west_end, east_end)
    west1, east1 = west1 * twice, east1 * twice
    first = west_end + face_near * west1 + face_far * east1
    last = east_end + face_far * west1 + face_near * east1
    west2, east2 = exchange(first, last)
    moved = (west2 - west1) + (east2 - east1)
    coarse = stiff * jnp.sum(moved * zsum[...], axis=0, keepdims=True)
    diagonal = stiff * np.float32(2 * NZ + 2 * BX) + np.float32(BX * NZ) * k_row
    target = jnp.broadcast_to(coarse / diagonal, (8, 128))
    coupling = stiff * np.float32(NZ) / diagonal
    both_hits = [coupling * (w + e) for w, e in zip(west_hits, east_hits)]
    correction = DAMPING * target
    for _ in range(CITERS - 1):
        beside = shifted(correction, both_hits)
        correction = correction + DAMPING * (target - correction + beside)
    correction = correction[0:1]
    west3 = west2 + zsum[...] * shifted(correction, west_hits)
    east3 = east2 + zsum[...] * shifted(correction, east_hits)
    first = west_end + face_near * west3 + face_far * east3
    last = east_end + face_far * west3 + face_near * east3
    west4, east4 = exchange(first, last)
    again = twice > 0.0
    west = jnp.where(again, west4, west3)
    east = jnp.where(again, east4, east3)
    sums = jnp.concatenate((west + east, west - east), axis=1)
    t_faces[...] = dot3(zbasis, halves(sums), TN)

    turned = jnp.concatenate(
        [
            jnp.concatenate(
                [
                    t_faces[16 * m : 16 * m + 16, 128 * parity + 32 * q : 128 * parity + 32 * q + 32]
                    for q in range(4)
                    for parity in range(2)
                ],
                axis=0,
            )
            for m in range(BLOCKS)
        ],
        axis=1,
    )
    faces = turned.T
    for m in range(BLOCKS):
        out[pl.ds(128 * m + 2, 32, stride=4), :] = faces[32 * m : 32 * m + 32]
    driven = jnp.zeros((256, 256), F32)
    for level in range(3):
        driven = driven + dot3(halves(jnp.where(hits[level], faces, 0.0)), links[level], NT)
    sides = interfaces(
        [even[m] + driven[32 * m : 32 * m + 32, 0:128] for m in range(BLOCKS)],
        [odd[m] + driven[32 * m : 32 * m + 32, 128:256] for m in range(BLOCKS)],
    )
    for m in range(BLOCKS):
        for kind in range(2):
            out[pl.ds(128 * m + kind, 32, stride=4), :] = sides[m][kind]
        out[pl.ds(128 * m + 3, 32, stride=4), :] = jnp.zeros((32, 128), F32)


def backward_kernel(
    levels, inbox, w_in, plane_h, plane_l, t0h, t0l, t2h, t2l, t1h, t1l, row_lambda, kq,
    out, features, rh, rl,
):
    easing = 1.0 / stiffness_scalar(levels[0])
    for kind in range(3):
        features[kind] = inbox[pl.ds(kind, DEVICES, stride=4), :].T
    iota = lax.broadcasted_iota(jnp.int32, (8, 256), 0)
    firsts = []
    for half in range(2):
        first = jnp.zeros((8, 256), F32)
        for b in range(8):
            first = jnp.where(iota == b, np.float32(SB[0, JB[8 * half + b]]), first)
        firsts.append(first)
    for parity in range(2):
        rows = slice(256 * parity, 256 * parity + 256)
        parts = []
        for q in range(4):
            cut = slice(256 * q, 256 * q + 256)
            place = slice(32 * q + 16 * parity, 32 * q + 16 * parity + 16)
            response = 1.0 / (row_lambda[rows] + kq[:, cut] * easing)
            ends = [features[half, place, :] for half in range(2)]
            side = features[2, place, :]
            pieces = []
            for a in range(16):
                face = np.float32(SX[0, IX[16 * parity + a]]) * side
                for half in range(2):
                    pieces.append(
                        firsts[half] * ends[half][a : a + 1] + face[8 * half : 8 * half + 8]
                    )
            u = w_in[rows, cut] + response * jnp.concatenate(pieces, axis=0)
            parts.append(halves(u))
        odd = tuple(jnp.concatenate((parts[2][h], parts[3][h]), axis=1) for h in range(2))
        ee = dot3(parts[0], (t0h[...], t0l[...]), NT)
        eo = dot3(parts[1], (t2h[...], t2l[...]), NT)
        o = dot3(odd, (t1h[...], t1l[...]), NT)
        total, difference = ee + eo, ee - eo
        o0, o1 = o[:, :256], o[:, 256:]
        for n, part in enumerate((total + o0, difference + o1, total - o0, difference - o1)):
            high, low = halves(part)
            rh[parity, :, 256 * n : 256 * n + 256] = high
            rl[parity, :, 256 * n : 256 * n + 256] = low
    for n in range(4):
        cut = slice(256 * n, 256 * n + 256)
        sides = [
            dot3((plane_h[parity], plane_l[parity]), (rh[parity, :, cut], rl[parity, :, cut]), TN)
            for parity in range(2)
        ]
        plus, minus = sides[0] + sides[1], sides[0] - sides[1]
        for k in range(16):
            out[k, :, cut] = plus[16 * k : 16 * k + 16]
            out[31 - k, :, cut] = minus[16 * k : 16 * k + 16]


def whole(shape):
    return pl.BlockSpec(shape, lambda *_: (0,) * len(shape))


SMEM = pl.BlockSpec(memory_space=pltpu.SMEM)
VMEM = pl.BlockSpec(memory_space=pltpu.VMEM)


def constants():
    tables = []
    for table in (PLANE, T0, T2, T1):
        tables.extend(jnp.asarray(t) for t in two_terms(table))
    tables.append(jnp.asarray(ROW_LAMBDA, F32))
    tables.append(jnp.asarray(KQ[None, :], F32))
    return tables


def run_forward(levels, neighbours, sweeps, x, tables, **kw):
    return pl.pallas_call(
        forward_kernel,
        grid=(4,),
        in_specs=[
            SMEM, SMEM, SMEM,
            pl.BlockSpec((4, 16, NY), lambda i: (i, 0, 0)),
            pl.BlockSpec((4, 16, NY), lambda i: (7 - i, 0, 0)),
        ]
        + [whole(t.shape) for t in tables],
        out_specs=[whole((1024, 128)), whole((512, NY))],
        out_shape=[
            jax.ShapeDtypeStruct((1024, 128), F32),
            jax.ShapeDtypeStruct((512, NY), F32),
        ],
        scratch_shapes=[
            pltpu.VMEM((2, 256, NY), BF16),
            pltpu.VMEM((2, 256, NY), BF16),
            pltpu.VMEM((3, 128, 256), F32),
        ],
        name="forward",
        **kw,
    )(levels, neighbours, sweeps, x, x, *tables)


def run_columns(device, inbox, **kw):
    lam_x = jnp.asarray(np.tile(LX[IX], 4)[None, :], F32)
    lam_z = jnp.asarray(LZ[:, None], F32)
    zbasis = [jnp.asarray(t) for t in two_terms(ZBASIS)]
    tables = [
        lam_x, lam_z, jnp.asarray(LINK_SCALE, F32), jnp.asarray(LINK_LAMBDA, F32), *zbasis,
        jnp.asarray(ZSUM, F32),
    ]
    return pl.pallas_call(
        column_kernel,
        grid_spec=pltpu.PrefetchScalarGridSpec(
            num_scalar_prefetch=1,
            grid=(1,),
            in_specs=[
                whole((1024, 128)),
                pl.BlockSpec((1, 1, 128), lambda i, own: (own[0], 0, 0)),
            ]
            + [whole(t.shape) for t in tables],
            out_specs=whole((1024, 128)),
            scratch_shapes=[pltpu.VMEM((256, 256), F32), pltpu.VMEM((128, 256), F32)],
        ),
        out_shape=jax.ShapeDtypeStruct((1024, 128), F32),
        name="columns",
        **kw,
    )(device, inbox, jnp.asarray(KQ_OWN, F32), *tables)


def run_backward(levels, inbox, w, tables, **kw):
    return pl.pallas_call(
        backward_kernel,
        in_specs=[SMEM] + [VMEM] * (2 + len(tables)),
        out_specs=VMEM,
        out_shape=jax.ShapeDtypeStruct((BX, ROWS, NY), F32),
        scratch_shapes=[
            pltpu.VMEM((3, 128, 256), F32),
            pltpu.VMEM((2, 256, NY), BF16),
            pltpu.VMEM((2, 256, NY), BF16),
        ],
        name="backward",
        **kw,
    )(levels, inbox, w, *tables)


def traded(outbox):
    pieces = outbox.reshape(DEVICES, 4, 128)
    pieces = lax.all_to_all(pieces, ("mode", "blk"), split_axis=0, concat_axis=0, tiled=True)
    return pieces.reshape(4 * DEVICES, 128)


def body(divergence, neighbours, levels, sweeps):
    tables = constants()
    device = lax.axis_index("mode") * 32 + lax.axis_index("blk")
    outbox, w = run_forward(levels, neighbours, sweeps, divergence[0], tables)
    outbox = run_columns(device.astype(jnp.int32)[None], traded(outbox))
    return run_backward(levels, traded(outbox), w, tables)[None]


def solution(mesh):
    return jax.shard_map(
        body,
        mesh=mesh,
        in_specs=(P("blk", None, "mode", None), P("blk", None), P("blk"), P()),
        out_specs=P("blk", None, "mode", None),
        check_vma=False,
    )
```

```python
import functools
import math

import jax
import jax.numpy as jnp
import numpy as np
from jax import lax
from jax.experimental import pallas as pl
from jax.experimental.pallas import tpu as pltpu
from jax.sharding import PartitionSpec as P

NY = 1024
BX = 32
NZ = 128
CITERS = 8
DAMPING = 0.8
REACH = 3
BLOCKS = 8
ROWS = NZ // BLOCKS
DEVICES = 256
F32 = jnp.float32
BF16 = jnp.bfloat16


def sine_table(extent):
    ordinal = np.arange(1, extent + 1)
    angles = np.pi * np.outer(ordinal, ordinal) / (extent + 1)
    matrix = np.sqrt(2.0 / (extent + 1)) * np.sin(angles)
    return matrix, 4.0 * np.sin(np.pi * ordinal / (2 * (extent + 1))) ** 2


def two_terms(array):
    high = np.asarray(array, np.float32).astype(BF16)
    low = (np.asarray(array, np.float64) - high.astype(np.float64)).astype(BF16)
    return high, low


def fourier_class(length, cosines, sines):
    y = np.arange(length)
    columns = []
    for waves, function in ((cosines, np.cos), (sines, np.sin)):
        for m in waves:
            weight = (1.0 if m in (0, NY // 2) else 2.0) / NY
            columns.append(math.sqrt(weight) * function(2 * np.pi * ((m * y) % NY) / NY))
    waves = np.concatenate((np.array(cosines), np.array(sines)))
    return np.stack(columns, axis=1), 4.0 * np.sin(np.pi * waves / NY) ** 2


def odd_class(residue):
    y = np.arange(128)
    columns = []
    waves = []
    for function in (0, 1):
        for m in range(residue, NY, 8):
            angle = 2 * np.pi * ((m * y) % NY) / NY
            if function == 0:
                column = np.concatenate((np.cos(angle), -np.sin(angle)))
            else:
                column = np.concatenate((np.sin(angle), np.cos(angle)))
                column = column if m < NY // 2 else -column
            columns.append(math.sqrt(2.0 / NY) * column)
            waves.append(min(m, NY - m))
    return np.stack(columns, axis=1), 4.0 * np.sin(np.pi * np.array(waves) / NY) ** 2


SX, LX = sine_table(BX)
SB, LB = sine_table(ROWS)
SZ, LZ = sine_table(NZ)
IX = np.concatenate((np.arange(0, BX, 2), np.arange(1, BX, 2)))
JB = np.concatenate((np.arange(0, ROWS, 2), np.arange(1, ROWS, 2)))
T0, K0 = fourier_class(256, range(0, 513, 4), range(4, 512, 4))
T2, K2 = fourier_class(256, range(2, 512, 4), range(2, 512, 4))
T1, K1 = odd_class(1)
T5, K5 = odd_class(5)
T = np.stack((T0, T2, T1, T5))
KQ = np.concatenate((K0, K2, K1, K5))
ROOT_HALF = math.sqrt(0.5)


def plane_table(parity):
    ways = SX[IX[16 * parity : 16 * parity + 16], :16]
    return np.einsum("ix,jz->ijxz", ways, SB[JB]).reshape(256, 256)


PLANE = np.stack((plane_table(0), plane_table(1)))
ZBASIS = np.einsum("jmz,kz->jmk", SZ.reshape(NZ, BLOCKS, ROWS), SB[JB]).reshape(NZ, NZ)
ZSUM = SZ.sum(axis=0).reshape(NZ, 1)


def link_tables():
    scale = np.zeros((2, 4, 32, 4, 2, 16))
    lam = np.zeros((2, 4, 32, 4, 2, 16))
    for half in range(2):
        for q in range(4):
            for a in range(32):
                lam[half, q, a] = LX[IX[a]] + LB[JB][None, None, :]
                for b in range(8 * half, 8 * half + 8):
                    scale[half, q, a, q, a // 16, b] = SX[0, IX[a]] * SB[0, JB[b]]
    return scale.reshape(256, 128), lam.reshape(256, 128)


LINK_SCALE, LINK_LAMBDA = link_tables()
KQ_OWN = np.repeat(KQ.reshape(4, DEVICES).T, 32, axis=1).reshape(DEVICES, 1, 128)


def halves(value):
    high = value.astype(BF16)
    return high, (value - high.astype(F32)).astype(BF16)


NN = (((1,), (0,)), ((), ()))
NT = (((1,), (1,)), ((), ()))


def dot3(a, b, dims=NN):
    ah, al = a
    bh, bl = b
    return lax.dot_general(
        jnp.concatenate((ah, al, ah), axis=1),
        jnp.concatenate((bh, bh, bl), axis=dims[0][1][0]),
        dims,
        preferred_element_type=F32,
    )


def inverted(value):
    guess = pl.reciprocal(value, approx=True)
    return guess * (2.0 - value * guess)


def stiffness_scalar(level):
    return lax.shift_left(jnp.int32(1), 2 * level).astype(F32)


def per_mode(values):
    iota = lax.broadcasted_iota(jnp.int32, (8, 256), 0)
    halves_of = []
    for half in range(2):
        column = jnp.zeros((8, 256), F32)
        for b in range(8):
            column = jnp.where(iota == b, np.float32(values[JB[8 * half + b]]), column)
        halves_of.append(column)
    return halves_of


def pieces_of(x, x_buffer, x_sems, step):
    first, second = 4 * step, 28 - 4 * step
    return [
        pltpu.make_async_copy(x.at[pl.ds(at, 4)], x_buffer.at[pl.ds(at, 4)], x_sems.at[n, step])
        for n, at in enumerate((first, second))
    ]


def forward_kernel(
    levels, neighbours, sweeps, mode, x, plane_h, plane_l, th, tl, kq,
    out, w_out, x_buffer, p_h, p_l, t_h, t_l, yh, yl, fh, fl, w_buffer, features,
    x_sems, t_sems, w_sems,
):
    tables = [
        pltpu.make_async_copy(source, place, t_sems.at[n])
        for n, (source, place) in enumerate(
            ((th, t_h), (tl, t_l), (plane_h, p_h), (plane_l, p_l))
        )
    ]
    for copy in pieces_of(x, x_buffer, x_sems, 0) + tables[:2]:
        copy.start()
    for step in range(1, 4):
        for copy in pieces_of(x, x_buffer, x_sems, step):
            copy.start()
    for copy in tables[2:]:
        copy.start()

    def fold(step, k):
        for parity in range(2):
            for k in (k,):
                a, b = x_buffer[4 * step + k], x_buffer[31 - 4 * step - k]
                v = a + b if parity == 0 else a - b
                v0, v1, v2, v3 = (v[:, 256 * n : 256 * n + 256] for n in range(4))
                e0, e1 = v0 + v2, v1 + v3
                f, g = v0 - v2, v1 - v3
                f0, f1 = f[:, :128], f[:, 128:] * ROOT_HALF
                g0, g1 = g[:, :128], g[:, 128:] * ROOT_HALF
                turn0, turn1 = f1 - g1, f1 + g1
                parts = (
                    e0 + e1,
                    e0 - e1,
                    jnp.concatenate((f0 + turn0, g0 + turn1), axis=1),
                    jnp.concatenate((f0 - turn0, g0 - turn1), axis=1),
                )
                rows = slice(128 * step + 64 * parity + 16 * k, 128 * step + 64 * parity + 16 * k + 16)
                for q in range(4):
                    high, low = halves(parts[q])
                    yh[q, rows, :] = high
                    yl[q, rows, :] = low

    def transform(step, q):
        rows = slice(128 * step, 128 * step + 128)
        for q in (q,):
            f = dot3((yh[q, rows, :], yl[q, rows, :]), (t_h[q], t_l[q]))
            for parity in range(2):
                place = slice(256 * parity + 64 * step, 256 * parity + 64 * step + 64)
                high, low = halves(f[64 * parity : 64 * parity + 64])
                fh[q, place, :] = high
                fl[q, place, :] = low

    for step in range(4):
        for copy in pieces_of(x, x_buffer, x_sems, step):
            copy.wait()
        if step == 1:
            for copy in tables[:2]:
                copy.wait()
        if step == 3:
            for copy in tables[2:]:
                copy.wait()
        for k in range(4):
            fold(step, k)
            if step > 0:
                transform(step - 1, k)
    for q in range(4):
        transform(3, q)
    level = levels[0]
    stiffness = stiffness_scalar(level)
    lambdas = [stiffness * column for column in per_mode(LB)]
    firsts = per_mode(SB[0])
    sublane = lax.broadcasted_iota(jnp.int32, (8, 256), 0)
    low_side = {size: sublane % (2 * size) < size for size in (4, 2, 1)}

    def summed(values):
        for size in (4, 2, 1):
            merged = []
            for n in range(size):
                one, other = values[n], values[n + size]
                kept = jnp.where(low_side[size], one, other)
                moved = jnp.where(low_side[size], other, one)
                if size == 4:
                    moved = pltpu.roll(moved, 4, 0)
                else:
                    moved = jnp.where(
                        low_side[size],
                        pltpu.roll(moved, 8 - size, 0),
                        pltpu.roll(moved, size, 0),
                    )
                merged.append(kept + moved)
            values = merged
        return values[0]

    copies = []
    for q in range(4):
        base = [column + kq[:, 256 * q : 256 * q + 256] for column in lambdas]
        for parity in range(2):
            rows = slice(256 * parity, 256 * parity + 256)
            g = dot3((p_h[parity], p_l[parity]), (fh[q, rows, :], fl[q, rows, :]))
            place = 32 * q + 16 * parity
            totals = [None, None]
            for group in range(2):
                ends = [[], []]
                for a in range(8 * group, 8 * group + 8):
                    shift = stiffness * np.float32(LX[IX[16 * parity + a]])
                    face = np.float32(SX[0, IX[16 * parity + a]])
                    for half in range(2):
                        row = 16 * a + 8 * half
                        w = g[row : row + 8] * inverted(base[half] + shift)
                        w_buffer[2 * q + parity, row : row + 8, :] = w
                        ends[half].append(w * firsts[half])
                        part = face * w
                        totals[half] = part if a == 0 else totals[half] + part
                at = place + 8 * group
                for half in range(2):
                    features[half, at : at + 8, :] = summed(ends[half])
            for half in range(2):
                features[2, place + 8 * half : place + 8 * half + 8, :] = totals[half]
        if q % 2 == 1:
            copy = pltpu.make_async_copy(
                w_buffer.at[pl.ds(4 * (q // 2), 4)], w_out.at[pl.ds(4 * (q // 2), 4)],
                w_sems.at[q // 2],
            )
            copy.start()
            copies.append(copy)
    last = mode[0] == BLOCKS - 1
    lane = lax.broadcasted_iota(jnp.int32, (8, 128), 1)
    meta = jnp.zeros((8, 128), F32)
    facts = (
        stiffness,
        sweeps[level].astype(F32),
        neighbours[0, 0].astype(F32),
        neighbours[0, 1].astype(F32),
    )
    for n, fact in enumerate(facts):
        meta = jnp.where(lane == n, fact, meta)
    meta = jnp.concatenate([meta] * (DEVICES // 8), axis=0)
    even, odd = features[0].T, features[1].T
    out[pl.ds(0, DEVICES, stride=3), :] = jnp.where(last, even + odd, even)
    out[pl.ds(1, DEVICES, stride=3), :] = jnp.where(last, meta, odd)
    out[pl.ds(2, DEVICES, stride=3), :] = features[2].T
    for copy in copies:
        copy.wait()


def end_responses(shift, extent):
    half = 0.5 * shift
    ratio = 1.0 / (1.0 + half + jnp.sqrt(half * (half + 2.0)))
    square = ratio * ratio
    power = ratio
    for _ in range(extent.bit_length() - 1):
        power = power * power
    rest = power * power
    below = 1.0 / (1.0 - rest * square)
    return ratio * (1.0 - rest) * below, power * (1.0 - square) * below


def column_kernel(
    own, inbox, k_own, lam_x, lam_z, link_scale, link_lambda, zbasis_h, zbasis_l, zback_h, zback_l,
    zsum,
    out, x_links, t_faces,
):
    del own
    k_row = k_own[0]
    meta = inbox[pl.ds(96 * (BLOCKS - 1) + 1, 32, stride=3), :]
    stiff_col = meta[:, 0:1]
    easing_col = 1.0 / stiff_col

    near, far = end_responses(lam_x[...] + k_row * easing_col, ROWS)
    passing, held = [], []
    carry = jnp.zeros((32, 128), F32)
    for m in range(BLOCKS):
        held.append((carry, 1.0 / (1.0 - near * carry)))
        carry = near + far * far * carry * held[-1][1]

    def interfaces(even, odd):
        firsts, offsets = [], []
        offset = jnp.zeros((32, 128), F32)
        for m in range(BLOCKS):
            ratio, scale = held[m]
            first, last = even[m] + odd[m], even[m] - odd[m]
            pushed = (first + near * offset) * scale
            offsets.append(offset)
            firsts.append(pushed)
            offset = last + far * (offset + ratio * pushed)
        above = jnp.zeros((32, 128), F32)
        sides = [None] * BLOCKS
        for m in reversed(range(BLOCKS)):
            ratio, scale = held[m]
            head = firsts[m] + far * scale * above
            below = ratio * head + offsets[m]
            sides[m] = (below + above, below - above)
            above = head
        return sides

    def received(kind, m):
        return inbox[pl.ds(96 * m + kind, 32, stride=3), :]

    even = [received(0, m) for m in range(BLOCKS)]
    odd = [received(1, m) for m in range(BLOCKS - 1)] + [jnp.zeros((32, 128), F32)]
    sides = interfaces(even, odd)
    for m in range(BLOCKS):
        x_links[32 * m : 32 * m + 32, 0:128] = sides[m][0]
        x_links[32 * m : 32 * m + 32, 128:256] = sides[m][1]

    links = [
        halves(link_scale[...] / (link_lambda[...] + k_row * np.float32(0.25**level)))
        for level in range(3)
    ]
    stiff_rows = jnp.concatenate([stiff_col] * BLOCKS, axis=0)
    hits = [stiff_rows == np.float32(4.0**level) for level in range(3)]
    x_all = x_links[...]
    faces = jnp.concatenate([received(2, m) for m in range(BLOCKS)], axis=0)
    for level in range(3):
        faces = faces + dot3(halves(jnp.where(hits[level], x_all, 0.0)), links[level])

    turned = faces.T
    for m in range(BLOCKS):
        for parity in range(2):
            t_faces[16 * m : 16 * m + 16, 128 * parity : 128 * parity + 128] = jnp.concatenate(
                [
                    turned[32 * q + 16 * parity : 32 * q + 16 * parity + 16, 32 * m : 32 * m + 32]
                    for q in range(4)
                ],
                axis=1,
            )
    zbasis = (zbasis_h[...], zbasis_l[...])
    zbasis_t = (zback_h[...], zback_l[...])
    modes = dot3(zbasis, halves(t_faces[...]))
    west_end = modes[:, :128] + modes[:, 128:]
    east_end = modes[:, :128] - modes[:, 128:]

    meta_t = meta.T
    facts = jnp.concatenate([meta_t[0:8]] * 4, axis=1)
    stiff, allowed = facts[0:1], facts[1:2]
    west_slot, east_slot = facts[2:3], facts[3:4]
    lane = lax.broadcasted_iota(jnp.int32, (1, 128), 1)
    column = (lane % 32).astype(F32)
    offsets = [o for o in range(-REACH, REACH + 1) if o != 0]
    west_hits = [
        ((west_slot >= 0.0) & (column - west_slot == np.float32(o))).astype(F32) for o in offsets
    ]
    east_hits = [
        ((east_slot >= 0.0) & (column - east_slot == np.float32(o))).astype(F32) for o in offsets
    ]

    def shifted(value, hits_by_offset):
        parts = [
            pltpu.roll(value, o % 128, 1) * hit for o, hit in zip(offsets, hits_by_offset)
        ]
        return ((parts[0] + parts[1]) + (parts[2] + parts[3])) + (parts[4] + parts[5])

    def exchange(first, last):
        return shifted(last, west_hits), shifted(first, east_hits)

    face_near, face_far = end_responses(lam_z[...] + k_row / stiff, BX)
    twice = (allowed > 1.0).astype(F32)
    west1, east1 = exchange(west_end, east_end)
    west1, east1 = west1 * twice, east1 * twice
    first = west_end + face_near * west1 + face_far * east1
    last = east_end + face_far * west1 + face_near * east1
    west2, east2 = exchange(first, last)
    moved = (west2 - west1) + (east2 - east1)
    coarse = stiff * jnp.sum(moved * zsum[...], axis=0, keepdims=True)
    diagonal = stiff * np.float32(2 * NZ + 2 * BX) + np.float32(BX * NZ) * k_row
    target = jnp.broadcast_to(coarse / diagonal, (8, 128))
    coupling = stiff * np.float32(NZ) / diagonal
    both_hits = [coupling * (w + e) for w, e in zip(west_hits, east_hits)]
    correction = DAMPING * target
    for _ in range(CITERS - 1):
        beside = shifted(correction, both_hits)
        correction = correction + DAMPING * (target - correction + beside)
    correction = correction[0:1]
    west3 = west2 + zsum[...] * shifted(correction, west_hits)
    east3 = east2 + zsum[...] * shifted(correction, east_hits)
    first = west_end + face_near * west3 + face_far * east3
    last = east_end + face_far * west3 + face_near * east3
    west4, east4 = exchange(first, last)
    again = twice > 0.0
    west = jnp.where(again, west4, west3)
    east = jnp.where(again, east4, east3)
    sums = jnp.concatenate((west + east, west - east), axis=1)
    t_faces[...] = dot3(zbasis_t, halves(sums))

    turned = jnp.concatenate(
        [
            jnp.concatenate(
                [
                    t_faces[16 * m : 16 * m + 16, 128 * parity + 32 * q : 128 * parity + 32 * q + 32]
                    for q in range(4)
                    for parity in range(2)
                ],
                axis=0,
            )
            for m in range(BLOCKS)
        ],
        axis=1,
    )
    faces = turned.T
    for m in range(BLOCKS):
        out[pl.ds(96 * m + 2, 32, stride=3), :] = faces[32 * m : 32 * m + 32]
    driven = jnp.zeros((256, 256), F32)
    for level in range(3):
        driven = driven + dot3(halves(jnp.where(hits[level], faces, 0.0)), links[level], NT)
    sides = interfaces(
        [even[m] + driven[32 * m : 32 * m + 32, 0:128] for m in range(BLOCKS)],
        [odd[m] + driven[32 * m : 32 * m + 32, 128:256] for m in range(BLOCKS)],
    )
    for m in range(BLOCKS):
        for kind in range(2):
            out[pl.ds(96 * m + kind, 32, stride=3), :] = sides[m][kind]


def backward_kernel(
    levels, inbox, w_in, back_h, back_l, th, tl, kq, out, features, sums, rows_out, sems,
):
    easing = 1.0 / stiffness_scalar(levels[0])
    for kind in range(3):
        features[kind] = inbox[pl.ds(kind, DEVICES, stride=3), :].T
    firsts, lambdas = per_mode(SB[0]), per_mode(LB)
    for q in range(4):
        base = [column + kq[:, 256 * q : 256 * q + 256] * easing for column in lambdas]
        for parity in range(2):
            place = 32 * q + 16 * parity
            side = features[2, place : place + 16, :]
            terms = []
            for a in range(16):
                shift = np.float32(LX[IX[16 * parity + a]])
                face = np.float32(SX[0, IX[16 * parity + a]])
                pair = []
                for half in range(2):
                    row = 16 * a + 8 * half
                    end = features[half, place + a : place + a + 1, :]
                    drive = firsts[half] * end + face * side[8 * half : 8 * half + 8]
                    w = w_in[2 * q + parity, row : row + 8, :]
                    pair.append(w + drive * inverted(base[half] + shift))
                terms.append(halves(jnp.concatenate(pair, axis=0)))
            u = [jnp.concatenate([t[h] for t in terms], axis=0) for h in range(2)]
            sums[q, 256 * parity : 256 * parity + 256, :] = dot3(u, (th[q], tl[q]), NT)
    copies = []
    for n in range(4):
        cut = slice(256 * n, 256 * n + 256)
        sides = []
        for parity in range(2):
            terms = []
            for k in range(16):
                rows = slice(256 * parity + 16 * k, 256 * parity + 16 * k + 16)
                p0, p2, p1, p5 = (sums[q, rows, :] for q in range(4))
                e = p0 + p2 if n % 2 == 0 else p0 - p2
                half = slice(128 * (n % 2), 128 * (n % 2) + 128)
                turn = (p1 - p5) * ROOT_HALF
                mixed = turn[:, :128] + turn[:, 128:] if n % 2 == 0 else turn[:, 128:] - turn[:, :128]
                f = jnp.concatenate((p1[:, half] + p5[:, half], mixed), axis=1)
                terms.append(halves(e + f if n < 2 else e - f))
            v = [jnp.concatenate([t[h] for t in terms], axis=0) for h in range(2)]
            sides.append(dot3((back_h[parity], back_l[parity]), v))
        for k in range(16):
            rows = slice(16 * k, 16 * k + 16)
            rows_out[k, :, cut] = sides[0][rows] + sides[1][rows]
            rows_out[31 - k, :, cut] = sides[0][rows] - sides[1][rows]
        copy = pltpu.make_async_copy(
            rows_out.at[:, :, pl.ds(256 * n, 256)], out.at[:, :, pl.ds(256 * n, 256)], sems.at[n]
        )
        copy.start()
        copies.append(copy)
    for copy in copies:
        copy.wait()


def whole(shape):
    return pl.BlockSpec(shape, lambda *_: (0,) * len(shape))


SMEM = pl.BlockSpec(memory_space=pltpu.SMEM)
VMEM = pl.BlockSpec(memory_space=pltpu.VMEM)


HBM = pl.BlockSpec(memory_space=pltpu.HBM)
GRANT = pltpu.CompilerParams(vmem_limit_bytes=20 * 2**20)


def constants(back=False):
    tables = []
    for table in (np.swapaxes(PLANE, 1, 2), T) if back else (PLANE, T):
        tables.extend(jnp.asarray(t) for t in two_terms(table))
    tables.append(jnp.asarray(KQ[None, :], F32))
    return tables


def run_forward(levels, neighbours, sweeps, mode, x, **kw):
    return pl.pallas_call(
        forward_kernel,
        in_specs=[SMEM] * 4 + [HBM] * 5 + [VMEM],
        out_specs=[VMEM, HBM],
        out_shape=[
            jax.ShapeDtypeStruct((768, 128), F32),
            jax.ShapeDtypeStruct((8, 256, 256), F32),
        ],
        scratch_shapes=[
            pltpu.VMEM((BX, ROWS, NY), F32),
            pltpu.VMEM((2, 256, 256), BF16),
            pltpu.VMEM((2, 256, 256), BF16),
            pltpu.VMEM((4, 256, 256), BF16),
            pltpu.VMEM((4, 256, 256), BF16),
            pltpu.VMEM((4, 512, 256), BF16),
            pltpu.VMEM((4, 512, 256), BF16),
            pltpu.VMEM((4, 512, 256), BF16),
            pltpu.VMEM((4, 512, 256), BF16),
            pltpu.VMEM((8, 256, 256), F32),
            pltpu.VMEM((3, 128, 256), F32),
            pltpu.SemaphoreType.DMA((2, 4)),
            pltpu.SemaphoreType.DMA((4,)),
            pltpu.SemaphoreType.DMA((2,)),
        ],
        name="forward",
        **kw,
    )(levels, neighbours, sweeps, mode, x, *constants())


def run_columns(device, inbox, **kw):
    lam_x = jnp.asarray(np.tile(LX[IX], 4)[None, :], F32)
    lam_z = jnp.asarray(LZ[:, None], F32)
    zbasis = [jnp.asarray(t) for table in (ZBASIS, ZBASIS.T) for t in two_terms(table)]
    tables = [
        lam_x, lam_z, jnp.asarray(LINK_SCALE, F32), jnp.asarray(LINK_LAMBDA, F32), *zbasis,
        jnp.asarray(ZSUM, F32),
    ]
    return pl.pallas_call(
        column_kernel,
        grid_spec=pltpu.PrefetchScalarGridSpec(
            num_scalar_prefetch=1,
            grid=(1,),
            in_specs=[
                whole((768, 128)),
                pl.BlockSpec((1, 1, 128), lambda i, own: (own[0], 0, 0)),
            ]
            + [whole(t.shape) for t in tables],
            out_specs=whole((768, 128)),
            scratch_shapes=[pltpu.VMEM((256, 256), F32), pltpu.VMEM((128, 256), F32)],
        ),
        out_shape=jax.ShapeDtypeStruct((768, 128), F32),
        name="columns",
        **kw,
    )(device, inbox, jnp.asarray(KQ_OWN, F32), *tables)


def run_backward(levels, inbox, w, **kw):
    tables = constants(True)
    return pl.pallas_call(
        backward_kernel,
        in_specs=[SMEM] + [VMEM] * (2 + len(tables)),
        out_specs=HBM,
        out_shape=jax.ShapeDtypeStruct((BX, ROWS, NY), F32),
        scratch_shapes=[
            pltpu.VMEM((3, 128, 256), F32),
            pltpu.VMEM((4, 512, 256), F32),
            pltpu.VMEM((BX, ROWS, NY), F32),
            pltpu.SemaphoreType.DMA((4,)),
        ],
        compiler_params=GRANT,
        name="backward",
        **kw,
    )(levels, inbox, w, *tables)


def traded(outbox):
    pieces = outbox.reshape(DEVICES, 1, 384)
    pieces = lax.all_to_all(pieces, ("mode", "blk"), split_axis=0, concat_axis=0, tiled=True)
    return pieces.reshape(3 * DEVICES, 128)


def body(divergence, neighbours, levels, sweeps):
    mode = lax.axis_index("mode").astype(jnp.int32)
    device = mode * 32 + lax.axis_index("blk").astype(jnp.int32)
    outbox, w = run_forward(levels, neighbours, sweeps, mode[None], divergence[0])
    outbox = run_columns(device[None], traded(outbox))
    return run_backward(levels, traded(outbox), w)[None]


def solution(mesh):
    return jax.shard_map(
        body,
        mesh=mesh,
        in_specs=(P("blk", None, "mode", None), P("blk", None), P("blk"), P()),
        out_specs=P("blk", None, "mode", None),
        check_vma=False,
    )
```

```python
import functools
import math

import jax
import jax.numpy as jnp
import numpy as np
from jax import lax
from jax.experimental import pallas as pl
from jax.experimental.pallas import tpu as pltpu
from jax.sharding import PartitionSpec as P

NY = 1024
BX = 32
NZ = 128
CITERS = 8
DAMPING = 0.8
REACH = 3
BLOCKS = 8
ROWS = NZ // BLOCKS
DEVICES = 256
F32 = jnp.float32
BF16 = jnp.bfloat16


def sine_table(extent):
    ordinal = np.arange(1, extent + 1)
    angles = np.pi * np.outer(ordinal, ordinal) / (extent + 1)
    matrix = np.sqrt(2.0 / (extent + 1)) * np.sin(angles)
    return matrix, 4.0 * np.sin(np.pi * ordinal / (2 * (extent + 1))) ** 2


def two_terms(array):
    high = np.asarray(array, np.float32).astype(BF16)
    low = (np.asarray(array, np.float64) - high.astype(np.float64)).astype(BF16)
    return high, low


def fourier_class(length, cosines, sines):
    y = np.arange(length)
    columns = []
    for waves, function in ((cosines, np.cos), (sines, np.sin)):
        for m in waves:
            weight = (1.0 if m in (0, NY // 2) else 2.0) / NY
            columns.append(math.sqrt(weight) * function(2 * np.pi * ((m * y) % NY) / NY))
    waves = np.concatenate((np.array(cosines), np.array(sines)))
    return np.stack(columns, axis=1), 4.0 * np.sin(np.pi * waves / NY) ** 2


def odd_class(residue):
    y = np.arange(128)
    columns = []
    waves = []
    for function in (0, 1):
        for m in range(residue, NY, 8):
            angle = 2 * np.pi * ((m * y) % NY) / NY
            if function == 0:
                column = np.concatenate((np.cos(angle), -np.sin(angle)))
            else:
                column = np.concatenate((np.sin(angle), np.cos(angle)))
                column = column if m < NY // 2 else -column
            columns.append(math.sqrt(2.0 / NY) * column)
            waves.append(min(m, NY - m))
    return np.stack(columns, axis=1), 4.0 * np.sin(np.pi * np.array(waves) / NY) ** 2


SX, LX = sine_table(BX)
SB, LB = sine_table(ROWS)
SZ, LZ = sine_table(NZ)
IX = np.concatenate((np.arange(0, BX, 2), np.arange(1, BX, 2)))
JB = np.concatenate((np.arange(0, ROWS, 2), np.arange(1, ROWS, 2)))
T0, K0 = fourier_class(256, range(0, 513, 4), range(4, 512, 4))
T2, K2 = fourier_class(256, range(2, 512, 4), range(2, 512, 4))
T1, K1 = odd_class(1)
T5, K5 = odd_class(5)
T = np.stack((T0, T2, T1, T5))
KQ = np.concatenate((K0, K2, K1, K5))
ROOT_HALF = math.sqrt(0.5)


def plane_table(parity):
    ways = SX[IX[16 * parity : 16 * parity + 16], :16]
    return np.einsum("ix,jz->ijxz", ways, SB[JB]).reshape(256, 256)


PLANE = np.stack((plane_table(0), plane_table(1)))
ZBASIS = np.einsum("jmz,kz->jmk", SZ.reshape(NZ, BLOCKS, ROWS), SB[JB]).reshape(NZ, NZ)
ZSUM = SZ.sum(axis=0).reshape(NZ, 1)


def link_tables():
    scale = np.zeros((2, 4, 32, 4, 2, 16))
    lam = np.zeros((2, 4, 32, 4, 2, 16))
    for half in range(2):
        for q in range(4):
            for a in range(32):
                lam[half, q, a] = LX[IX[a]] + LB[JB][None, None, :]
                for b in range(8 * half, 8 * half + 8):
                    scale[half, q, a, q, a // 16, b] = SX[0, IX[a]] * SB[0, JB[b]]
    return scale.reshape(256, 128), lam.reshape(256, 128)


LINK_SCALE, LINK_LAMBDA = link_tables()
KQ_OWN = np.repeat(KQ.reshape(4, DEVICES).T, 32, axis=1).reshape(DEVICES, 1, 128)


def halves(value):
    high = value.astype(BF16)
    return high, (value - high.astype(F32)).astype(BF16)


NN = (((1,), (0,)), ((), ()))
NT = (((1,), (1,)), ((), ()))


def dot3(a, b, dims=NN):
    ah, al = a
    bh, bl = b
    return lax.dot_general(
        jnp.concatenate((ah, al, ah), axis=1),
        jnp.concatenate((bh, bh, bl), axis=dims[0][1][0]),
        dims,
        preferred_element_type=F32,
    )


def inverted(value):
    guess = pl.reciprocal(value, approx=True)
    return guess * (2.0 - value * guess)


def stiffness_scalar(level):
    return lax.shift_left(jnp.int32(1), 2 * level).astype(F32)


def per_mode(values):
    iota = lax.broadcasted_iota(jnp.int32, (8, 256), 0)
    halves_of = []
    for half in range(2):
        column = jnp.zeros((8, 256), F32)
        for b in range(8):
            column = jnp.where(iota == b, np.float32(values[JB[8 * half + b]]), column)
        halves_of.append(column)
    return halves_of


def pieces_of(x, x_buffer, x_sems, step):
    first, second = 4 * step, 28 - 4 * step
    return [
        pltpu.make_async_copy(x.at[pl.ds(at, 4)], x_buffer.at[pl.ds(at, 4)], x_sems.at[n, step])
        for n, at in enumerate((first, second))
    ]


def forward_kernel(
    levels, neighbours, sweeps, mode, x, tables_in, kq,
    out, w_out, token, x_buffer, p_h, p_l, t_h, t_l, yh, yl, fh, fl, w_buffer, features,
    x_sems, t_sems, w_sems,
):
    tables = [
        pltpu.make_async_copy(source, place, t_sems.at[n])
        for n, (source, place) in enumerate(
            (
                (tables_in.at[pl.ds(0, 4)], t_h), (tables_in.at[pl.ds(4, 4)], t_l),
                (tables_in.at[pl.ds(8, 2)], p_h), (tables_in.at[pl.ds(10, 2)], p_l),
            )
        )
    ]
    token[...] = jnp.zeros((8, 128), F32)
    for copy in pieces_of(x, x_buffer, x_sems, 0) + tables[:2]:
        copy.start()
    for step in range(1, 4):
        for copy in pieces_of(x, x_buffer, x_sems, step):
            copy.start()
    for copy in tables[2:]:
        copy.start()

    def fold(step, k):
        for parity in range(2):
            for k in (k,):
                a, b = x_buffer[4 * step + k], x_buffer[31 - 4 * step - k]
                v = a + b if parity == 0 else a - b
                v0, v1, v2, v3 = (v[:, 256 * n : 256 * n + 256] for n in range(4))
                e0, e1 = v0 + v2, v1 + v3
                f, g = v0 - v2, v1 - v3
                f0, f1 = f[:, :128], f[:, 128:] * ROOT_HALF
                g0, g1 = g[:, :128], g[:, 128:] * ROOT_HALF
                turn0, turn1 = f1 - g1, f1 + g1
                parts = (
                    e0 + e1,
                    e0 - e1,
                    jnp.concatenate((f0 + turn0, g0 + turn1), axis=1),
                    jnp.concatenate((f0 - turn0, g0 - turn1), axis=1),
                )
                rows = slice(128 * step + 64 * parity + 16 * k, 128 * step + 64 * parity + 16 * k + 16)
                for q in range(4):
                    high, low = halves(parts[q])
                    yh[q, rows, :] = high
                    yl[q, rows, :] = low

    def transform(step, q):
        rows = slice(128 * step, 128 * step + 128)
        for q in (q,):
            f = dot3((yh[q, rows, :], yl[q, rows, :]), (t_h[q], t_l[q]))
            for parity in range(2):
                place = slice(256 * parity + 64 * step, 256 * parity + 64 * step + 64)
                high, low = halves(f[64 * parity : 64 * parity + 64])
                fh[q, place, :] = high
                fl[q, place, :] = low

    for step in range(4):
        for copy in pieces_of(x, x_buffer, x_sems, step):
            copy.wait()
        if step == 1:
            for copy in tables[:2]:
                copy.wait()
        if step == 3:
            for copy in tables[2:]:
                copy.wait()
        for k in range(4):
            fold(step, k)
            if step > 0:
                transform(step - 1, k)
    for q in range(4):
        transform(3, q)
    level = levels[0]
    stiffness = stiffness_scalar(level)
    lambdas = [stiffness * column for column in per_mode(LB)]
    firsts = per_mode(SB[0])
    sublane = lax.broadcasted_iota(jnp.int32, (8, 256), 0)
    low_side = {size: sublane % (2 * size) < size for size in (4, 2, 1)}

    def summed(values):
        for size in (4, 2, 1):
            merged = []
            for n in range(size):
                one, other = values[n], values[n + size]
                kept = jnp.where(low_side[size], one, other)
                moved = jnp.where(low_side[size], other, one)
                if size == 4:
                    moved = pltpu.roll(moved, 4, 0)
                else:
                    moved = jnp.where(
                        low_side[size],
                        pltpu.roll(moved, 8 - size, 0),
                        pltpu.roll(moved, size, 0),
                    )
                merged.append(kept + moved)
            values = merged
        return values[0]

    copies = []
    for q in range(4):
        base = [column + kq[:, 256 * q : 256 * q + 256] for column in lambdas]
        for parity in range(2):
            rows = slice(256 * parity, 256 * parity + 256)
            g = dot3((p_h[parity], p_l[parity]), (fh[q, rows, :], fl[q, rows, :]))
            place = 32 * q + 16 * parity
            totals = [None, None]
            for group in range(2):
                ends = [[], []]
                for a in range(8 * group, 8 * group + 8):
                    shift = stiffness * np.float32(LX[IX[16 * parity + a]])
                    face = np.float32(SX[0, IX[16 * parity + a]])
                    for half in range(2):
                        row = 16 * a + 8 * half
                        w = g[row : row + 8] * inverted(base[half] + shift)
                        w_buffer[2 * q + parity, row : row + 8, :] = w
                        ends[half].append(w * firsts[half])
                        part = face * w
                        totals[half] = part if a == 0 else totals[half] + part
                at = place + 8 * group
                for half in range(2):
                    features[half, at : at + 8, :] = summed(ends[half])
            for half in range(2):
                features[2, place + 8 * half : place + 8 * half + 8, :] = totals[half]
        if q % 2 == 1:
            copy = pltpu.make_async_copy(
                w_buffer.at[pl.ds(4 * (q // 2), 4)], w_out.at[pl.ds(4 * (q // 2), 4)],
                w_sems.at[q // 2],
            )
            copy.start()
            copies.append(copy)
    last = mode[0] == BLOCKS - 1
    lane = lax.broadcasted_iota(jnp.int32, (8, 128), 1)
    meta = jnp.zeros((8, 128), F32)
    facts = (
        stiffness,
        sweeps[level].astype(F32),
        neighbours[0, 0].astype(F32),
        neighbours[0, 1].astype(F32),
    )
    for n, fact in enumerate(facts):
        meta = jnp.where(lane == n, fact, meta)
    meta = jnp.concatenate([meta] * (DEVICES // 8), axis=0)
    even, odd = features[0].T, features[1].T
    out[pl.ds(0, DEVICES, stride=3), :] = jnp.where(last, even + odd, even)
    out[pl.ds(1, DEVICES, stride=3), :] = jnp.where(last, meta, odd)
    out[pl.ds(2, DEVICES, stride=3), :] = features[2].T
    for copy in copies:
        copy.wait()


def end_responses(shift, extent):
    half = 0.5 * shift
    ratio = 1.0 / (1.0 + half + jnp.sqrt(half * (half + 2.0)))
    square = ratio * ratio
    power = ratio
    for _ in range(extent.bit_length() - 1):
        power = power * power
    rest = power * power
    below = 1.0 / (1.0 - rest * square)
    return ratio * (1.0 - rest) * below, power * (1.0 - square) * below


RATIOS, SCALES, NEAR_FAR, FACE_NEAR, FACE_FAR, Z_SUM = 8, 72, 136, 152, 536, 920


def prepare_kernel(
    own, token, k_own, lam_x, lam_z, link_scale, link_lambda, zbasis, zsum,
    numbers, terms,
):
    del own, token
    k_row = k_own[0]
    numbers[0:8] = jnp.broadcast_to(k_row, (8, 128))
    level = lax.broadcasted_iota(jnp.int32, (8, 128), 0)
    easing = jnp.where(level == 0, 1.0, jnp.where(level == 1, 0.25, 0.0625))
    near, far = end_responses(lam_x[...] + k_row * easing, ROWS)
    numbers[NEAR_FAR : NEAR_FAR + 8] = near
    numbers[NEAR_FAR + 8 : NEAR_FAR + 16] = far
    carry = jnp.zeros((8, 128), F32)
    for m in range(BLOCKS):
        scale = 1.0 / (1.0 - near * carry)
        numbers[RATIOS + 8 * m : RATIOS + 8 * m + 8] = carry
        numbers[SCALES + 8 * m : SCALES + 8 * m + 8] = scale
        carry = near + far * far * carry * scale
    for level in range(3):
        shift = k_row * np.float32(0.25**level)
        face_near, face_far = end_responses(lam_z[...] + shift, BX)
        numbers[FACE_NEAR + 128 * level : FACE_NEAR + 128 * level + 128] = face_near
        numbers[FACE_FAR + 128 * level : FACE_FAR + 128 * level + 128] = face_far
        high, low = halves(link_scale[...] / (link_lambda[...] + shift))
        terms[256 * level : 256 * level + 256] = high
        terms[768 + 256 * level : 768 + 256 * level + 256] = low
    for n in range(4):
        terms[1536 + 128 * n : 1536 + 128 * n + 128] = zbasis[n]
    numbers[Z_SUM : Z_SUM + 128] = jnp.broadcast_to(zsum[...], (128, 128))


def column_kernel(
    inbox, numbers, terms_in, out, x_links, t_faces, turned, passing,
):
    k_row = numbers[0:1]
    links = (terms_in[0:768], terms_in[768:1536])
    zsum = numbers[Z_SUM : Z_SUM + 128]
    zbasis = [terms_in[1536 + 128 * n : 1536 + 128 * n + 128] for n in range(4)]
    meta = inbox[pl.ds(96 * (BLOCKS - 1) + 1, 32, stride=3), :]
    stiff_col = meta[:, 0:1]
    flat = stiff_col < 2.0
    middle = stiff_col < 8.0

    meta_t = meta.T
    facts = jnp.concatenate([meta_t[0:8]] * 4, axis=1)
    stiff, allowed = facts[0:1], facts[1:2]
    west_slot, east_slot = facts[2:3], facts[3:4]
    lane = lax.broadcasted_iota(jnp.int32, (1, 128), 1)
    first_lane = (lane - lane % 32).astype(F32)
    row = lax.broadcasted_iota(jnp.int32, (128, 128), 0).astype(F32)
    west_pick = ((row == first_lane + west_slot) & (west_slot >= 0.0)).astype(F32)
    east_pick = ((row == first_lane + east_slot) & (east_slot >= 0.0)).astype(F32)
    diagonal = stiff * np.float32(2 * NZ + 2 * BX) + np.float32(BX * NZ) * k_row
    coupling = stiff * np.float32(NZ) / diagonal
    column = lax.broadcasted_iota(jnp.int32, (128, 128), 1).astype(F32)
    unit = (row == column).astype(F32)
    step1 = (1.0 - DAMPING) * unit + DAMPING * coupling * (west_pick + east_pick)
    step1_terms = halves(step1)
    step2_terms = halves(dot3(step1_terms, step1_terms))
    step4 = dot3(step2_terms, step2_terms)
    run2 = step1 + unit
    run4 = run2 + dot3(halves(run2), step2_terms)
    run8 = run4 + dot3(halves(run4), halves(step4))
    picks = jnp.concatenate((west_pick, east_pick), axis=1).astype(BF16)
    run_high, run_low = halves(run8)
    sideways = jnp.dot(
        jnp.concatenate((run_high, run_low), axis=1),
        jnp.concatenate((picks, picks), axis=0),
        preferred_element_type=F32,
    )
    passing[0], passing[1] = halves(sideways)
    west_bits = jnp.concatenate([west_pick.astype(BF16)] * 2, axis=0)
    east_bits = jnp.concatenate([east_pick.astype(BF16)] * 2, axis=0)

    def exchange(first, last):
        west = jnp.dot(
            jnp.concatenate(halves(last), axis=1), west_bits, preferred_element_type=F32
        )
        east = jnp.dot(
            jnp.concatenate(halves(first), axis=1), east_bits, preferred_element_type=F32
        )
        return west, east

    def by_level(at):
        values = numbers[at : at + 8]
        return jnp.where(flat, values[0:1], jnp.where(middle, values[1:2], values[2:3]))

    near, far = by_level(NEAR_FAR), by_level(NEAR_FAR + 8)
    held = [(by_level(RATIOS + 8 * m), by_level(SCALES + 8 * m)) for m in range(BLOCKS)]

    def interfaces(even, odd):
        firsts, offsets = [], []
        offset = jnp.zeros((32, 128), F32)
        for m in range(BLOCKS):
            ratio, scale = held[m]
            first, last = even[m] + odd[m], even[m] - odd[m]
            pushed = (first + near * offset) * scale
            offsets.append(offset)
            firsts.append(pushed)
            offset = last + far * (offset + ratio * pushed)
        above = jnp.zeros((32, 128), F32)
        sides = [None] * BLOCKS
        for m in reversed(range(BLOCKS)):
            ratio, scale = held[m]
            head = firsts[m] + far * scale * above
            below = ratio * head + offsets[m]
            sides[m] = (below + above, below - above)
            above = head
        return sides

    def received(kind, m):
        return inbox[pl.ds(96 * m + kind, 32, stride=3), :]

    even = [received(0, m) for m in range(BLOCKS)]
    odd = [received(1, m) for m in range(BLOCKS - 1)] + [jnp.zeros((32, 128), F32)]
    sides = interfaces(even, odd)
    for m in range(BLOCKS):
        x_links[32 * m : 32 * m + 32, 0:128] = sides[m][0]
        x_links[32 * m : 32 * m + 32, 128:256] = sides[m][1]

    stiff_rows = jnp.broadcast_to(jnp.concatenate([stiff_col] * BLOCKS, axis=0), (256, 128))
    hits = [(stiff_rows == np.float32(4.0**level)).astype(BF16) for level in range(3)]

    def spread(value):
        wide = value.shape[1] // 128
        return [
            jnp.concatenate(
                [
                    term[:, 128 * n : 128 * n + 128] * hits[level]
                    for level in range(3)
                    for n in range(wide)
                ],
                axis=1,
            )
            for term in halves(value)
        ]

    faces = jnp.concatenate([received(2, m) for m in range(BLOCKS)], axis=0)
    faces = faces + dot3(spread(x_links[...]), links)

    block = lax.broadcasted_iota(jnp.int32, (16, 128), 1) // 32

    def joined(parts):
        result = parts[0]
        for n in range(1, 4):
            result = jnp.where(block == n, parts[n], result)
        return result

    def turn(value, shift):
        return value if shift % 4 == 0 else pltpu.roll(value, 32 * (shift % 4), 1)

    turned[...] = faces.T
    for m in range(BLOCKS):
        for parity in range(2):
            t_faces[16 * m : 16 * m + 16, 128 * parity : 128 * parity + 128] = joined(
                [
                    turn(
                        turned[
                            32 * q + 16 * parity : 32 * q + 16 * parity + 16,
                            128 * (m // 4) : 128 * (m // 4) + 128,
                        ],
                        q - m,
                    )
                    for q in range(4)
                ]
            )
    modes = dot3((zbasis[0], zbasis[1]), halves(t_faces[...]))
    west_end = modes[:, :128] + modes[:, 128:]
    east_end = modes[:, :128] - modes[:, 128:]

    def by_lane(at):
        values = [numbers[at + 128 * n : at + 128 * n + 128] for n in range(3)]
        return jnp.where(stiff < 2.0, values[0], jnp.where(stiff < 8.0, values[1], values[2]))

    face_near, face_far = by_lane(FACE_NEAR), by_lane(FACE_FAR)
    twice = (allowed > 1.0).astype(F32)
    west1, east1 = exchange(west_end, east_end)
    west1, east1 = west1 * twice, east1 * twice
    first = west_end + face_near * west1 + face_far * east1
    last = east_end + face_far * west1 + face_near * east1
    west2, east2 = exchange(first, last)
    moved = (west2 - west1) + (east2 - east1)
    coarse = stiff * jnp.sum(moved * zsum, axis=0, keepdims=True)
    target = jnp.broadcast_to(DAMPING * coarse / diagonal, (16, 128))
    corrections = dot3(halves(target), (passing[0], passing[1]))
    west3 = west2 + zsum * corrections[0:1, :128]
    east3 = east2 + zsum * corrections[0:1, 128:]
    first = west_end + face_near * west3 + face_far * east3
    last = east_end + face_far * west3 + face_near * east3
    west4, east4 = exchange(first, last)
    again = twice > 0.0
    west = jnp.where(again, west4, west3)
    east = jnp.where(again, east4, east3)
    sums = jnp.concatenate((west + east, west - east), axis=1)
    t_faces[...] = dot3((zbasis[2], zbasis[3]), halves(sums))

    for q in range(4):
        for parity in range(2):
            for h in range(2):
                turned[
                    32 * q + 16 * parity : 32 * q + 16 * parity + 16, 128 * h : 128 * h + 128
                ] = joined(
                    [
                        turn(
                            t_faces[
                                64 * h + 16 * m : 64 * h + 16 * m + 16,
                                128 * parity : 128 * parity + 128,
                            ],
                            m - q,
                        )
                        for m in range(4)
                    ]
                )
    faces = turned[...].T
    for m in range(BLOCKS):
        out[pl.ds(96 * m + 2, 32, stride=3), :] = faces[32 * m : 32 * m + 32]
    levelled = [
        jnp.concatenate([link[256 * n : 256 * n + 256, :] for n in range(3)], axis=1)
        for link in links
    ]
    driven = dot3(spread(faces), levelled, NT)
    sides = interfaces(
        [even[m] + driven[32 * m : 32 * m + 32, 0:128] for m in range(BLOCKS)],
        [odd[m] + driven[32 * m : 32 * m + 32, 128:256] for m in range(BLOCKS)],
    )
    for m in range(BLOCKS):
        for kind in range(2):
            out[pl.ds(96 * m + kind, 32, stride=3), :] = sides[m][kind]


def backward_kernel(
    levels, inbox, w_in, tables, kq, out, features, sums, rows_out, sems,
):
    easing = 1.0 / stiffness_scalar(levels[0])
    for kind in range(3):
        features[kind] = inbox[pl.ds(kind, DEVICES, stride=3), :].T
    firsts, lambdas = per_mode(SB[0]), per_mode(LB)
    for q in range(4):
        base = [column + kq[:, 256 * q : 256 * q + 256] * easing for column in lambdas]
        for parity in range(2):
            place = 32 * q + 16 * parity
            side = features[2, place : place + 16, :]
            terms = []
            for a in range(16):
                shift = np.float32(LX[IX[16 * parity + a]])
                face = np.float32(SX[0, IX[16 * parity + a]])
                pair = []
                for half in range(2):
                    row = 16 * a + 8 * half
                    end = features[half, place + a : place + a + 1, :]
                    drive = firsts[half] * end + face * side[8 * half : 8 * half + 8]
                    w = w_in[2 * q + parity, row : row + 8, :]
                    pair.append(w + drive * inverted(base[half] + shift))
                terms.append(halves(jnp.concatenate(pair, axis=0)))
            u = [jnp.concatenate([t[h] for t in terms], axis=0) for h in range(2)]
            sums[q, 256 * parity : 256 * parity + 256, :] = dot3(u, (tables[q], tables[4 + q]), NT)
    copies = []
    for n in range(4):
        cut = slice(256 * n, 256 * n + 256)
        sides = []
        for parity in range(2):
            terms = []
            for k in range(16):
                rows = slice(256 * parity + 16 * k, 256 * parity + 16 * k + 16)
                p0, p2, p1, p5 = (sums[q, rows, :] for q in range(4))
                e = p0 + p2 if n % 2 == 0 else p0 - p2
                half = slice(128 * (n % 2), 128 * (n % 2) + 128)
                turn = (p1 - p5) * ROOT_HALF
                mixed = turn[:, :128] + turn[:, 128:] if n % 2 == 0 else turn[:, 128:] - turn[:, :128]
                f = jnp.concatenate((p1[:, half] + p5[:, half], mixed), axis=1)
                terms.append(halves(e + f if n < 2 else e - f))
            v = [jnp.concatenate([t[h] for t in terms], axis=0) for h in range(2)]
            sides.append(dot3((tables[12 + parity], tables[14 + parity]), v))
        for k in range(16):
            rows = slice(16 * k, 16 * k + 16)
            rows_out[k, :, cut] = sides[0][rows] + sides[1][rows]
            rows_out[31 - k, :, cut] = sides[0][rows] - sides[1][rows]
        copy = pltpu.make_async_copy(
            rows_out.at[:, :, pl.ds(256 * n, 256)], out.at[:, :, pl.ds(256 * n, 256)], sems.at[n]
        )
        copy.start()
        copies.append(copy)
    for copy in copies:
        copy.wait()


def whole(shape):
    return pl.BlockSpec(shape, lambda *_: (0,) * len(shape))


SMEM = pl.BlockSpec(memory_space=pltpu.SMEM)
VMEM = pl.BlockSpec(memory_space=pltpu.VMEM)


HBM = pl.BlockSpec(memory_space=pltpu.HBM)
GRANT = pltpu.CompilerParams(vmem_limit_bytes=20 * 2**20)


def constants():
    tables = []
    for table in (T, PLANE, np.swapaxes(PLANE, 1, 2)):
        tables.extend(two_terms(table))
    return jnp.asarray(np.concatenate(tables)), jnp.asarray(KQ[None, :], F32)


def run_forward(levels, neighbours, sweeps, mode, x, **kw):
    return pl.pallas_call(
        forward_kernel,
        in_specs=[SMEM] * 4 + [HBM] * 2 + [VMEM],
        out_specs=[VMEM, HBM, VMEM],
        out_shape=[
            jax.ShapeDtypeStruct((768, 128), F32),
            jax.ShapeDtypeStruct((8, 256, 256), F32),
            jax.ShapeDtypeStruct((8, 128), F32),
        ],
        scratch_shapes=[
            pltpu.VMEM((BX, ROWS, NY), F32),
            pltpu.VMEM((2, 256, 256), BF16),
            pltpu.VMEM((2, 256, 256), BF16),
            pltpu.VMEM((4, 256, 256), BF16),
            pltpu.VMEM((4, 256, 256), BF16),
            pltpu.VMEM((4, 512, 256), BF16),
            pltpu.VMEM((4, 512, 256), BF16),
            pltpu.VMEM((4, 512, 256), BF16),
            pltpu.VMEM((4, 512, 256), BF16),
            pltpu.VMEM((8, 256, 256), F32),
            pltpu.VMEM((3, 128, 256), F32),
            pltpu.SemaphoreType.DMA((2, 4)),
            pltpu.SemaphoreType.DMA((4,)),
            pltpu.SemaphoreType.DMA((2,)),
        ],
        name="forward",
        **kw,
    )(levels, neighbours, sweeps, mode, x, *constants())


def run_prepare(device, token, **kw):
    zbasis = np.stack([t for table in (ZBASIS, ZBASIS.T) for t in two_terms(table)])
    tables = [
        jnp.asarray(np.tile(LX[IX], 4)[None, :], F32), jnp.asarray(LZ[:, None], F32),
        jnp.asarray(LINK_SCALE, F32), jnp.asarray(LINK_LAMBDA, F32), jnp.asarray(zbasis),
        jnp.asarray(ZSUM, F32),
    ]
    shapes = [((Z_SUM + 128, 128), F32), ((2048, 128), BF16)]
    return pl.pallas_call(
        prepare_kernel,
        grid_spec=pltpu.PrefetchScalarGridSpec(
            num_scalar_prefetch=1,
            grid=(1,),
            in_specs=[
                whole((8, 128)),
                pl.BlockSpec((1, 1, 128), lambda i, own: (own[0], 0, 0)),
            ]
            + [whole(t.shape) for t in tables],
            out_specs=[VMEM] * len(shapes),
        ),
        out_shape=[jax.ShapeDtypeStruct(*shape) for shape in shapes],
        compiler_params=GRANT,
        name="prepare",
        **kw,
    )(device, token, jnp.asarray(KQ_OWN, F32), *tables)


def run_columns(inbox, prepared, **kw):
    return pl.pallas_call(
        column_kernel,
        in_specs=[VMEM] * (1 + len(prepared)),
        out_specs=VMEM,
        scratch_shapes=[
            pltpu.VMEM((256, 256), F32),
            pltpu.VMEM((128, 256), F32),
            pltpu.VMEM((128, 256), F32),
            pltpu.VMEM((2, 128, 256), BF16),
        ],
        out_shape=jax.ShapeDtypeStruct((768, 128), F32),
        compiler_params=GRANT,
        name="columns",
        **kw,
    )(inbox, *prepared)


def run_backward(levels, inbox, w, **kw):
    return pl.pallas_call(
        backward_kernel,
        in_specs=[SMEM] + [VMEM] * 4,
        out_specs=HBM,
        out_shape=jax.ShapeDtypeStruct((BX, ROWS, NY), F32),
        scratch_shapes=[
            pltpu.VMEM((3, 128, 256), F32),
            pltpu.VMEM((4, 512, 256), F32),
            pltpu.VMEM((BX, ROWS, NY), F32),
            pltpu.SemaphoreType.DMA((4,)),
        ],
        compiler_params=GRANT,
        name="backward",
        **kw,
    )(levels, inbox, w, *constants())


def traded(outbox):
    pieces = outbox.reshape(DEVICES, 1, 384)
    pieces = lax.all_to_all(pieces, ("mode", "blk"), split_axis=0, concat_axis=0, tiled=True)
    return pieces.reshape(3 * DEVICES, 128)


def body(divergence, neighbours, levels, sweeps):
    mode = lax.axis_index("mode").astype(jnp.int32)
    device = mode * 32 + lax.axis_index("blk").astype(jnp.int32)
    outbox, w, token = run_forward(levels, neighbours, sweeps, mode[None], divergence[0])
    outbox = run_columns(traded(outbox), run_prepare(device[None], token))
    return run_backward(levels, traded(outbox), w)[None]


def solution(mesh):
    return jax.shard_map(
        body,
        mesh=mesh,
        in_specs=(P("blk", None, "mode", None), P("blk", None), P("blk"), P()),
        out_specs=P("blk", None, "mode", None),
        check_vma=False,
    )
```

```python
import functools
import math

import jax
import jax.numpy as jnp
import numpy as np
from jax import lax
from jax.experimental import pallas as pl
from jax.experimental.pallas import tpu as pltpu
from jax.sharding import PartitionSpec as P

NY = 1024
BX = 32
NZ = 128
CITERS = 8
DAMPING = 0.8
REACH = 3
BLOCKS = 8
ROWS = NZ // BLOCKS
DEVICES = 256
F32 = jnp.float32
BF16 = jnp.bfloat16


def sine_table(extent):
    ordinal = np.arange(1, extent + 1)
    angles = np.pi * np.outer(ordinal, ordinal) / (extent + 1)
    matrix = np.sqrt(2.0 / (extent + 1)) * np.sin(angles)
    return matrix, 4.0 * np.sin(np.pi * ordinal / (2 * (extent + 1))) ** 2


def two_terms(array):
    high = np.asarray(array, np.float32).astype(BF16)
    low = (np.asarray(array, np.float64) - high.astype(np.float64)).astype(BF16)
    return high, low


def fourier_class(length, cosines, sines):
    y = np.arange(length)
    columns = []
    for waves, function in ((cosines, np.cos), (sines, np.sin)):
        for m in waves:
            weight = (1.0 if m in (0, NY // 2) else 2.0) / NY
            columns.append(math.sqrt(weight) * function(2 * np.pi * ((m * y) % NY) / NY))
    waves = np.concatenate((np.array(cosines), np.array(sines)))
    return np.stack(columns, axis=1), 4.0 * np.sin(np.pi * waves / NY) ** 2


def odd_class(residue):
    y = np.arange(128)
    columns = []
    waves = []
    for function in (0, 1):
        for m in range(residue, NY, 8):
            angle = 2 * np.pi * ((m * y) % NY) / NY
            if function == 0:
                column = np.concatenate((np.cos(angle), -np.sin(angle)))
            else:
                column = np.concatenate((np.sin(angle), np.cos(angle)))
                column = column if m < NY // 2 else -column
            columns.append(math.sqrt(2.0 / NY) * column)
            waves.append(min(m, NY - m))
    return np.stack(columns, axis=1), 4.0 * np.sin(np.pi * np.array(waves) / NY) ** 2


SX, LX = sine_table(BX)
SB, LB = sine_table(ROWS)
SZ, LZ = sine_table(NZ)
IX = np.concatenate((np.arange(0, BX, 2), np.arange(1, BX, 2)))
JB = np.concatenate((np.arange(0, ROWS, 2), np.arange(1, ROWS, 2)))
T0, K0 = fourier_class(256, range(0, 513, 4), range(4, 512, 4))
T2, K2 = fourier_class(256, range(2, 512, 4), range(2, 512, 4))
T1, K1 = odd_class(1)
T5, K5 = odd_class(5)
T = np.stack((T0, T2, T1, T5))
KQ = np.concatenate((K0, K2, K1, K5))
ROOT_HALF = math.sqrt(0.5)


def plane_table(parity):
    ways = SX[IX[16 * parity : 16 * parity + 16], :16]
    return np.einsum("ix,jz->ijxz", ways, SB[JB]).reshape(256, 256)


PLANE = np.stack((plane_table(0), plane_table(1)))
ZBASIS = np.einsum("jmz,kz->jmk", SZ.reshape(NZ, BLOCKS, ROWS), SB[JB]).reshape(NZ, NZ)
ZSUM = SZ.sum(axis=0).reshape(NZ, 1)


def link_tables():
    scale = np.zeros((2, 4, 32, 4, 2, 16))
    lam = np.zeros((2, 4, 32, 4, 2, 16))
    for half in range(2):
        for q in range(4):
            for a in range(32):
                lam[half, q, a] = LX[IX[a]] + LB[JB][None, None, :]
                for b in range(8 * half, 8 * half + 8):
                    scale[half, q, a, q, a // 16, b] = SX[0, IX[a]] * SB[0, JB[b]]
    return scale.reshape(256, 128), lam.reshape(256, 128)


LINK_SCALE, LINK_LAMBDA = link_tables()
KQ_OWN = np.repeat(KQ.reshape(4, DEVICES).T, 32, axis=1).reshape(DEVICES, 1, 128)


def halves(value):
    high = value.astype(BF16)
    return high, (value - high.astype(F32)).astype(BF16)


NN = (((1,), (0,)), ((), ()))
NT = (((1,), (1,)), ((), ()))


def dot3(a, b, dims=NN):
    ah, al = a
    bh, bl = b
    return lax.dot_general(
        jnp.concatenate((ah, al, ah), axis=1),
        jnp.concatenate((bh, bh, bl), axis=dims[0][1][0]),
        dims,
        preferred_element_type=F32,
    )


def inverted(value):
    guess = pl.reciprocal(value, approx=True)
    return guess * (2.0 - value * guess)


def stiffness_scalar(level):
    return lax.shift_left(jnp.int32(1), 2 * level).astype(F32)


def per_mode(values):
    iota = lax.broadcasted_iota(jnp.int32, (8, 256), 0)
    halves_of = []
    for half in range(2):
        column = jnp.zeros((8, 256), F32)
        for b in range(8):
            column = jnp.where(iota == b, np.float32(values[JB[8 * half + b]]), column)
        halves_of.append(column)
    return halves_of


def pieces_of(x, x_buffer, x_sems, step):
    first, second = 4 * step, 28 - 4 * step
    return [
        pltpu.make_async_copy(x.at[pl.ds(at, 4)], x_buffer.at[pl.ds(at, 4)], x_sems.at[n, step])
        for n, at in enumerate((first, second))
    ]


def forward_kernel(
    levels, neighbours, sweeps, mode, x, tables_in, kq,
    out, w_out, x_buffer, p_h, p_l, t_h, t_l, yh, yl, fh, fl, w_buffer, features,
    x_sems, t_sems, w_sems,
):
    tables = [
        pltpu.make_async_copy(source, place, t_sems.at[n])
        for n, (source, place) in enumerate(
            (
                (tables_in.at[pl.ds(0, 4)], t_h), (tables_in.at[pl.ds(4, 4)], t_l),
                (tables_in.at[pl.ds(8, 2)], p_h), (tables_in.at[pl.ds(10, 2)], p_l),
            )
        )
    ]
    for step in range(4):
        for copy in pieces_of(x, x_buffer, x_sems, step):
            copy.start()
    for copy in tables:
        copy.start()

    def fold(step, k):
        for parity in range(2):
            for k in (k,):
                a, b = x_buffer[4 * step + k], x_buffer[31 - 4 * step - k]
                v = a + b if parity == 0 else a - b
                v0, v1, v2, v3 = (v[:, 256 * n : 256 * n + 256] for n in range(4))
                e0, e1 = v0 + v2, v1 + v3
                f, g = v0 - v2, v1 - v3
                f0, f1 = f[:, :128], f[:, 128:] * ROOT_HALF
                g0, g1 = g[:, :128], g[:, 128:] * ROOT_HALF
                turn0, turn1 = f1 - g1, f1 + g1
                parts = (
                    e0 + e1,
                    e0 - e1,
                    jnp.concatenate((f0 + turn0, g0 + turn1), axis=1),
                    jnp.concatenate((f0 - turn0, g0 - turn1), axis=1),
                )
                at = 256 * parity + 16 * (4 * step + k)
                rows = slice(at, at + 16)
                for q in range(4):
                    high, low = halves(parts[q])
                    yh[q, rows, :] = high
                    yl[q, rows, :] = low

    def transform(q):
        for parity in range(2):
            rows = slice(256 * parity, 256 * parity + 256)
            f = dot3((yh[q, rows, :], yl[q, rows, :]), (t_h[q], t_l[q]))
            high, low = halves(f)
            fh[q, rows, :] = high
            fl[q, rows, :] = low

    for step in range(4):
        for copy in pieces_of(x, x_buffer, x_sems, step):
            copy.wait()
        if step == 3:
            for copy in tables:
                copy.wait()
        for k in range(4):
            fold(step, k)
    level = levels[0]
    stiffness = stiffness_scalar(level)
    lambdas = [stiffness * column for column in per_mode(LB)]
    firsts = per_mode(SB[0])
    sublane = lax.broadcasted_iota(jnp.int32, (8, 256), 0)
    low_side = {size: sublane % (2 * size) < size for size in (4, 2, 1)}

    def summed(values):
        for size in (4, 2, 1):
            merged = []
            for n in range(size):
                one, other = values[n], values[n + size]
                kept = jnp.where(low_side[size], one, other)
                moved = jnp.where(low_side[size], other, one)
                if size == 4:
                    moved = pltpu.roll(moved, 4, 0)
                else:
                    moved = jnp.where(
                        low_side[size],
                        pltpu.roll(moved, 8 - size, 0),
                        pltpu.roll(moved, size, 0),
                    )
                merged.append(kept + moved)
            values = merged
        return values[0]

    copies = []
    transform(0)
    for q in range(4):
        if q < 3:
            transform(q + 1)
        base = [column + kq[:, 256 * q : 256 * q + 256] for column in lambdas]
        for parity in range(2):
            rows = slice(256 * parity, 256 * parity + 256)
            g = dot3((p_h[parity], p_l[parity]), (fh[q, rows, :], fl[q, rows, :]))
            place = 32 * q + 16 * parity
            totals = [None, None]
            for group in range(2):
                ends = [[], []]
                for a in range(8 * group, 8 * group + 8):
                    shift = stiffness * np.float32(LX[IX[16 * parity + a]])
                    face = np.float32(SX[0, IX[16 * parity + a]])
                    for half in range(2):
                        row = 16 * a + 8 * half
                        w = g[row : row + 8] * inverted(base[half] + shift)
                        w_buffer[2 * q + parity, row : row + 8, :] = w
                        ends[half].append(w * firsts[half])
                        part = face * w
                        totals[half] = part if a == 0 else totals[half] + part
                at = place + 8 * group
                for half in range(2):
                    features[half, at : at + 8, :] = summed(ends[half])
            for half in range(2):
                features[2, place + 8 * half : place + 8 * half + 8, :] = totals[half]
        if q % 2 == 1:
            copy = pltpu.make_async_copy(
                w_buffer.at[pl.ds(4 * (q // 2), 4)], w_out.at[pl.ds(4 * (q // 2), 4)],
                w_sems.at[q // 2],
            )
            copy.start()
            copies.append(copy)
    last = mode[0] == BLOCKS - 1
    lane = lax.broadcasted_iota(jnp.int32, (8, 128), 1)
    meta = jnp.zeros((8, 128), F32)
    facts = (
        stiffness,
        sweeps[level].astype(F32),
        neighbours[0, 0].astype(F32),
        neighbours[0, 1].astype(F32),
    )
    for n, fact in enumerate(facts):
        meta = jnp.where(lane == n, fact, meta)
    meta = jnp.concatenate([meta] * (DEVICES // 8), axis=0)
    even, odd = features[0].T, features[1].T
    out[pl.ds(0, DEVICES, stride=3), :] = jnp.where(last, even + odd, even)
    out[pl.ds(1, DEVICES, stride=3), :] = jnp.where(last, meta, odd)
    out[pl.ds(2, DEVICES, stride=3), :] = features[2].T
    for copy in copies:
        copy.wait()


def end_responses(shift, extent):
    half = 0.5 * shift
    ratio = 1.0 / (1.0 + half + jnp.sqrt(half * (half + 2.0)))
    square = ratio * ratio
    power = ratio
    for _ in range(extent.bit_length() - 1):
        power = power * power
    rest = power * power
    below = 1.0 / (1.0 - rest * square)
    return ratio * (1.0 - rest) * below, power * (1.0 - square) * below


RATIOS, SCALES, NEAR_FAR, FACE_NEAR, FACE_FAR, Z_SUM = 8, 72, 136, 152, 536, 920


def prepare_kernel(own, w_in, k_own, constants_in, zbasis, numbers, terms, w_out, sem):
    del own
    copy = pltpu.make_async_copy(w_in, w_out, sem)
    copy.start()
    link_scale, link_lambda = constants_in[0:256], constants_in[256:512]
    zsum, lam_z, lam_x = constants_in[512:640], constants_in[640:768], constants_in[768:776]
    k_row = k_own[0]
    numbers[0:8] = jnp.broadcast_to(k_row, (8, 128))
    level = lax.broadcasted_iota(jnp.int32, (8, 128), 0)
    easing = jnp.where(level == 0, 1.0, jnp.where(level == 1, 0.25, 0.0625))
    near, far = end_responses(lam_x + k_row * easing, ROWS)
    numbers[NEAR_FAR : NEAR_FAR + 8] = near
    numbers[NEAR_FAR + 8 : NEAR_FAR + 16] = far
    carry = jnp.zeros((8, 128), F32)
    for m in range(BLOCKS):
        scale = 1.0 / (1.0 - near * carry)
        numbers[RATIOS + 8 * m : RATIOS + 8 * m + 8] = carry
        numbers[SCALES + 8 * m : SCALES + 8 * m + 8] = scale
        carry = near + far * far * carry * scale
    for level in range(3):
        shift = k_row * np.float32(0.25**level)
        face_near, face_far = end_responses(lam_z + shift, BX)
        numbers[FACE_NEAR + 128 * level : FACE_NEAR + 128 * level + 128] = face_near
        numbers[FACE_FAR + 128 * level : FACE_FAR + 128 * level + 128] = face_far
        high, low = halves(link_scale / (link_lambda + shift))
        terms[256 * level : 256 * level + 256] = high
        terms[768 + 256 * level : 768 + 256 * level + 256] = low
    for n in range(4):
        terms[1536 + 128 * n : 1536 + 128 * n + 128] = zbasis[n]
    numbers[Z_SUM : Z_SUM + 128] = zsum
    copy.wait()


def column_kernel(
    inbox, numbers, terms_in, out, x_links, t_faces, turned, passing,
):
    k_row = numbers[0:1]
    links = (terms_in[0:768], terms_in[768:1536])
    zsum = numbers[Z_SUM : Z_SUM + 128]
    zbasis = [terms_in[1536 + 128 * n : 1536 + 128 * n + 128] for n in range(4)]
    meta = inbox[pl.ds(96 * (BLOCKS - 1) + 1, 32, stride=3), :]
    stiff_col = meta[:, 0:1]
    flat = stiff_col < 2.0
    middle = stiff_col < 8.0

    meta_t = meta.T
    facts = jnp.concatenate([meta_t[0:8]] * 4, axis=1)
    stiff, allowed = facts[0:1], facts[1:2]
    west_slot, east_slot = facts[2:3], facts[3:4]
    lane = lax.broadcasted_iota(jnp.int32, (1, 128), 1)
    first_lane = (lane - lane % 32).astype(F32)
    row = lax.broadcasted_iota(jnp.int32, (128, 128), 0).astype(F32)
    west_pick = ((row == first_lane + west_slot) & (west_slot >= 0.0)).astype(F32)
    east_pick = ((row == first_lane + east_slot) & (east_slot >= 0.0)).astype(F32)
    diagonal = stiff * np.float32(2 * NZ + 2 * BX) + np.float32(BX * NZ) * k_row
    coupling = stiff * np.float32(NZ) / diagonal
    column = lax.broadcasted_iota(jnp.int32, (128, 128), 1).astype(F32)
    unit = (row == column).astype(F32)
    step1 = (1.0 - DAMPING) * unit + DAMPING * coupling * (west_pick + east_pick)
    step1_terms = halves(step1)
    step2_terms = halves(dot3(step1_terms, step1_terms))
    step4 = dot3(step2_terms, step2_terms)
    run2 = step1 + unit
    run4 = run2 + dot3(halves(run2), step2_terms)
    run8 = run4 + dot3(halves(run4), halves(step4))
    picks = jnp.concatenate((west_pick, east_pick), axis=1).astype(BF16)
    run_high, run_low = halves(run8)
    sideways = jnp.dot(
        jnp.concatenate((run_high, run_low), axis=1),
        jnp.concatenate((picks, picks), axis=0),
        preferred_element_type=F32,
    )
    passing[0], passing[1] = halves(sideways)
    west_bits = jnp.concatenate([west_pick.astype(BF16)] * 2, axis=0)
    east_bits = jnp.concatenate([east_pick.astype(BF16)] * 2, axis=0)

    def exchange(first, last):
        west = jnp.dot(
            jnp.concatenate(halves(last), axis=1), west_bits, preferred_element_type=F32
        )
        east = jnp.dot(
            jnp.concatenate(halves(first), axis=1), east_bits, preferred_element_type=F32
        )
        return west, east

    def by_level(at):
        values = numbers[at : at + 8]
        return jnp.where(flat, values[0:1], jnp.where(middle, values[1:2], values[2:3]))

    near, far = by_level(NEAR_FAR), by_level(NEAR_FAR + 8)
    held = [(by_level(RATIOS + 8 * m), by_level(SCALES + 8 * m)) for m in range(BLOCKS)]

    def interfaces(even, odd):
        firsts, offsets = [], []
        offset = jnp.zeros((32, 128), F32)
        for m in range(BLOCKS):
            ratio, scale = held[m]
            first, last = even[m] + odd[m], even[m] - odd[m]
            pushed = (first + near * offset) * scale
            offsets.append(offset)
            firsts.append(pushed)
            offset = last + far * (offset + ratio * pushed)
        above = jnp.zeros((32, 128), F32)
        sides = [None] * BLOCKS
        for m in reversed(range(BLOCKS)):
            ratio, scale = held[m]
            head = firsts[m] + far * scale * above
            below = ratio * head + offsets[m]
            sides[m] = (below + above, below - above)
            above = head
        return sides

    def received(kind, m):
        return inbox[pl.ds(96 * m + kind, 32, stride=3), :]

    even = [received(0, m) for m in range(BLOCKS)]
    odd = [received(1, m) for m in range(BLOCKS - 1)] + [jnp.zeros((32, 128), F32)]
    sides = interfaces(even, odd)
    for m in range(BLOCKS):
        x_links[32 * m : 32 * m + 32, 0:128] = sides[m][0]
        x_links[32 * m : 32 * m + 32, 128:256] = sides[m][1]

    stiff_rows = jnp.broadcast_to(jnp.concatenate([stiff_col] * BLOCKS, axis=0), (256, 128))
    hits = [(stiff_rows == np.float32(4.0**level)).astype(BF16) for level in range(3)]

    def spread(value):
        wide = value.shape[1] // 128
        return [
            jnp.concatenate(
                [
                    term[:, 128 * n : 128 * n + 128] * hits[level]
                    for level in range(3)
                    for n in range(wide)
                ],
                axis=1,
            )
            for term in halves(value)
        ]

    faces = jnp.concatenate([received(2, m) for m in range(BLOCKS)], axis=0)
    faces = faces + dot3(spread(x_links[...]), links)

    block = lax.broadcasted_iota(jnp.int32, (16, 128), 1) // 32

    def joined(parts):
        result = parts[0]
        for n in range(1, 4):
            result = jnp.where(block == n, parts[n], result)
        return result

    def turn(value, shift):
        return value if shift % 4 == 0 else pltpu.roll(value, 32 * (shift % 4), 1)

    turned[...] = faces.T
    for m in range(BLOCKS):
        for parity in range(2):
            t_faces[16 * m : 16 * m + 16, 128 * parity : 128 * parity + 128] = joined(
                [
                    turn(
                        turned[
                            32 * q + 16 * parity : 32 * q + 16 * parity + 16,
                            128 * (m // 4) : 128 * (m // 4) + 128,
                        ],
                        q - m,
                    )
                    for q in range(4)
                ]
            )
    modes = dot3((zbasis[0], zbasis[1]), halves(t_faces[...]))
    west_end = modes[:, :128] + modes[:, 128:]
    east_end = modes[:, :128] - modes[:, 128:]

    def by_lane(at):
        values = [numbers[at + 128 * n : at + 128 * n + 128] for n in range(3)]
        return jnp.where(stiff < 2.0, values[0], jnp.where(stiff < 8.0, values[1], values[2]))

    face_near, face_far = by_lane(FACE_NEAR), by_lane(FACE_FAR)
    twice = (allowed > 1.0).astype(F32)
    west1, east1 = exchange(west_end, east_end)
    west1, east1 = west1 * twice, east1 * twice
    first = west_end + face_near * west1 + face_far * east1
    last = east_end + face_far * west1 + face_near * east1
    west2, east2 = exchange(first, last)
    moved = (west2 - west1) + (east2 - east1)
    coarse = stiff * jnp.sum(moved * zsum, axis=0, keepdims=True)
    target = jnp.broadcast_to(DAMPING * coarse / diagonal, (16, 128))
    corrections = dot3(halves(target), (passing[0], passing[1]))
    west3 = west2 + zsum * corrections[0:1, :128]
    east3 = east2 + zsum * corrections[0:1, 128:]
    first = west_end + face_near * west3 + face_far * east3
    last = east_end + face_far * west3 + face_near * east3
    west4, east4 = exchange(first, last)
    again = twice > 0.0
    west = jnp.where(again, west4, west3)
    east = jnp.where(again, east4, east3)
    sums = jnp.concatenate((west + east, west - east), axis=1)
    t_faces[...] = dot3((zbasis[2], zbasis[3]), halves(sums))

    for q in range(4):
        for parity in range(2):
            for h in range(2):
                turned[
                    32 * q + 16 * parity : 32 * q + 16 * parity + 16, 128 * h : 128 * h + 128
                ] = joined(
                    [
                        turn(
                            t_faces[
                                64 * h + 16 * m : 64 * h + 16 * m + 16,
                                128 * parity : 128 * parity + 128,
                            ],
                            m - q,
                        )
                        for m in range(4)
                    ]
                )
    faces = turned[...].T
    for m in range(BLOCKS):
        out[pl.ds(96 * m + 2, 32, stride=3), :] = faces[32 * m : 32 * m + 32]
    levelled = [
        jnp.concatenate([link[256 * n : 256 * n + 256, :] for n in range(3)], axis=1)
        for link in links
    ]
    driven = dot3(spread(faces), levelled, NT)
    sides = interfaces(
        [even[m] + driven[32 * m : 32 * m + 32, 0:128] for m in range(BLOCKS)],
        [odd[m] + driven[32 * m : 32 * m + 32, 128:256] for m in range(BLOCKS)],
    )
    for m in range(BLOCKS):
        for kind in range(2):
            out[pl.ds(96 * m + kind, 32, stride=3), :] = sides[m][kind]


def backward_kernel(
    levels, inbox, w_in, tables, kq, out, features, sums, rows_out, sems,
):
    easing = 1.0 / stiffness_scalar(levels[0])
    for kind in range(3):
        features[kind] = inbox[pl.ds(kind, DEVICES, stride=3), :].T
    firsts, lambdas = per_mode(SB[0]), per_mode(LB)
    for q in range(4):
        base = [column + kq[:, 256 * q : 256 * q + 256] * easing for column in lambdas]
        for parity in range(2):
            place = 32 * q + 16 * parity
            side = features[2, place : place + 16, :]
            terms = []
            for a in range(16):
                shift = np.float32(LX[IX[16 * parity + a]])
                face = np.float32(SX[0, IX[16 * parity + a]])
                pair = []
                for half in range(2):
                    row = 16 * a + 8 * half
                    end = features[half, place + a : place + a + 1, :]
                    drive = firsts[half] * end + face * side[8 * half : 8 * half + 8]
                    w = w_in[2 * q + parity, row : row + 8, :]
                    pair.append(w + drive * inverted(base[half] + shift))
                terms.append(halves(jnp.concatenate(pair, axis=0)))
            u = [jnp.concatenate([t[h] for t in terms], axis=0) for h in range(2)]
            sums[q, 256 * parity : 256 * parity + 256, :] = dot3(u, (tables[q], tables[4 + q]), NT)
    copies = []
    for n in range(4):
        cut = slice(256 * n, 256 * n + 256)
        sides = []
        for parity in range(2):
            terms = []
            for k in range(16):
                rows = slice(256 * parity + 16 * k, 256 * parity + 16 * k + 16)
                p0, p2, p1, p5 = (sums[q, rows, :] for q in range(4))
                e = p0 + p2 if n % 2 == 0 else p0 - p2
                half = slice(128 * (n % 2), 128 * (n % 2) + 128)
                turn = (p1 - p5) * ROOT_HALF
                mixed = turn[:, :128] + turn[:, 128:] if n % 2 == 0 else turn[:, 128:] - turn[:, :128]
                f = jnp.concatenate((p1[:, half] + p5[:, half], mixed), axis=1)
                terms.append(halves(e + f if n < 2 else e - f))
            v = [jnp.concatenate([t[h] for t in terms], axis=0) for h in range(2)]
            sides.append(dot3((tables[12 + parity], tables[14 + parity]), v))
        for k in range(16):
            rows = slice(16 * k, 16 * k + 16)
            rows_out[k, :, cut] = sides[0][rows] + sides[1][rows]
            rows_out[31 - k, :, cut] = sides[0][rows] - sides[1][rows]
        copy = pltpu.make_async_copy(
            rows_out.at[:, :, pl.ds(256 * n, 256)], out.at[:, :, pl.ds(256 * n, 256)], sems.at[n]
        )
        copy.start()
        copies.append(copy)
    for copy in copies:
        copy.wait()


def whole(shape):
    return pl.BlockSpec(shape, lambda *_: (0,) * len(shape))


SMEM = pl.BlockSpec(memory_space=pltpu.SMEM)
VMEM = pl.BlockSpec(memory_space=pltpu.VMEM)


HBM = pl.BlockSpec(memory_space=pltpu.HBM)
GRANT = pltpu.CompilerParams(vmem_limit_bytes=20 * 2**20)


def constants():
    tables = []
    for table in (T, PLANE, np.swapaxes(PLANE, 1, 2)):
        tables.extend(two_terms(table))
    return jnp.asarray(np.concatenate(tables)), jnp.asarray(KQ[None, :], F32)


def run_forward(levels, neighbours, sweeps, mode, x, **kw):
    return pl.pallas_call(
        forward_kernel,
        in_specs=[SMEM] * 4 + [HBM] * 2 + [VMEM],
        out_specs=[VMEM, HBM],
        out_shape=[
            jax.ShapeDtypeStruct((768, 128), F32),
            jax.ShapeDtypeStruct((8, 256, 256), F32),
        ],
        scratch_shapes=[
            pltpu.VMEM((BX, ROWS, NY), F32),
            pltpu.VMEM((2, 256, 256), BF16),
            pltpu.VMEM((2, 256, 256), BF16),
            pltpu.VMEM((4, 256, 256), BF16),
            pltpu.VMEM((4, 256, 256), BF16),
            pltpu.VMEM((4, 512, 256), BF16),
            pltpu.VMEM((4, 512, 256), BF16),
            pltpu.VMEM((4, 512, 256), BF16),
            pltpu.VMEM((4, 512, 256), BF16),
            pltpu.VMEM((8, 256, 256), F32),
            pltpu.VMEM((3, 128, 256), F32),
            pltpu.SemaphoreType.DMA((2, 4)),
            pltpu.SemaphoreType.DMA((4,)),
            pltpu.SemaphoreType.DMA((2,)),
        ],
        name="forward",
        **kw,
    )(levels, neighbours, sweeps, mode, x, *constants())


def run_prepare(device, w, **kw):
    zbasis = np.stack([t for table in (ZBASIS, ZBASIS.T) for t in two_terms(table)])
    wide = np.ones((1, 128))
    numbers = np.concatenate(
        (
            LINK_SCALE, LINK_LAMBDA, ZSUM * wide, LZ[:, None] * wide,
            np.tile(LX[IX], 4)[None, :] * np.ones((8, 1)),
        )
    )
    shapes = [((Z_SUM + 128, 128), F32), ((2048, 128), BF16), (w.shape, F32)]
    return pl.pallas_call(
        prepare_kernel,
        grid_spec=pltpu.PrefetchScalarGridSpec(
            num_scalar_prefetch=1,
            grid=(1,),
            in_specs=[
                HBM,
                pl.BlockSpec((1, 1, 128), lambda i, own: (own[0], 0, 0)),
                whole(numbers.shape),
                whole(zbasis.shape),
            ],
            out_specs=[VMEM] * len(shapes),
            scratch_shapes=[pltpu.SemaphoreType.DMA],
        ),
        out_shape=[jax.ShapeDtypeStruct(*shape) for shape in shapes],
        compiler_params=GRANT,
        name="prepare",
        **kw,
    )(device, w, jnp.asarray(KQ_OWN, F32), jnp.asarray(numbers, F32), jnp.asarray(zbasis))


def run_columns(inbox, numbers, terms, **kw):
    return pl.pallas_call(
        column_kernel,
        in_specs=[VMEM] * 3,
        out_specs=VMEM,
        scratch_shapes=[
            pltpu.VMEM((256, 256), F32),
            pltpu.VMEM((128, 256), F32),
            pltpu.VMEM((128, 256), F32),
            pltpu.VMEM((2, 128, 256), BF16),
        ],
        out_shape=jax.ShapeDtypeStruct((768, 128), F32),
        compiler_params=GRANT,
        name="columns",
        **kw,
    )(inbox, numbers, terms)


def run_backward(levels, inbox, w, **kw):
    return pl.pallas_call(
        backward_kernel,
        in_specs=[SMEM] + [VMEM] * 4,
        out_specs=HBM,
        out_shape=jax.ShapeDtypeStruct((BX, ROWS, NY), F32),
        scratch_shapes=[
            pltpu.VMEM((3, 128, 256), F32),
            pltpu.VMEM((4, 512, 256), F32),
            pltpu.VMEM((BX, ROWS, NY), F32),
            pltpu.SemaphoreType.DMA((4,)),
        ],
        compiler_params=GRANT,
        name="backward",
        **kw,
    )(levels, inbox, w, *constants())


def traded(outbox):
    pieces = outbox.reshape(DEVICES, 1, 384)
    pieces = lax.all_to_all(pieces, ("mode", "blk"), split_axis=0, concat_axis=0, tiled=True)
    return pieces.reshape(3 * DEVICES, 128)


def body(divergence, neighbours, levels, sweeps):
    mode = lax.axis_index("mode").astype(jnp.int32)
    device = mode * 32 + lax.axis_index("blk").astype(jnp.int32)
    outbox, w = run_forward(levels, neighbours, sweeps, mode[None], divergence[0])
    numbers, terms, w = run_prepare(device[None], w)
    outbox = run_columns(traded(outbox), numbers, terms)
    return run_backward(levels, traded(outbox), w)[None]


def solution(mesh):
    return jax.shard_map(
        body,
        mesh=mesh,
        in_specs=(P("blk", None, "mode", None), P("blk", None), P("blk"), P()),
        out_specs=P("blk", None, "mode", None),
        check_vma=False,
    )
```

```python
import functools
import math

import jax
import jax.numpy as jnp
import numpy as np
from jax import lax
from jax.experimental import pallas as pl
from jax.experimental.pallas import tpu as pltpu
from jax.sharding import PartitionSpec as P

NY = 1024
BX = 32
NZ = 128
CITERS = 8
DAMPING = 0.8
REACH = 3
BLOCKS = 8
ROWS = NZ // BLOCKS
DEVICES = 256
F32 = jnp.float32
BF16 = jnp.bfloat16


def sine_table(extent):
    ordinal = np.arange(1, extent + 1)
    angles = np.pi * np.outer(ordinal, ordinal) / (extent + 1)
    matrix = np.sqrt(2.0 / (extent + 1)) * np.sin(angles)
    return matrix, 4.0 * np.sin(np.pi * ordinal / (2 * (extent + 1))) ** 2


def two_terms(array):
    high = np.asarray(array, np.float32).astype(BF16)
    low = (np.asarray(array, np.float64) - high.astype(np.float64)).astype(BF16)
    return high, low


def fourier_class(length, cosines, sines):
    y = np.arange(length)
    columns = []
    for waves, function in ((cosines, np.cos), (sines, np.sin)):
        for m in waves:
            weight = (1.0 if m in (0, NY // 2) else 2.0) / NY
            columns.append(math.sqrt(weight) * function(2 * np.pi * ((m * y) % NY) / NY))
    waves = np.concatenate((np.array(cosines), np.array(sines)))
    return np.stack(columns, axis=1), 4.0 * np.sin(np.pi * waves / NY) ** 2


def odd_class(residue):
    y = np.arange(128)
    columns = []
    waves = []
    for function in (0, 1):
        for m in range(residue, NY, 8):
            angle = 2 * np.pi * ((m * y) % NY) / NY
            if function == 0:
                column = np.concatenate((np.cos(angle), -np.sin(angle)))
            else:
                column = np.concatenate((np.sin(angle), np.cos(angle)))
                column = column if m < NY // 2 else -column
            columns.append(math.sqrt(2.0 / NY) * column)
            waves.append(min(m, NY - m))
    return np.stack(columns, axis=1), 4.0 * np.sin(np.pi * np.array(waves) / NY) ** 2


SX, LX = sine_table(BX)
SB, LB = sine_table(ROWS)
SZ, LZ = sine_table(NZ)
IX = np.concatenate((np.arange(0, BX, 2), np.arange(1, BX, 2)))
JB = np.concatenate((np.arange(0, ROWS, 2), np.arange(1, ROWS, 2)))
T0, K0 = fourier_class(256, range(0, 513, 4), range(4, 512, 4))
T2, K2 = fourier_class(256, range(2, 512, 4), range(2, 512, 4))
T1, K1 = odd_class(1)
T5, K5 = odd_class(5)
T = np.stack((T0, T2, T1, T5))
KQ = np.concatenate((K0, K2, K1, K5))
ROOT_HALF = math.sqrt(0.5)


def plane_table(parity):
    ways = SX[IX[16 * parity : 16 * parity + 16], :16]
    return np.einsum("ix,jz->ijxz", ways, SB[JB]).reshape(256, 256)


PLANE = np.stack((plane_table(0), plane_table(1)))
ZBASIS = np.einsum("jmz,kz->jmk", SZ.reshape(NZ, BLOCKS, ROWS), SB[JB]).reshape(NZ, NZ)
ZSUM = SZ.sum(axis=0).reshape(NZ, 1)


def link_tables():
    scale = np.zeros((2, 4, 32, 4, 2, 16))
    lam = np.zeros((2, 4, 32, 4, 2, 16))
    for half in range(2):
        for q in range(4):
            for a in range(32):
                lam[half, q, a] = LX[IX[a]] + LB[JB][None, None, :]
                for b in range(8 * half, 8 * half + 8):
                    scale[half, q, a, q, a // 16, b] = SX[0, IX[a]] * SB[0, JB[b]]
    return scale.reshape(256, 128), lam.reshape(256, 128)


LINK_SCALE, LINK_LAMBDA = link_tables()
KQ_OWN = np.repeat(KQ.reshape(4, DEVICES).T, 32, axis=1).reshape(DEVICES, 1, 128)


def halves(value):
    high = value.astype(BF16)
    return high, (value - high.astype(F32)).astype(BF16)


NN = (((1,), (0,)), ((), ()))
NT = (((1,), (1,)), ((), ()))


def dot3(a, b, dims=NN):
    ah, al = a
    bh, bl = b
    return lax.dot_general(
        jnp.concatenate((ah, al, ah), axis=1),
        jnp.concatenate((bh, bh, bl), axis=dims[0][1][0]),
        dims,
        preferred_element_type=F32,
    )


def inverted(value):
    guess = pl.reciprocal(value, approx=True)
    return guess * (2.0 - value * guess)


def stiffness_scalar(level):
    return lax.shift_left(jnp.int32(1), 2 * level).astype(F32)


def per_mode(values):
    iota = lax.broadcasted_iota(jnp.int32, (8, 256), 0)
    halves_of = []
    for half in range(2):
        column = jnp.zeros((8, 256), F32)
        for b in range(8):
            column = jnp.where(iota == b, np.float32(values[JB[8 * half + b]]), column)
        halves_of.append(column)
    return halves_of


def pieces_of(x, x_buffer, x_sems, step):
    first, second = 4 * step, 28 - 4 * step
    return [
        pltpu.make_async_copy(x.at[pl.ds(at, 4)], x_buffer.at[pl.ds(at, 4)], x_sems.at[n, step])
        for n, at in enumerate((first, second))
    ]


def forward_kernel(
    levels, neighbours, sweeps, mode, x, tables_in, kq,
    out_hbm, w_out, out, x_buffer, p_h, p_l, t_h, t_l, yh, yl, fh, fl, w_buffer, features,
    x_sems, t_sems, w_sems,
):
    tables = [
        pltpu.make_async_copy(source, place, t_sems.at[n])
        for n, (source, place) in enumerate(
            (
                (tables_in.at[pl.ds(0, 4)], t_h), (tables_in.at[pl.ds(4, 4)], t_l),
                (tables_in.at[pl.ds(8, 2)], p_h), (tables_in.at[pl.ds(10, 2)], p_l),
            )
        )
    ]
    for step in range(4):
        for copy in pieces_of(x, x_buffer, x_sems, step):
            copy.start()
    for copy in tables:
        copy.start()

    def fold(step, k):
        for parity in range(2):
            for k in (k,):
                a, b = x_buffer[4 * step + k], x_buffer[31 - 4 * step - k]
                v = a + b if parity == 0 else a - b
                v0, v1, v2, v3 = (v[:, 256 * n : 256 * n + 256] for n in range(4))
                e0, e1 = v0 + v2, v1 + v3
                f, g = v0 - v2, v1 - v3
                f0, f1 = f[:, :128], f[:, 128:] * ROOT_HALF
                g0, g1 = g[:, :128], g[:, 128:] * ROOT_HALF
                turn0, turn1 = f1 - g1, f1 + g1
                parts = (
                    e0 + e1,
                    e0 - e1,
                    jnp.concatenate((f0 + turn0, g0 + turn1), axis=1),
                    jnp.concatenate((f0 - turn0, g0 - turn1), axis=1),
                )
                at = 256 * parity + 16 * (4 * step + k)
                rows = slice(at, at + 16)
                for q in range(4):
                    high, low = halves(parts[q])
                    yh[q, rows, :] = high
                    yl[q, rows, :] = low

    def transform(q):
        for parity in range(2):
            rows = slice(256 * parity, 256 * parity + 256)
            f = dot3((yh[q, rows, :], yl[q, rows, :]), (t_h[q], t_l[q]))
            high, low = halves(f)
            fh[q, rows, :] = high
            fl[q, rows, :] = low

    for step in range(4):
        for copy in pieces_of(x, x_buffer, x_sems, step):
            copy.wait()
        if step == 3:
            for copy in tables[:2]:
                copy.wait()
        for k in range(4):
            fold(step, k)
    level = levels[0]
    stiffness = stiffness_scalar(level)
    lambdas = [stiffness * column for column in per_mode(LB)]
    firsts = per_mode(SB[0])
    sublane = lax.broadcasted_iota(jnp.int32, (8, 256), 0)
    low_side = {size: sublane % (2 * size) < size for size in (4, 2, 1)}

    def summed(values):
        for size in (4, 2, 1):
            merged = []
            for n in range(size):
                one, other = values[n], values[n + size]
                kept = jnp.where(low_side[size], one, other)
                moved = jnp.where(low_side[size], other, one)
                if size == 4:
                    moved = pltpu.roll(moved, 4, 0)
                else:
                    moved = jnp.where(
                        low_side[size],
                        pltpu.roll(moved, 8 - size, 0),
                        pltpu.roll(moved, size, 0),
                    )
                merged.append(kept + moved)
            values = merged
        return values[0]

    copies = []
    transform(0)
    for copy in tables[2:]:
        copy.wait()
    for q in range(4):
        if q < 3:
            transform(q + 1)
        base = [column + kq[:, 256 * q : 256 * q + 256] for column in lambdas]
        for parity in range(2):
            rows = slice(256 * parity, 256 * parity + 256)
            g = dot3((p_h[parity], p_l[parity]), (fh[q, rows, :], fl[q, rows, :]))
            place = 32 * q + 16 * parity
            totals = [None, None]
            for group in range(2):
                ends = [[], []]
                for a in range(8 * group, 8 * group + 8):
                    shift = stiffness * np.float32(LX[IX[16 * parity + a]])
                    face = np.float32(SX[0, IX[16 * parity + a]])
                    for half in range(2):
                        row = 16 * a + 8 * half
                        w = g[row : row + 8] * inverted(base[half] + shift)
                        w_buffer[2 * q + parity, row : row + 8, :] = w
                        ends[half].append(w * firsts[half])
                        part = face * w
                        totals[half] = part if a == 0 else totals[half] + part
                at = place + 8 * group
                for half in range(2):
                    features[half, at : at + 8, :] = summed(ends[half])
            for half in range(2):
                features[2, place + 8 * half : place + 8 * half + 8, :] = totals[half]
        if q >= 2:
            span = pl.ds(0, 6) if q == 2 else pl.ds(6, 2)
            copy = pltpu.make_async_copy(w_buffer.at[span], w_out.at[span], w_sems.at[q - 2])
            copy.start()
            copies.append(copy)
    last = mode[0] == BLOCKS - 1
    lane = lax.broadcasted_iota(jnp.int32, (8, 128), 1)
    meta = jnp.zeros((8, 128), F32)
    facts = (
        stiffness,
        sweeps[level].astype(F32),
        neighbours[0, 0].astype(F32),
        neighbours[0, 1].astype(F32),
    )
    for n, fact in enumerate(facts):
        meta = jnp.where(lane == n, fact, meta)
    meta = jnp.concatenate([meta] * (DEVICES // 8), axis=0)
    even, odd = features[0].T, features[1].T
    out[pl.ds(0, DEVICES, stride=3), :] = jnp.where(last, even + odd, even)
    out[pl.ds(1, DEVICES, stride=3), :] = jnp.where(last, meta, odd)
    out[pl.ds(2, DEVICES, stride=3), :] = features[2].T
    copy = pltpu.make_async_copy(out, out_hbm, w_sems.at[2])
    copy.start()
    copies.append(copy)
    for copy in copies:
        copy.wait()


def end_responses(shift, extent):
    half = 0.5 * shift
    ratio = 1.0 / (1.0 + half + jnp.sqrt(half * (half + 2.0)))
    square = ratio * ratio
    power = ratio
    for _ in range(extent.bit_length() - 1):
        power = power * power
    rest = power * power
    below = 1.0 / (1.0 - rest * square)
    return ratio * (1.0 - rest) * below, power * (1.0 - square) * below


RATIOS, SCALES, NEAR_FAR, FACE_NEAR, FACE_FAR, Z_SUM = 8, 72, 136, 152, 536, 920


def prepare_kernel(own, w_in, k_own, constants_in, zbasis, numbers, terms, w_out, sem):
    del own
    copy = pltpu.make_async_copy(w_in, w_out, sem)
    copy.start()
    link_scale, link_lambda = constants_in[0:256], constants_in[256:512]
    zsum, lam_z, lam_x = constants_in[512:640], constants_in[640:768], constants_in[768:776]
    k_row = k_own[0]
    numbers[0:8] = jnp.broadcast_to(k_row, (8, 128))
    level = lax.broadcasted_iota(jnp.int32, (8, 128), 0)
    easing = jnp.where(level == 0, 1.0, jnp.where(level == 1, 0.25, 0.0625))
    near, far = end_responses(lam_x + k_row * easing, ROWS)
    numbers[NEAR_FAR : NEAR_FAR + 8] = near
    numbers[NEAR_FAR + 8 : NEAR_FAR + 16] = far
    carry = jnp.zeros((8, 128), F32)
    for m in range(BLOCKS):
        scale = 1.0 / (1.0 - near * carry)
        numbers[RATIOS + 8 * m : RATIOS + 8 * m + 8] = carry
        numbers[SCALES + 8 * m : SCALES + 8 * m + 8] = scale
        carry = near + far * far * carry * scale
    for level in range(3):
        shift = k_row * np.float32(0.25**level)
        face_near, face_far = end_responses(lam_z + shift, BX)
        numbers[FACE_NEAR + 128 * level : FACE_NEAR + 128 * level + 128] = face_near
        numbers[FACE_FAR + 128 * level : FACE_FAR + 128 * level + 128] = face_far
        high, low = halves(link_scale / (link_lambda + shift))
        terms[256 * level : 256 * level + 256] = high
        terms[768 + 256 * level : 768 + 256 * level + 256] = low
    for n in range(4):
        terms[1536 + 128 * n : 1536 + 128 * n + 128] = zbasis[n]
    numbers[Z_SUM : Z_SUM + 128] = zsum
    copy.wait()


def column_kernel(
    inbox, numbers, terms_in, out, x_links, t_faces, turned, passing,
):
    k_row = numbers[0:1]
    links = (terms_in[0:768], terms_in[768:1536])
    zsum = numbers[Z_SUM : Z_SUM + 128]
    zbasis = [terms_in[1536 + 128 * n : 1536 + 128 * n + 128] for n in range(4)]
    meta = inbox[pl.ds(96 * (BLOCKS - 1) + 1, 32, stride=3), :]
    stiff_col = meta[:, 0:1]
    flat = stiff_col < 2.0
    middle = stiff_col < 8.0

    meta_t = meta.T
    facts = jnp.concatenate([meta_t[0:8]] * 4, axis=1)
    stiff, allowed = facts[0:1], facts[1:2]
    west_slot, east_slot = facts[2:3], facts[3:4]
    lane = lax.broadcasted_iota(jnp.int32, (1, 128), 1)
    first_lane = (lane - lane % 32).astype(F32)
    row = lax.broadcasted_iota(jnp.int32, (128, 128), 0).astype(F32)
    west_pick = ((row == first_lane + west_slot) & (west_slot >= 0.0)).astype(F32)
    east_pick = ((row == first_lane + east_slot) & (east_slot >= 0.0)).astype(F32)
    diagonal = stiff * np.float32(2 * NZ + 2 * BX) + np.float32(BX * NZ) * k_row
    coupling = stiff * np.float32(NZ) / diagonal
    column = lax.broadcasted_iota(jnp.int32, (128, 128), 1).astype(F32)
    unit = (row == column).astype(F32)
    step1 = (1.0 - DAMPING) * unit + DAMPING * coupling * (west_pick + east_pick)
    step1_terms = halves(step1)
    step2_terms = halves(dot3(step1_terms, step1_terms))
    step4 = dot3(step2_terms, step2_terms)
    run2 = step1 + unit
    run4 = run2 + dot3(halves(run2), step2_terms)
    run8 = run4 + dot3(halves(run4), halves(step4))
    picks = jnp.concatenate((west_pick, east_pick), axis=1).astype(BF16)
    run_high, run_low = halves(run8)
    sideways = jnp.dot(
        jnp.concatenate((run_high, run_low), axis=1),
        jnp.concatenate((picks, picks), axis=0),
        preferred_element_type=F32,
    )
    passing[0], passing[1] = halves(sideways)
    west_bits = jnp.concatenate([west_pick.astype(BF16)] * 2, axis=0)
    east_bits = jnp.concatenate([east_pick.astype(BF16)] * 2, axis=0)

    def exchange(first, last):
        west = jnp.dot(
            jnp.concatenate(halves(last), axis=1), west_bits, preferred_element_type=F32
        )
        east = jnp.dot(
            jnp.concatenate(halves(first), axis=1), east_bits, preferred_element_type=F32
        )
        return west, east

    def by_level(at):
        values = numbers[at : at + 8]
        return jnp.where(flat, values[0:1], jnp.where(middle, values[1:2], values[2:3]))

    near, far = by_level(NEAR_FAR), by_level(NEAR_FAR + 8)
    held = [(by_level(RATIOS + 8 * m), by_level(SCALES + 8 * m)) for m in range(BLOCKS)]

    def interfaces(even, odd):
        firsts, offsets = [], []
        offset = jnp.zeros((32, 128), F32)
        for m in range(BLOCKS):
            ratio, scale = held[m]
            first, last = even[m] + odd[m], even[m] - odd[m]
            pushed = (first + near * offset) * scale
            offsets.append(offset)
            firsts.append(pushed)
            offset = last + far * (offset + ratio * pushed)
        above = jnp.zeros((32, 128), F32)
        sides = [None] * BLOCKS
        for m in reversed(range(BLOCKS)):
            ratio, scale = held[m]
            head = firsts[m] + far * scale * above
            below = ratio * head + offsets[m]
            sides[m] = (below + above, below - above)
            above = head
        return sides

    def received(kind, m):
        return inbox[pl.ds(96 * m + kind, 32, stride=3), :]

    even = [received(0, m) for m in range(BLOCKS)]
    odd = [received(1, m) for m in range(BLOCKS - 1)] + [jnp.zeros((32, 128), F32)]
    sides = interfaces(even, odd)
    for m in range(BLOCKS):
        x_links[32 * m : 32 * m + 32, 0:128] = sides[m][0]
        x_links[32 * m : 32 * m + 32, 128:256] = sides[m][1]

    stiff_rows = jnp.broadcast_to(jnp.concatenate([stiff_col] * BLOCKS, axis=0), (256, 128))
    hits = [(stiff_rows == np.float32(4.0**level)).astype(BF16) for level in range(3)]

    def spread(value):
        wide = value.shape[1] // 128
        return [
            jnp.concatenate(
                [
                    term[:, 128 * n : 128 * n + 128] * hits[level]
                    for level in range(3)
                    for n in range(wide)
                ],
                axis=1,
            )
            for term in halves(value)
        ]

    faces = jnp.concatenate([received(2, m) for m in range(BLOCKS)], axis=0)
    faces = faces + dot3(spread(x_links[...]), links)

    block = lax.broadcasted_iota(jnp.int32, (16, 128), 1) // 32

    def joined(parts):
        result = parts[0]
        for n in range(1, 4):
            result = jnp.where(block == n, parts[n], result)
        return result

    def turn(value, shift):
        return value if shift % 4 == 0 else pltpu.roll(value, 32 * (shift % 4), 1)

    turned[...] = faces.T
    for m in range(BLOCKS):
        for parity in range(2):
            t_faces[16 * m : 16 * m + 16, 128 * parity : 128 * parity + 128] = joined(
                [
                    turn(
                        turned[
                            32 * q + 16 * parity : 32 * q + 16 * parity + 16,
                            128 * (m // 4) : 128 * (m // 4) + 128,
                        ],
                        q - m,
                    )
                    for q in range(4)
                ]
            )
    modes = dot3((zbasis[0], zbasis[1]), halves(t_faces[...]))
    west_end = modes[:, :128] + modes[:, 128:]
    east_end = modes[:, :128] - modes[:, 128:]

    def by_lane(at):
        values = [numbers[at + 128 * n : at + 128 * n + 128] for n in range(3)]
        return jnp.where(stiff < 2.0, values[0], jnp.where(stiff < 8.0, values[1], values[2]))

    face_near, face_far = by_lane(FACE_NEAR), by_lane(FACE_FAR)
    twice = (allowed > 1.0).astype(F32)
    west1, east1 = exchange(west_end, east_end)
    west1, east1 = west1 * twice, east1 * twice
    first = west_end + face_near * west1 + face_far * east1
    last = east_end + face_far * west1 + face_near * east1
    west2, east2 = exchange(first, last)
    moved = (west2 - west1) + (east2 - east1)
    coarse = stiff * jnp.sum(moved * zsum, axis=0, keepdims=True)
    target = jnp.broadcast_to(DAMPING * coarse / diagonal, (16, 128))
    corrections = dot3(halves(target), (passing[0], passing[1]))
    west3 = west2 + zsum * corrections[0:1, :128]
    east3 = east2 + zsum * corrections[0:1, 128:]
    first = west_end + face_near * west3 + face_far * east3
    last = east_end + face_far * west3 + face_near * east3
    west4, east4 = exchange(first, last)
    again = twice > 0.0
    west = jnp.where(again, west4, west3)
    east = jnp.where(again, east4, east3)
    sums = jnp.concatenate((west + east, west - east), axis=1)
    t_faces[...] = dot3((zbasis[2], zbasis[3]), halves(sums))

    for q in range(4):
        for parity in range(2):
            for h in range(2):
                turned[
                    32 * q + 16 * parity : 32 * q + 16 * parity + 16, 128 * h : 128 * h + 128
                ] = joined(
                    [
                        turn(
                            t_faces[
                                64 * h + 16 * m : 64 * h + 16 * m + 16,
                                128 * parity : 128 * parity + 128,
                            ],
                            m - q,
                        )
                        for m in range(4)
                    ]
                )
    faces = turned[...].T
    for m in range(BLOCKS):
        out[pl.ds(96 * m + 2, 32, stride=3), :] = faces[32 * m : 32 * m + 32]
    levelled = [
        jnp.concatenate([link[256 * n : 256 * n + 256, :] for n in range(3)], axis=1)
        for link in links
    ]
    driven = dot3(spread(faces), levelled, NT)
    sides = interfaces(
        [even[m] + driven[32 * m : 32 * m + 32, 0:128] for m in range(BLOCKS)],
        [odd[m] + driven[32 * m : 32 * m + 32, 128:256] for m in range(BLOCKS)],
    )
    for m in range(BLOCKS):
        for kind in range(2):
            out[pl.ds(96 * m + kind, 32, stride=3), :] = sides[m][kind]


def backward_kernel(
    levels, inbox, w_in, tables, kq, out, features, sums, rows_out, sems,
):
    easing = 1.0 / stiffness_scalar(levels[0])
    for kind in range(3):
        features[kind] = inbox[pl.ds(kind, DEVICES, stride=3), :].T
    firsts, lambdas = per_mode(SB[0]), per_mode(LB)
    for q in range(4):
        base = [column + kq[:, 256 * q : 256 * q + 256] * easing for column in lambdas]
        for parity in range(2):
            place = 32 * q + 16 * parity
            side = features[2, place : place + 16, :]
            terms = []
            for a in range(16):
                shift = np.float32(LX[IX[16 * parity + a]])
                face = np.float32(SX[0, IX[16 * parity + a]])
                pair = []
                for half in range(2):
                    row = 16 * a + 8 * half
                    end = features[half, place + a : place + a + 1, :]
                    drive = firsts[half] * end + face * side[8 * half : 8 * half + 8]
                    w = w_in[2 * q + parity, row : row + 8, :]
                    pair.append(w + drive * inverted(base[half] + shift))
                terms.append(halves(jnp.concatenate(pair, axis=0)))
            u = [jnp.concatenate([t[h] for t in terms], axis=0) for h in range(2)]
            sums[q, 256 * parity : 256 * parity + 256, :] = dot3(u, (tables[q], tables[4 + q]), NT)
    copies = []
    for n in range(4):
        cut = slice(256 * n, 256 * n + 256)
        sides = []
        for parity in range(2):
            terms = []
            for k in range(16):
                rows = slice(256 * parity + 16 * k, 256 * parity + 16 * k + 16)
                p0, p2, p1, p5 = (sums[q, rows, :] for q in range(4))
                e = p0 + p2 if n % 2 == 0 else p0 - p2
                half = slice(128 * (n % 2), 128 * (n % 2) + 128)
                turn = (p1 - p5) * ROOT_HALF
                mixed = turn[:, :128] + turn[:, 128:] if n % 2 == 0 else turn[:, 128:] - turn[:, :128]
                f = jnp.concatenate((p1[:, half] + p5[:, half], mixed), axis=1)
                terms.append(halves(e + f if n < 2 else e - f))
            v = [jnp.concatenate([t[h] for t in terms], axis=0) for h in range(2)]
            sides.append(dot3((tables[12 + parity], tables[14 + parity]), v))
        spans = {15: [(0, 32, n)]} if n < 3 else {7: [(0, 8, 3), (24, 8, 4)], 15: [(8, 16, 5)]}
        for k in range(16):
            rows = slice(16 * k, 16 * k + 16)
            rows_out[k, :, cut] = sides[0][rows] + sides[1][rows]
            rows_out[31 - k, :, cut] = sides[0][rows] - sides[1][rows]
            for at, size, sem in spans.get(k, ()):
                place = (pl.ds(at, size), slice(None), pl.ds(256 * n, 256))
                copy = pltpu.make_async_copy(rows_out.at[place], out.at[place], sems.at[sem])
                copy.start()
                copies.append(copy)
    for copy in copies:
        copy.wait()


def whole(shape):
    return pl.BlockSpec(shape, lambda *_: (0,) * len(shape))


SMEM = pl.BlockSpec(memory_space=pltpu.SMEM)
VMEM = pl.BlockSpec(memory_space=pltpu.VMEM)


HBM = pl.BlockSpec(memory_space=pltpu.HBM)
GRANT = pltpu.CompilerParams(vmem_limit_bytes=20 * 2**20)


def constants():
    tables = []
    for table in (T, PLANE, np.swapaxes(PLANE, 1, 2)):
        tables.extend(two_terms(table))
    return jnp.asarray(np.concatenate(tables)), jnp.asarray(KQ[None, :], F32)


def run_forward(levels, neighbours, sweeps, mode, x, **kw):
    return pl.pallas_call(
        forward_kernel,
        in_specs=[SMEM] * 4 + [HBM] * 2 + [VMEM],
        out_specs=[HBM, HBM],
        out_shape=[
            jax.ShapeDtypeStruct((768, 128), F32),
            jax.ShapeDtypeStruct((8, 256, 256), F32),
        ],
        scratch_shapes=[
            pltpu.VMEM((768, 128), F32),
            pltpu.VMEM((BX, ROWS, NY), F32),
            pltpu.VMEM((2, 256, 256), BF16),
            pltpu.VMEM((2, 256, 256), BF16),
            pltpu.VMEM((4, 256, 256), BF16),
            pltpu.VMEM((4, 256, 256), BF16),
            pltpu.VMEM((4, 512, 256), BF16),
            pltpu.VMEM((4, 512, 256), BF16),
            pltpu.VMEM((4, 512, 256), BF16),
            pltpu.VMEM((4, 512, 256), BF16),
            pltpu.VMEM((8, 256, 256), F32),
            pltpu.VMEM((3, 128, 256), F32),
            pltpu.SemaphoreType.DMA((2, 4)),
            pltpu.SemaphoreType.DMA((4,)),
            pltpu.SemaphoreType.DMA((3,)),
        ],
        name="forward",
        **kw,
    )(levels, neighbours, sweeps, mode, x, *constants())


def run_prepare(device, w, **kw):
    zbasis = np.stack([t for table in (ZBASIS, ZBASIS.T) for t in two_terms(table)])
    wide = np.ones((1, 128))
    numbers = np.concatenate(
        (
            LINK_SCALE, LINK_LAMBDA, ZSUM * wide, LZ[:, None] * wide,
            np.tile(LX[IX], 4)[None, :] * np.ones((8, 1)),
        )
    )
    shapes = [((Z_SUM + 128, 128), F32), ((2048, 128), BF16), (w.shape, F32)]
    return pl.pallas_call(
        prepare_kernel,
        grid_spec=pltpu.PrefetchScalarGridSpec(
            num_scalar_prefetch=1,
            grid=(1,),
            in_specs=[
                HBM,
                pl.BlockSpec((1, 1, 128), lambda i, own: (own[0], 0, 0)),
                whole(numbers.shape),
                whole(zbasis.shape),
            ],
            out_specs=[VMEM] * len(shapes),
            scratch_shapes=[pltpu.SemaphoreType.DMA],
        ),
        out_shape=[jax.ShapeDtypeStruct(*shape) for shape in shapes],
        compiler_params=GRANT,
        name="prepare",
        **kw,
    )(device, w, jnp.asarray(KQ_OWN, F32), jnp.asarray(numbers, F32), jnp.asarray(zbasis))


def run_columns(inbox, numbers, terms, **kw):
    return pl.pallas_call(
        column_kernel,
        in_specs=[VMEM] * 3,
        out_specs=VMEM,
        scratch_shapes=[
            pltpu.VMEM((256, 256), F32),
            pltpu.VMEM((128, 256), F32),
            pltpu.VMEM((128, 256), F32),
            pltpu.VMEM((2, 128, 256), BF16),
        ],
        out_shape=jax.ShapeDtypeStruct((768, 128), F32),
        compiler_params=GRANT,
        name="columns",
        **kw,
    )(inbox, numbers, terms)


def run_backward(levels, inbox, w, **kw):
    return pl.pallas_call(
        backward_kernel,
        in_specs=[SMEM] + [VMEM] * 4,
        out_specs=HBM,
        out_shape=jax.ShapeDtypeStruct((BX, ROWS, NY), F32),
        scratch_shapes=[
            pltpu.VMEM((3, 128, 256), F32),
            pltpu.VMEM((4, 512, 256), F32),
            pltpu.VMEM((BX, ROWS, NY), F32),
            pltpu.SemaphoreType.DMA((6,)),
        ],
        compiler_params=GRANT,
        name="backward",
        **kw,
    )(levels, inbox, w, *constants())


def traded(outbox):
    pieces = outbox.reshape(DEVICES, 1, 384)
    pieces = lax.all_to_all(pieces, ("mode", "blk"), split_axis=0, concat_axis=0, tiled=True)
    return pieces.reshape(3 * DEVICES, 128)


def body(divergence, neighbours, levels, sweeps):
    mode = lax.axis_index("mode").astype(jnp.int32)
    device = mode * 32 + lax.axis_index("blk").astype(jnp.int32)
    outbox, w = run_forward(levels, neighbours, sweeps, mode[None], divergence[0])
    numbers, terms, w = run_prepare(device[None], w)
    outbox = run_columns(traded(outbox), numbers, terms)
    return run_backward(levels, traded(outbox), w)[None]


def solution(mesh):
    return jax.shard_map(
        body,
        mesh=mesh,
        in_specs=(P("blk", None, "mode", None), P("blk", None), P("blk"), P()),
        out_specs=P("blk", None, "mode", None),
        check_vma=False,
    )
```

```python
import functools
import math

import jax
import jax.numpy as jnp
import numpy as np
from jax import lax
from jax.experimental import pallas as pl
from jax.experimental.pallas import tpu as pltpu
from jax.sharding import PartitionSpec as P

NY = 1024
BX = 32
NZ = 128
CITERS = 8
DAMPING = 0.8
REACH = 3
BLOCKS = 8
ROWS = NZ // BLOCKS
DEVICES = 256
F32 = jnp.float32
BF16 = jnp.bfloat16


def sine_table(extent):
    ordinal = np.arange(1, extent + 1)
    angles = np.pi * np.outer(ordinal, ordinal) / (extent + 1)
    matrix = np.sqrt(2.0 / (extent + 1)) * np.sin(angles)
    return matrix, 4.0 * np.sin(np.pi * ordinal / (2 * (extent + 1))) ** 2


def two_terms(array):
    high = np.asarray(array, np.float32).astype(BF16)
    low = (np.asarray(array, np.float64) - high.astype(np.float64)).astype(BF16)
    return high, low


def fourier_class(length, cosines, sines):
    y = np.arange(length)
    columns = []
    for waves, function in ((cosines, np.cos), (sines, np.sin)):
        for m in waves:
            weight = (1.0 if m in (0, NY // 2) else 2.0) / NY
            columns.append(math.sqrt(weight) * function(2 * np.pi * ((m * y) % NY) / NY))
    waves = np.concatenate((np.array(cosines), np.array(sines)))
    return np.stack(columns, axis=1), 4.0 * np.sin(np.pi * waves / NY) ** 2


def odd_class(residue):
    y = np.arange(128)
    columns = []
    waves = []
    for function in (0, 1):
        for m in range(residue, NY, 8):
            angle = 2 * np.pi * ((m * y) % NY) / NY
            if function == 0:
                column = np.concatenate((np.cos(angle), -np.sin(angle)))
            else:
                column = np.concatenate((np.sin(angle), np.cos(angle)))
                column = column if m < NY // 2 else -column
            columns.append(math.sqrt(2.0 / NY) * column)
            waves.append(min(m, NY - m))
    return np.stack(columns, axis=1), 4.0 * np.sin(np.pi * np.array(waves) / NY) ** 2


SX, LX = sine_table(BX)
SB, LB = sine_table(ROWS)
SZ, LZ = sine_table(NZ)
IX = np.concatenate((np.arange(0, BX, 2), np.arange(1, BX, 2)))
JB = np.concatenate((np.arange(0, ROWS, 2), np.arange(1, ROWS, 2)))
T0, K0 = fourier_class(256, range(0, 513, 4), range(4, 512, 4))
T2, K2 = fourier_class(256, range(2, 512, 4), range(2, 512, 4))
T1, K1 = odd_class(1)
T5, K5 = odd_class(5)
T = np.stack((T0, T2, T1, T5))
KQ = np.concatenate((K0, K2, K1, K5))
ROOT_HALF = math.sqrt(0.5)


def plane_table(parity):
    ways = SX[IX[16 * parity : 16 * parity + 16], :16]
    return np.einsum("ix,jz->ijxz", ways, SB[JB]).reshape(256, 256)


PLANE = np.stack((plane_table(0), plane_table(1)))
ZBASIS = np.einsum("jmz,kz->jmk", SZ.reshape(NZ, BLOCKS, ROWS), SB[JB]).reshape(NZ, NZ)
ZSUM = SZ.sum(axis=0).reshape(NZ, 1)


def link_tables():
    scale = np.zeros((2, 4, 32, 4, 2, 16))
    lam = np.zeros((2, 4, 32, 4, 2, 16))
    for half in range(2):
        for q in range(4):
            for a in range(32):
                lam[half, q, a] = LX[IX[a]] + LB[JB][None, None, :]
                for b in range(8 * half, 8 * half + 8):
                    scale[half, q, a, q, a // 16, b] = SX[0, IX[a]] * SB[0, JB[b]]
    return scale.reshape(256, 128), lam.reshape(256, 128)


LINK_SCALE, LINK_LAMBDA = link_tables()
KQ_OWN = np.repeat(KQ.reshape(4, DEVICES).T, 32, axis=1).reshape(DEVICES, 1, 128)


def halves(value):
    high = value.astype(BF16)
    return high, (value - high.astype(F32)).astype(BF16)


NN = (((1,), (0,)), ((), ()))
NT = (((1,), (1,)), ((), ()))


def dot3(a, b, dims=NN):
    ah, al = a
    bh, bl = b
    return lax.dot_general(
        jnp.concatenate((ah, al, ah), axis=1),
        jnp.concatenate((bh, bh, bl), axis=dims[0][1][0]),
        dims,
        preferred_element_type=F32,
    )


def inverted(value):
    guess = pl.reciprocal(value, approx=True)
    return guess * (2.0 - value * guess)


def stiffness_scalar(level):
    return lax.shift_left(jnp.int32(1), 2 * level).astype(F32)


def per_mode(values):
    iota = lax.broadcasted_iota(jnp.int32, (8, 256), 0)
    halves_of = []
    for half in range(2):
        column = jnp.zeros((8, 256), F32)
        for b in range(8):
            column = jnp.where(iota == b, np.float32(values[JB[8 * half + b]]), column)
        halves_of.append(column)
    return halves_of


def pieces_of(x, x_buffer, x_sems, step):
    first, second = 4 * step, 28 - 4 * step
    return [
        pltpu.make_async_copy(x.at[pl.ds(at, 4)], x_buffer.at[pl.ds(at, 4)], x_sems.at[n, step])
        for n, at in enumerate((first, second))
    ]


def forward_kernel(
    levels, neighbours, sweeps, mode, x, tables_in, kq,
    out_hbm, w_out, out, x_buffer, p_h, p_l, t_h, t_l, yh, yl, fh, fl, w_buffer, features,
    x_sems, t_sems, w_sems,
):
    tables = [
        pltpu.make_async_copy(source, place, t_sems.at[n])
        for n, (source, place) in enumerate(
            (
                (tables_in.at[pl.ds(0, 4)], t_h), (tables_in.at[pl.ds(4, 4)], t_l),
                (tables_in.at[pl.ds(8, 2)], p_h), (tables_in.at[pl.ds(10, 2)], p_l),
            )
        )
    ]
    for step in range(4):
        for copy in pieces_of(x, x_buffer, x_sems, step):
            copy.start()
    for copy in tables:
        copy.start()

    def fold(step, k):
        for parity in range(2):
            for k in (k,):
                a, b = x_buffer[4 * step + k], x_buffer[31 - 4 * step - k]
                v = a + b if parity == 0 else a - b
                v0, v1, v2, v3 = (v[:, 256 * n : 256 * n + 256] for n in range(4))
                e0, e1 = v0 + v2, v1 + v3
                f, g = v0 - v2, v1 - v3
                f0, f1 = f[:, :128], f[:, 128:] * ROOT_HALF
                g0, g1 = g[:, :128], g[:, 128:] * ROOT_HALF
                turn0, turn1 = f1 - g1, f1 + g1
                parts = (
                    e0 + e1,
                    e0 - e1,
                    jnp.concatenate((f0 + turn0, g0 + turn1), axis=1),
                    jnp.concatenate((f0 - turn0, g0 - turn1), axis=1),
                )
                at = 256 * parity + 16 * (4 * step + k)
                rows = slice(at, at + 16)
                for q in range(4):
                    high, low = halves(parts[q])
                    yh[q, rows, :] = high
                    yl[q, rows, :] = low

    def transform(unit):
        q, parity = divmod(unit, 2)
        rows = slice(256 * parity, 256 * parity + 256)
        high, low = halves(dot3((yh[q, rows, :], yl[q, rows, :]), (t_h[q], t_l[q])))
        fh[q, rows, :] = high
        fl[q, rows, :] = low

    def in_plane(unit):
        q, parity = divmod(unit, 2)
        rows = slice(256 * parity, 256 * parity + 256)
        w_buffer[unit] = dot3((p_h[parity], p_l[parity]), (fh[q, rows, :], fl[q, rows, :]))

    for step in range(4):
        for copy in pieces_of(x, x_buffer, x_sems, step):
            copy.wait()
        if step == 3:
            for copy in tables:
                copy.wait()
        for k in range(4):
            fold(step, k)
    level = levels[0]
    stiffness = stiffness_scalar(level)
    lambdas = [stiffness * column for column in per_mode(LB)]
    firsts = per_mode(SB[0])
    sublane = lax.broadcasted_iota(jnp.int32, (8, 256), 0)
    low_side = {size: sublane % (2 * size) < size for size in (4, 2, 1)}

    def summed(values):
        for size in (4, 2, 1):
            merged = []
            for n in range(size):
                one, other = values[n], values[n + size]
                kept = jnp.where(low_side[size], one, other)
                moved = jnp.where(low_side[size], other, one)
                if size == 4:
                    moved = pltpu.roll(moved, 4, 0)
                else:
                    moved = jnp.where(
                        low_side[size],
                        pltpu.roll(moved, 8 - size, 0),
                        pltpu.roll(moved, size, 0),
                    )
                merged.append(kept + moved)
            values = merged
        return values[0]

    def divide(unit):
        q, parity = divmod(unit, 2)
        base = [column + kq[:, 256 * q : 256 * q + 256] for column in lambdas]
        place = 32 * q + 16 * parity
        totals = [None, None]
        for group in range(2):
            ends = [[], []]
            for a in range(8 * group, 8 * group + 8):
                shift = stiffness * np.float32(LX[IX[16 * parity + a]])
                face = np.float32(SX[0, IX[16 * parity + a]])
                for half in range(2):
                    row = slice(16 * a + 8 * half, 16 * a + 8 * half + 8)
                    w = w_buffer[unit, row, :] * inverted(base[half] + shift)
                    w_buffer[unit, row, :] = w
                    ends[half].append(w * firsts[half])
                    part = face * w
                    totals[half] = part if a == 0 else totals[half] + part
            at = place + 8 * group
            for half in range(2):
                features[half, at : at + 8, :] = summed(ends[half])
        for half in range(2):
            features[2, place + 8 * half : place + 8 * half + 8, :] = totals[half]

    copies = []
    transform(0)
    for unit in range(8):
        if unit < 7:
            transform(unit + 1)
        in_plane(unit)
        divide(unit)
        q, parity = divmod(unit, 2)
        if q >= 2 and parity == 1:
            span = pl.ds(0, 6) if q == 2 else pl.ds(6, 2)
            copy = pltpu.make_async_copy(w_buffer.at[span], w_out.at[span], w_sems.at[q - 2])
            copy.start()
            copies.append(copy)
    last = mode[0] == BLOCKS - 1
    lane = lax.broadcasted_iota(jnp.int32, (8, 128), 1)
    meta = jnp.zeros((8, 128), F32)
    facts = (
        stiffness,
        sweeps[level].astype(F32),
        neighbours[0, 0].astype(F32),
        neighbours[0, 1].astype(F32),
    )
    for n, fact in enumerate(facts):
        meta = jnp.where(lane == n, fact, meta)
    meta = jnp.concatenate([meta] * (DEVICES // 8), axis=0)
    even, odd = features[0].T, features[1].T
    out[pl.ds(0, DEVICES, stride=3), :] = jnp.where(last, even + odd, even)
    out[pl.ds(1, DEVICES, stride=3), :] = jnp.where(last, meta, odd)
    out[pl.ds(2, DEVICES, stride=3), :] = features[2].T
    copy = pltpu.make_async_copy(out, out_hbm, w_sems.at[2])
    copy.start()
    copies.append(copy)
    for copy in copies:
        copy.wait()


def end_responses(shift, extent):
    half = 0.5 * shift
    ratio = 1.0 / (1.0 + half + jnp.sqrt(half * (half + 2.0)))
    square = ratio * ratio
    power = ratio
    for _ in range(extent.bit_length() - 1):
        power = power * power
    rest = power * power
    below = 1.0 / (1.0 - rest * square)
    return ratio * (1.0 - rest) * below, power * (1.0 - square) * below


RATIOS, SCALES, NEAR_FAR, FACE_NEAR, FACE_FAR, Z_SUM = 8, 72, 136, 152, 536, 920


def prepare_kernel(own, w_in, k_own, constants_in, zbasis, numbers, terms, w_out, sem):
    del own
    copy = pltpu.make_async_copy(w_in, w_out, sem)
    copy.start()
    link_scale, link_lambda = constants_in[0:256], constants_in[256:512]
    zsum, lam_z, lam_x = constants_in[512:640], constants_in[640:768], constants_in[768:776]
    k_row = k_own[0]
    numbers[0:8] = jnp.broadcast_to(k_row, (8, 128))
    level = lax.broadcasted_iota(jnp.int32, (8, 128), 0)
    easing = jnp.where(level == 0, 1.0, jnp.where(level == 1, 0.25, 0.0625))
    near, far = end_responses(lam_x + k_row * easing, ROWS)
    numbers[NEAR_FAR : NEAR_FAR + 8] = near
    numbers[NEAR_FAR + 8 : NEAR_FAR + 16] = far
    carry = jnp.zeros((8, 128), F32)
    for m in range(BLOCKS):
        scale = 1.0 / (1.0 - near * carry)
        numbers[RATIOS + 8 * m : RATIOS + 8 * m + 8] = carry
        numbers[SCALES + 8 * m : SCALES + 8 * m + 8] = scale
        carry = near + far * far * carry * scale
    for level in range(3):
        shift = k_row * np.float32(0.25**level)
        face_near, face_far = end_responses(lam_z + shift, BX)
        numbers[FACE_NEAR + 128 * level : FACE_NEAR + 128 * level + 128] = face_near
        numbers[FACE_FAR + 128 * level : FACE_FAR + 128 * level + 128] = face_far
        high, low = halves(link_scale / (link_lambda + shift))
        terms[256 * level : 256 * level + 256] = high
        terms[768 + 256 * level : 768 + 256 * level + 256] = low
    for n in range(4):
        terms[1536 + 128 * n : 1536 + 128 * n + 128] = zbasis[n]
    numbers[Z_SUM : Z_SUM + 128] = zsum
    copy.wait()


def column_kernel(
    inbox, numbers, terms_in, out, x_links, t_faces, turned, passing,
):
    k_row = numbers[0:1]
    links = (terms_in[0:768], terms_in[768:1536])
    zsum = numbers[Z_SUM : Z_SUM + 128]
    zbasis = [terms_in[1536 + 128 * n : 1536 + 128 * n + 128] for n in range(4)]
    meta = inbox[pl.ds(3 * (BLOCKS - 1) + 1, 32, stride=24), :]
    stiff_col = meta[:, 0:1]
    flat = stiff_col < 2.0
    middle = stiff_col < 8.0

    meta_t = meta.T
    facts = jnp.concatenate([meta_t[0:8]] * 4, axis=1)
    stiff, allowed = facts[0:1], facts[1:2]
    west_slot, east_slot = facts[2:3], facts[3:4]
    lane = lax.broadcasted_iota(jnp.int32, (1, 128), 1)
    first_lane = (lane - lane % 32).astype(F32)
    row = lax.broadcasted_iota(jnp.int32, (128, 128), 0).astype(F32)
    west_pick = ((row == first_lane + west_slot) & (west_slot >= 0.0)).astype(F32)
    east_pick = ((row == first_lane + east_slot) & (east_slot >= 0.0)).astype(F32)
    diagonal = stiff * np.float32(2 * NZ + 2 * BX) + np.float32(BX * NZ) * k_row
    coupling = stiff * np.float32(NZ) / diagonal
    column = lax.broadcasted_iota(jnp.int32, (128, 128), 1).astype(F32)
    unit = (row == column).astype(F32)
    step1 = (1.0 - DAMPING) * unit + DAMPING * coupling * (west_pick + east_pick)
    step1_terms = halves(step1)
    step2_terms = halves(dot3(step1_terms, step1_terms))
    step4 = dot3(step2_terms, step2_terms)
    run2 = step1 + unit
    run4 = run2 + dot3(halves(run2), step2_terms)
    run8 = run4 + dot3(halves(run4), halves(step4))
    picks = jnp.concatenate((west_pick, east_pick), axis=1).astype(BF16)
    run_high, run_low = halves(run8)
    sideways = jnp.dot(
        jnp.concatenate((run_high, run_low), axis=1),
        jnp.concatenate((picks, picks), axis=0),
        preferred_element_type=F32,
    )
    passing[0], passing[1] = halves(sideways)
    west_bits = jnp.concatenate([west_pick.astype(BF16)] * 2, axis=0)
    east_bits = jnp.concatenate([east_pick.astype(BF16)] * 2, axis=0)

    def exchange(first, last):
        west = jnp.dot(
            jnp.concatenate(halves(last), axis=1), west_bits, preferred_element_type=F32
        )
        east = jnp.dot(
            jnp.concatenate(halves(first), axis=1), east_bits, preferred_element_type=F32
        )
        return west, east

    def by_level(at):
        values = numbers[at : at + 8]
        return jnp.where(flat, values[0:1], jnp.where(middle, values[1:2], values[2:3]))

    near, far = by_level(NEAR_FAR), by_level(NEAR_FAR + 8)
    held = [(by_level(RATIOS + 8 * m), by_level(SCALES + 8 * m)) for m in range(BLOCKS)]

    def interfaces(even, odd):
        firsts, offsets = [], []
        offset = jnp.zeros((32, 128), F32)
        for m in range(BLOCKS):
            ratio, scale = held[m]
            first, last = even[m] + odd[m], even[m] - odd[m]
            pushed = (first + near * offset) * scale
            offsets.append(offset)
            firsts.append(pushed)
            offset = last + far * (offset + ratio * pushed)
        above = jnp.zeros((32, 128), F32)
        sides = [None] * BLOCKS
        for m in reversed(range(BLOCKS)):
            ratio, scale = held[m]
            head = firsts[m] + far * scale * above
            below = ratio * head + offsets[m]
            sides[m] = (below + above, below - above)
            above = head
        return sides

    def received(kind, m):
        return inbox[pl.ds(3 * m + kind, 32, stride=24), :]

    even = [received(0, m) for m in range(BLOCKS)]
    odd = [received(1, m) for m in range(BLOCKS - 1)] + [jnp.zeros((32, 128), F32)]
    sides = interfaces(even, odd)
    for m in range(BLOCKS):
        x_links[32 * m : 32 * m + 32, 0:128] = sides[m][0]
        x_links[32 * m : 32 * m + 32, 128:256] = sides[m][1]

    stiff_rows = jnp.broadcast_to(jnp.concatenate([stiff_col] * BLOCKS, axis=0), (256, 128))
    hits = [(stiff_rows == np.float32(4.0**level)).astype(BF16) for level in range(3)]

    def spread(value):
        wide = value.shape[1] // 128
        return [
            jnp.concatenate(
                [
                    term[:, 128 * n : 128 * n + 128] * hits[level]
                    for level in range(3)
                    for n in range(wide)
                ],
                axis=1,
            )
            for term in halves(value)
        ]

    faces = jnp.concatenate([received(2, m) for m in range(BLOCKS)], axis=0)
    faces = faces + dot3(spread(x_links[...]), links)

    block = lax.broadcasted_iota(jnp.int32, (16, 128), 1) // 32

    def joined(parts):
        result = parts[0]
        for n in range(1, 4):
            result = jnp.where(block == n, parts[n], result)
        return result

    def turn(value, shift):
        return value if shift % 4 == 0 else pltpu.roll(value, 32 * (shift % 4), 1)

    turned[...] = faces.T
    for m in range(BLOCKS):
        for parity in range(2):
            t_faces[16 * m : 16 * m + 16, 128 * parity : 128 * parity + 128] = joined(
                [
                    turn(
                        turned[
                            32 * q + 16 * parity : 32 * q + 16 * parity + 16,
                            128 * (m // 4) : 128 * (m // 4) + 128,
                        ],
                        q - m,
                    )
                    for q in range(4)
                ]
            )
    modes = dot3((zbasis[0], zbasis[1]), halves(t_faces[...]))
    west_end = modes[:, :128] + modes[:, 128:]
    east_end = modes[:, :128] - modes[:, 128:]

    def by_lane(at):
        values = [numbers[at + 128 * n : at + 128 * n + 128] for n in range(3)]
        return jnp.where(stiff < 2.0, values[0], jnp.where(stiff < 8.0, values[1], values[2]))

    face_near, face_far = by_lane(FACE_NEAR), by_lane(FACE_FAR)
    twice = (allowed > 1.0).astype(F32)
    west1, east1 = exchange(west_end, east_end)
    west1, east1 = west1 * twice, east1 * twice
    first = west_end + face_near * west1 + face_far * east1
    last = east_end + face_far * west1 + face_near * east1
    west2, east2 = exchange(first, last)
    moved = (west2 - west1) + (east2 - east1)
    coarse = stiff * jnp.sum(moved * zsum, axis=0, keepdims=True)
    target = jnp.broadcast_to(DAMPING * coarse / diagonal, (16, 128))
    corrections = dot3(halves(target), (passing[0], passing[1]))
    west3 = west2 + zsum * corrections[0:1, :128]
    east3 = east2 + zsum * corrections[0:1, 128:]
    first = west_end + face_near * west3 + face_far * east3
    last = east_end + face_far * west3 + face_near * east3
    west4, east4 = exchange(first, last)
    again = twice > 0.0
    west = jnp.where(again, west4, west3)
    east = jnp.where(again, east4, east3)
    sums = jnp.concatenate((west + east, west - east), axis=1)
    t_faces[...] = dot3((zbasis[2], zbasis[3]), halves(sums))

    for q in range(4):
        for parity in range(2):
            for h in range(2):
                turned[
                    32 * q + 16 * parity : 32 * q + 16 * parity + 16, 128 * h : 128 * h + 128
                ] = joined(
                    [
                        turn(
                            t_faces[
                                64 * h + 16 * m : 64 * h + 16 * m + 16,
                                128 * parity : 128 * parity + 128,
                            ],
                            m - q,
                        )
                        for m in range(4)
                    ]
                )
    faces = turned[...].T
    for m in range(BLOCKS):
        out[pl.ds(3 * m + 2, 32, stride=24), :] = faces[32 * m : 32 * m + 32]
    levelled = [
        jnp.concatenate([link[256 * n : 256 * n + 256, :] for n in range(3)], axis=1)
        for link in links
    ]
    driven = dot3(spread(faces), levelled, NT)
    sides = interfaces(
        [even[m] + driven[32 * m : 32 * m + 32, 0:128] for m in range(BLOCKS)],
        [odd[m] + driven[32 * m : 32 * m + 32, 128:256] for m in range(BLOCKS)],
    )
    for m in range(BLOCKS):
        for kind in range(2):
            out[pl.ds(3 * m + kind, 32, stride=24), :] = sides[m][kind]


def backward_kernel(
    levels, inbox, w_in, tables, kq, out, features, sums, rows_out, sems,
):
    easing = 1.0 / stiffness_scalar(levels[0])
    for kind in range(3):
        features[kind] = inbox[pl.ds(kind, DEVICES, stride=3), :].T
    firsts, lambdas = per_mode(SB[0]), per_mode(LB)
    for q in range(4):
        base = [column + kq[:, 256 * q : 256 * q + 256] * easing for column in lambdas]
        for parity in range(2):
            place = 32 * q + 16 * parity
            side = features[2, place : place + 16, :]
            terms = []
            for a in range(16):
                shift = np.float32(LX[IX[16 * parity + a]])
                face = np.float32(SX[0, IX[16 * parity + a]])
                pair = []
                for half in range(2):
                    row = 16 * a + 8 * half
                    end = features[half, place + a : place + a + 1, :]
                    drive = firsts[half] * end + face * side[8 * half : 8 * half + 8]
                    w = w_in[2 * q + parity, row : row + 8, :]
                    pair.append(w + drive * inverted(base[half] + shift))
                terms.append(halves(jnp.concatenate(pair, axis=0)))
            u = [jnp.concatenate([t[h] for t in terms], axis=0) for h in range(2)]
            sums[q, 256 * parity : 256 * parity + 256, :] = dot3(u, (tables[q], tables[4 + q]), NT)
    copies = []
    for n in range(4):
        cut = slice(256 * n, 256 * n + 256)
        sides = []
        for parity in range(2):
            terms = []
            for k in range(16):
                rows = slice(256 * parity + 16 * k, 256 * parity + 16 * k + 16)
                p0, p2, p1, p5 = (sums[q, rows, :] for q in range(4))
                e = p0 + p2 if n % 2 == 0 else p0 - p2
                half = slice(128 * (n % 2), 128 * (n % 2) + 128)
                turn = (p1 - p5) * ROOT_HALF
                mixed = turn[:, :128] + turn[:, 128:] if n % 2 == 0 else turn[:, 128:] - turn[:, :128]
                f = jnp.concatenate((p1[:, half] + p5[:, half], mixed), axis=1)
                terms.append(halves(e + f if n < 2 else e - f))
            v = [jnp.concatenate([t[h] for t in terms], axis=0) for h in range(2)]
            sides.append(dot3((tables[12 + parity], tables[14 + parity]), v))
        spans = {15: [(0, 32, n)]} if n < 3 else {7: [(0, 8, 3), (24, 8, 4)], 15: [(8, 16, 5)]}
        for k in range(16):
            rows = slice(16 * k, 16 * k + 16)
            rows_out[k, :, cut] = sides[0][rows] + sides[1][rows]
            rows_out[31 - k, :, cut] = sides[0][rows] - sides[1][rows]
            for at, size, sem in spans.get(k, ()):
                place = (pl.ds(at, size), slice(None), pl.ds(256 * n, 256))
                copy = pltpu.make_async_copy(rows_out.at[place], out.at[place], sems.at[sem])
                copy.start()
                copies.append(copy)
    for copy in copies:
        copy.wait()


def whole(shape):
    return pl.BlockSpec(shape, lambda *_: (0,) * len(shape))


SMEM = pl.BlockSpec(memory_space=pltpu.SMEM)
VMEM = pl.BlockSpec(memory_space=pltpu.VMEM)


HBM = pl.BlockSpec(memory_space=pltpu.HBM)
GRANT = pltpu.CompilerParams(vmem_limit_bytes=20 * 2**20)


def constants():
    tables = []
    for table in (T, PLANE, np.swapaxes(PLANE, 1, 2)):
        tables.extend(two_terms(table))
    return jnp.asarray(np.concatenate(tables)), jnp.asarray(KQ[None, :], F32)


def run_forward(levels, neighbours, sweeps, mode, x, **kw):
    return pl.pallas_call(
        forward_kernel,
        in_specs=[SMEM] * 4 + [HBM] * 2 + [VMEM],
        out_specs=[HBM, HBM],
        out_shape=[
            jax.ShapeDtypeStruct((768, 128), F32),
            jax.ShapeDtypeStruct((8, 256, 256), F32),
        ],
        scratch_shapes=[
            pltpu.VMEM((768, 128), F32),
            pltpu.VMEM((BX, ROWS, NY), F32),
            pltpu.VMEM((2, 256, 256), BF16),
            pltpu.VMEM((2, 256, 256), BF16),
            pltpu.VMEM((4, 256, 256), BF16),
            pltpu.VMEM((4, 256, 256), BF16),
            pltpu.VMEM((4, 512, 256), BF16),
            pltpu.VMEM((4, 512, 256), BF16),
            pltpu.VMEM((4, 512, 256), BF16),
            pltpu.VMEM((4, 512, 256), BF16),
            pltpu.VMEM((8, 256, 256), F32),
            pltpu.VMEM((3, 128, 256), F32),
            pltpu.SemaphoreType.DMA((2, 4)),
            pltpu.SemaphoreType.DMA((4,)),
            pltpu.SemaphoreType.DMA((3,)),
        ],
        name="forward",
        **kw,
    )(levels, neighbours, sweeps, mode, x, *constants())


def run_prepare(device, w, **kw):
    zbasis = np.stack([t for table in (ZBASIS, ZBASIS.T) for t in two_terms(table)])
    wide = np.ones((1, 128))
    numbers = np.concatenate(
        (
            LINK_SCALE, LINK_LAMBDA, ZSUM * wide, LZ[:, None] * wide,
            np.tile(LX[IX], 4)[None, :] * np.ones((8, 1)),
        )
    )
    shapes = [((Z_SUM + 128, 128), F32), ((2048, 128), BF16), (w.shape, F32)]
    return pl.pallas_call(
        prepare_kernel,
        grid_spec=pltpu.PrefetchScalarGridSpec(
            num_scalar_prefetch=1,
            grid=(1,),
            in_specs=[
                HBM,
                pl.BlockSpec((1, 1, 128), lambda i, own: (own[0], 0, 0)),
                whole(numbers.shape),
                whole(zbasis.shape),
            ],
            out_specs=[VMEM] * len(shapes),
            scratch_shapes=[pltpu.SemaphoreType.DMA],
        ),
        out_shape=[jax.ShapeDtypeStruct(*shape) for shape in shapes],
        compiler_params=GRANT,
        name="prepare",
        **kw,
    )(device, w, jnp.asarray(KQ_OWN, F32), jnp.asarray(numbers, F32), jnp.asarray(zbasis))


def run_columns(inbox, numbers, terms, **kw):
    return pl.pallas_call(
        column_kernel,
        in_specs=[VMEM] * 3,
        out_specs=VMEM,
        scratch_shapes=[
            pltpu.VMEM((256, 256), F32),
            pltpu.VMEM((128, 256), F32),
            pltpu.VMEM((128, 256), F32),
            pltpu.VMEM((2, 128, 256), BF16),
        ],
        out_shape=jax.ShapeDtypeStruct((768, 128), F32),
        compiler_params=GRANT,
        name="columns",
        **kw,
    )(inbox, numbers, terms)


def run_backward(levels, inbox, w, **kw):
    return pl.pallas_call(
        backward_kernel,
        in_specs=[SMEM] + [VMEM] * 4,
        out_specs=HBM,
        out_shape=jax.ShapeDtypeStruct((BX, ROWS, NY), F32),
        scratch_shapes=[
            pltpu.VMEM((3, 128, 256), F32),
            pltpu.VMEM((4, 512, 256), F32),
            pltpu.VMEM((BX, ROWS, NY), F32),
            pltpu.SemaphoreType.DMA((6,)),
        ],
        compiler_params=GRANT,
        name="backward",
        **kw,
    )(levels, inbox, w, *constants())


def traded(outbox):
    pieces = outbox.reshape(DEVICES, 1, 384)
    pieces = lax.all_to_all(pieces, ("blk", "mode"), split_axis=0, concat_axis=0, tiled=True)
    return pieces.reshape(3 * DEVICES, 128)


def body(divergence, neighbours, levels, sweeps):
    mode = lax.axis_index("mode").astype(jnp.int32)
    device = lax.axis_index("blk").astype(jnp.int32) * BLOCKS + mode
    outbox, w = run_forward(levels, neighbours, sweeps, mode[None], divergence[0])
    numbers, terms, w = run_prepare(device[None], w)
    outbox = run_columns(traded(outbox), numbers, terms)
    return run_backward(levels, traded(outbox), w)[None]


def solution(mesh):
    return jax.shard_map(
        body,
        mesh=mesh,
        in_specs=(P("blk", None, "mode", None), P("blk", None), P("blk"), P()),
        out_specs=P("blk", None, "mode", None),
        check_vma=False,
    )
```

```python
import functools
import math

import jax
import jax.numpy as jnp
import numpy as np
from jax import lax
from jax.experimental import pallas as pl
from jax.experimental.pallas import tpu as pltpu
from jax.sharding import PartitionSpec as P

NY = 1024
BX = 32
NZ = 128
CITERS = 8
DAMPING = 0.8
REACH = 3
BLOCKS = 8
ROWS = NZ // BLOCKS
DEVICES = 256
F32 = jnp.float32
BF16 = jnp.bfloat16


def sine_table(extent):
    ordinal = np.arange(1, extent + 1)
    angles = np.pi * np.outer(ordinal, ordinal) / (extent + 1)
    matrix = np.sqrt(2.0 / (extent + 1)) * np.sin(angles)
    return matrix, 4.0 * np.sin(np.pi * ordinal / (2 * (extent + 1))) ** 2


def two_terms(array):
    high = np.asarray(array, np.float32).astype(BF16)
    low = (np.asarray(array, np.float64) - high.astype(np.float64)).astype(BF16)
    return high, low


def fourier_class(length, cosines, sines):
    y = np.arange(length)
    columns = []
    for waves, function in ((cosines, np.cos), (sines, np.sin)):
        for m in waves:
            weight = (1.0 if m in (0, NY // 2) else 2.0) / NY
            columns.append(math.sqrt(weight) * function(2 * np.pi * ((m * y) % NY) / NY))
    waves = np.concatenate((np.array(cosines), np.array(sines)))
    return np.stack(columns, axis=1), 4.0 * np.sin(np.pi * waves / NY) ** 2


def odd_class(residue):
    y = np.arange(128)
    columns = []
    waves = []
    for function in (0, 1):
        for m in range(residue, NY, 8):
            angle = 2 * np.pi * ((m * y) % NY) / NY
            if function == 0:
                column = np.concatenate((np.cos(angle), -np.sin(angle)))
            else:
                column = np.concatenate((np.sin(angle), np.cos(angle)))
                column = column if m < NY // 2 else -column
            columns.append(math.sqrt(2.0 / NY) * column)
            waves.append(min(m, NY - m))
    return np.stack(columns, axis=1), 4.0 * np.sin(np.pi * np.array(waves) / NY) ** 2


SX, LX = sine_table(BX)
SB, LB = sine_table(ROWS)
SZ, LZ = sine_table(NZ)
IX = np.concatenate((np.arange(0, BX, 2), np.arange(1, BX, 2)))
JB = np.concatenate((np.arange(0, ROWS, 2), np.arange(1, ROWS, 2)))
T0, K0 = fourier_class(256, range(0, 513, 4), range(4, 512, 4))
T2, K2 = fourier_class(256, range(2, 512, 4), range(2, 512, 4))
T1, K1 = odd_class(1)
T5, K5 = odd_class(5)
T = np.stack((T0, T2, T1, T5))
KQ = np.concatenate((K0, K2, K1, K5))
ROOT_HALF = math.sqrt(0.5)


def plane_table(parity):
    ways = SX[IX[16 * parity : 16 * parity + 16], :16]
    return np.einsum("ix,jz->ijxz", ways, SB[JB]).reshape(256, 256)


PLANE = np.stack((plane_table(0), plane_table(1)))
ZBASIS = np.einsum("jmz,kz->jmk", SZ.reshape(NZ, BLOCKS, ROWS), SB[JB]).reshape(NZ, NZ)
ZSUM = SZ.sum(axis=0).reshape(NZ, 1)


def link_tables():
    scale = np.zeros((2, 4, 32, 4, 2, 16))
    lam = np.zeros((2, 4, 32, 4, 2, 16))
    for half in range(2):
        for q in range(4):
            for a in range(32):
                lam[half, q, a] = LX[IX[a]] + LB[JB][None, None, :]
                for b in range(8 * half, 8 * half + 8):
                    scale[half, q, a, q, a // 16, b] = SX[0, IX[a]] * SB[0, JB[b]]
    return scale.reshape(256, 128), lam.reshape(256, 128)


LINK_SCALE, LINK_LAMBDA = link_tables()
KQ_OWN = np.repeat(KQ.reshape(4, DEVICES).T, 32, axis=1).reshape(DEVICES, 1, 128)


def halves(value):
    high = value.astype(BF16)
    return high, (value - high.astype(F32)).astype(BF16)


NN = (((1,), (0,)), ((), ()))
NT = (((1,), (1,)), ((), ()))


def dot3(a, b, dims=NN):
    ah, al = a
    bh, bl = b
    return lax.dot_general(
        jnp.concatenate((ah, al, ah), axis=1),
        jnp.concatenate((bh, bh, bl), axis=dims[0][1][0]),
        dims,
        preferred_element_type=F32,
    )


def inverted(value):
    guess = pl.reciprocal(value, approx=True)
    return guess * (2.0 - value * guess)


def stiffness_scalar(level):
    return lax.shift_left(jnp.int32(1), 2 * level).astype(F32)


def per_mode(values):
    iota = lax.broadcasted_iota(jnp.int32, (8, 256), 0)
    halves_of = []
    for half in range(2):
        column = jnp.zeros((8, 256), F32)
        for b in range(8):
            column = jnp.where(iota == b, np.float32(values[JB[8 * half + b]]), column)
        halves_of.append(column)
    return halves_of


def pieces_of(x, x_buffer, x_sems, step):
    first, second = 4 * step, 28 - 4 * step
    return [
        pltpu.make_async_copy(x.at[pl.ds(at, 4)], x_buffer.at[pl.ds(at, 4)], x_sems.at[n, step])
        for n, at in enumerate((first, second))
    ]


def forward_kernel(
    levels, neighbours, sweeps, mode, x, tables_in, kq,
    out_hbm, w_out, out, x_buffer, p_h, p_l, t_h, t_l, yh, yl, fh, fl, w_buffer, features,
    x_sems, t_sems, w_sems,
):
    planes = [
        pltpu.make_async_copy(tables_in.at[pl.ds(8 + 2 * n, 2)], place, t_sems.at[8 + n])
        for n, place in enumerate((p_h, p_l))
    ]
    classes = [
        [
            pltpu.make_async_copy(tables_in.at[4 * n + q], place.at[q], t_sems.at[2 * q + n])
            for n, place in enumerate((t_h, t_l))
        ]
        for q in range(4)
    ]
    for step in range(4):
        for copy in pieces_of(x, x_buffer, x_sems, step):
            copy.start()
    for copy in classes[0] + planes + classes[1] + classes[2] + classes[3]:
        copy.start()

    def fold(step, k):
        for parity in range(2):
            for k in (k,):
                a, b = x_buffer[4 * step + k], x_buffer[31 - 4 * step - k]
                v = a + b if parity == 0 else a - b
                v0, v1, v2, v3 = (v[:, 256 * n : 256 * n + 256] for n in range(4))
                e0, e1 = v0 + v2, v1 + v3
                f, g = v0 - v2, v1 - v3
                f0, f1 = f[:, :128], f[:, 128:] * ROOT_HALF
                g0, g1 = g[:, :128], g[:, 128:] * ROOT_HALF
                turn0, turn1 = f1 - g1, f1 + g1
                parts = (
                    e0 + e1,
                    e0 - e1,
                    jnp.concatenate((f0 + turn0, g0 + turn1), axis=1),
                    jnp.concatenate((f0 - turn0, g0 - turn1), axis=1),
                )
                at = 256 * parity + 16 * (4 * step + k)
                rows = slice(at, at + 16)
                for q in range(4):
                    high, low = halves(parts[q])
                    yh[q, rows, :] = high
                    yl[q, rows, :] = low

    def transform(unit):
        q, parity = divmod(unit, 2)
        rows = slice(256 * parity, 256 * parity + 256)
        high, low = halves(dot3((yh[q, rows, :], yl[q, rows, :]), (t_h[q], t_l[q])))
        fh[q, rows, :] = high
        fl[q, rows, :] = low

    def in_plane(unit):
        q, parity = divmod(unit, 2)
        rows = slice(256 * parity, 256 * parity + 256)
        w_buffer[unit] = dot3((p_h[parity], p_l[parity]), (fh[q, rows, :], fl[q, rows, :]))

    for step in range(4):
        for copy in pieces_of(x, x_buffer, x_sems, step):
            copy.wait()
        if step == 3:
            for copy in classes[0]:
                copy.wait()
        for k in range(4):
            fold(step, k)
    level = levels[0]
    stiffness = stiffness_scalar(level)
    lambdas = [stiffness * column for column in per_mode(LB)]
    firsts = per_mode(SB[0])
    sublane = lax.broadcasted_iota(jnp.int32, (8, 256), 0)
    low_side = {size: sublane % (2 * size) < size for size in (4, 2, 1)}

    def summed(values):
        for size in (4, 2, 1):
            merged = []
            for n in range(size):
                one, other = values[n], values[n + size]
                kept = jnp.where(low_side[size], one, other)
                moved = jnp.where(low_side[size], other, one)
                if size == 4:
                    moved = pltpu.roll(moved, 4, 0)
                else:
                    moved = jnp.where(
                        low_side[size],
                        pltpu.roll(moved, 8 - size, 0),
                        pltpu.roll(moved, size, 0),
                    )
                merged.append(kept + moved)
            values = merged
        return values[0]

    def divide(unit):
        q, parity = divmod(unit, 2)
        base = [column + kq[:, 256 * q : 256 * q + 256] for column in lambdas]
        place = 32 * q + 16 * parity
        totals = [None, None]
        for group in range(2):
            ends = [[], []]
            for a in range(8 * group, 8 * group + 8):
                shift = stiffness * np.float32(LX[IX[16 * parity + a]])
                face = np.float32(SX[0, IX[16 * parity + a]])
                for half in range(2):
                    row = slice(16 * a + 8 * half, 16 * a + 8 * half + 8)
                    w = w_buffer[unit, row, :] * inverted(base[half] + shift)
                    w_buffer[unit, row, :] = w
                    ends[half].append(w * firsts[half])
                    part = face * w
                    totals[half] = part if a == 0 else totals[half] + part
            at = place + 8 * group
            for half in range(2):
                features[half, at : at + 8, :] = summed(ends[half])
        for half in range(2):
            features[2, place + 8 * half : place + 8 * half + 8, :] = totals[half]

    copies = []
    transform(0)
    for unit in range(8):
        if unit < 7:
            transform(unit + 1)
        if unit == 0:
            for copy in planes + classes[1] + classes[2] + classes[3]:
                copy.wait()
        in_plane(unit)
        divide(unit)
        q, parity = divmod(unit, 2)
        if q >= 2 and parity == 1:
            span = pl.ds(0, 6) if q == 2 else pl.ds(6, 2)
            copy = pltpu.make_async_copy(w_buffer.at[span], w_out.at[span], w_sems.at[q - 2])
            copy.start()
            copies.append(copy)
    last = mode[0] == BLOCKS - 1
    lane = lax.broadcasted_iota(jnp.int32, (8, 128), 1)
    meta = jnp.zeros((8, 128), F32)
    facts = (
        stiffness,
        sweeps[level].astype(F32),
        neighbours[0, 0].astype(F32),
        neighbours[0, 1].astype(F32),
    )
    for n, fact in enumerate(facts):
        meta = jnp.where(lane == n, fact, meta)
    meta = jnp.concatenate([meta] * (DEVICES // 8), axis=0)
    even, odd = features[0].T, features[1].T
    out[pl.ds(0, DEVICES, stride=3), :] = jnp.where(last, even + odd, even)
    out[pl.ds(1, DEVICES, stride=3), :] = jnp.where(last, meta, odd)
    out[pl.ds(2, DEVICES, stride=3), :] = features[2].T
    copy = pltpu.make_async_copy(out, out_hbm, w_sems.at[2])
    copy.start()
    copies.append(copy)
    for copy in copies:
        copy.wait()


def end_responses(shift, extent):
    half = 0.5 * shift
    ratio = 1.0 / (1.0 + half + jnp.sqrt(half * (half + 2.0)))
    square = ratio * ratio
    power = ratio
    for _ in range(extent.bit_length() - 1):
        power = power * power
    rest = power * power
    below = 1.0 / (1.0 - rest * square)
    return ratio * (1.0 - rest) * below, power * (1.0 - square) * below


RATIOS, SCALES, NEAR_FAR, FACE_NEAR, FACE_FAR, Z_SUM = 8, 72, 136, 152, 536, 920


def prepare_kernel(own, w_in, k_own, constants_in, zbasis, numbers, terms, w_out, sem):
    del own
    copy = pltpu.make_async_copy(w_in, w_out, sem)
    copy.start()
    link_scale, link_lambda = constants_in[0:256], constants_in[256:512]
    zsum, lam_z, lam_x = constants_in[512:640], constants_in[640:768], constants_in[768:776]
    k_row = k_own[0]
    numbers[0:8] = jnp.broadcast_to(k_row, (8, 128))
    level = lax.broadcasted_iota(jnp.int32, (8, 128), 0)
    easing = jnp.where(level == 0, 1.0, jnp.where(level == 1, 0.25, 0.0625))
    near, far = end_responses(lam_x + k_row * easing, ROWS)
    numbers[NEAR_FAR : NEAR_FAR + 8] = near
    numbers[NEAR_FAR + 8 : NEAR_FAR + 16] = far
    carry = jnp.zeros((8, 128), F32)
    for m in range(BLOCKS):
        scale = 1.0 / (1.0 - near * carry)
        numbers[RATIOS + 8 * m : RATIOS + 8 * m + 8] = carry
        numbers[SCALES + 8 * m : SCALES + 8 * m + 8] = scale
        carry = near + far * far * carry * scale
    for level in range(3):
        shift = k_row * np.float32(0.25**level)
        face_near, face_far = end_responses(lam_z + shift, BX)
        numbers[FACE_NEAR + 128 * level : FACE_NEAR + 128 * level + 128] = face_near
        numbers[FACE_FAR + 128 * level : FACE_FAR + 128 * level + 128] = face_far
        high, low = halves(link_scale / (link_lambda + shift))
        terms[256 * level : 256 * level + 256] = high
        terms[768 + 256 * level : 768 + 256 * level + 256] = low
    for n in range(4):
        terms[1536 + 128 * n : 1536 + 128 * n + 128] = zbasis[n]
    numbers[Z_SUM : Z_SUM + 128] = zsum
    copy.wait()


def column_kernel(
    inbox, numbers, terms_in, out, x_links, t_faces, turned, passing,
):
    k_row = numbers[0:1]
    links = (terms_in[0:768], terms_in[768:1536])
    zsum = numbers[Z_SUM : Z_SUM + 128]
    zbasis = [terms_in[1536 + 128 * n : 1536 + 128 * n + 128] for n in range(4)]
    meta = inbox[pl.ds(3 * (BLOCKS - 1) + 1, 32, stride=24), :]
    stiff_col = meta[:, 0:1]
    flat = stiff_col < 2.0
    middle = stiff_col < 8.0

    meta_t = meta.T
    facts = jnp.concatenate([meta_t[0:8]] * 4, axis=1)
    stiff, allowed = facts[0:1], facts[1:2]
    west_slot, east_slot = facts[2:3], facts[3:4]
    lane = lax.broadcasted_iota(jnp.int32, (1, 128), 1)
    first_lane = (lane - lane % 32).astype(F32)
    row = lax.broadcasted_iota(jnp.int32, (128, 128), 0).astype(F32)
    west_pick = ((row == first_lane + west_slot) & (west_slot >= 0.0)).astype(F32)
    east_pick = ((row == first_lane + east_slot) & (east_slot >= 0.0)).astype(F32)
    diagonal = stiff * np.float32(2 * NZ + 2 * BX) + np.float32(BX * NZ) * k_row
    coupling = stiff * np.float32(NZ) / diagonal
    column = lax.broadcasted_iota(jnp.int32, (128, 128), 1).astype(F32)
    unit = (row == column).astype(F32)
    step1 = (1.0 - DAMPING) * unit + DAMPING * coupling * (west_pick + east_pick)
    step1_terms = halves(step1)
    step2_terms = halves(dot3(step1_terms, step1_terms))
    step4 = dot3(step2_terms, step2_terms)
    run2 = step1 + unit
    run4 = run2 + dot3(halves(run2), step2_terms)
    run8 = run4 + dot3(halves(run4), halves(step4))
    picks = jnp.concatenate((west_pick, east_pick), axis=1).astype(BF16)
    run_high, run_low = halves(run8)
    sideways = jnp.dot(
        jnp.concatenate((run_high, run_low), axis=1),
        jnp.concatenate((picks, picks), axis=0),
        preferred_element_type=F32,
    )
    passing[0], passing[1] = halves(sideways)
    west_bits = jnp.concatenate([west_pick.astype(BF16)] * 2, axis=0)
    east_bits = jnp.concatenate([east_pick.astype(BF16)] * 2, axis=0)

    def exchange(first, last):
        west = jnp.dot(
            jnp.concatenate(halves(last), axis=1), west_bits, preferred_element_type=F32
        )
        east = jnp.dot(
            jnp.concatenate(halves(first), axis=1), east_bits, preferred_element_type=F32
        )
        return west, east

    def by_level(at):
        values = numbers[at : at + 8]
        return jnp.where(flat, values[0:1], jnp.where(middle, values[1:2], values[2:3]))

    near, far = by_level(NEAR_FAR), by_level(NEAR_FAR + 8)
    held = [(by_level(RATIOS + 8 * m), by_level(SCALES + 8 * m)) for m in range(BLOCKS)]

    def interfaces(even, odd):
        firsts, offsets = [], []
        offset = jnp.zeros((32, 128), F32)
        for m in range(BLOCKS):
            ratio, scale = held[m]
            first, last = even[m] + odd[m], even[m] - odd[m]
            pushed = (first + near * offset) * scale
            offsets.append(offset)
            firsts.append(pushed)
            offset = last + far * (offset + ratio * pushed)
        above = jnp.zeros((32, 128), F32)
        sides = [None] * BLOCKS
        for m in reversed(range(BLOCKS)):
            ratio, scale = held[m]
            head = firsts[m] + far * scale * above
            below = ratio * head + offsets[m]
            sides[m] = (below + above, below - above)
            above = head
        return sides

    def received(kind, m):
        return inbox[pl.ds(3 * m + kind, 32, stride=24), :]

    even = [received(0, m) for m in range(BLOCKS)]
    odd = [received(1, m) for m in range(BLOCKS - 1)] + [jnp.zeros((32, 128), F32)]
    sides = interfaces(even, odd)
    for m in range(BLOCKS):
        x_links[32 * m : 32 * m + 32, 0:128] = sides[m][0]
        x_links[32 * m : 32 * m + 32, 128:256] = sides[m][1]

    stiff_rows = jnp.broadcast_to(jnp.concatenate([stiff_col] * BLOCKS, axis=0), (256, 128))
    hits = [(stiff_rows == np.float32(4.0**level)).astype(BF16) for level in range(3)]

    def spread(value):
        wide = value.shape[1] // 128
        return [
            jnp.concatenate(
                [
                    term[:, 128 * n : 128 * n + 128] * hits[level]
                    for level in range(3)
                    for n in range(wide)
                ],
                axis=1,
            )
            for term in halves(value)
        ]

    faces = jnp.concatenate([received(2, m) for m in range(BLOCKS)], axis=0)
    faces = faces + dot3(spread(x_links[...]), links)

    block = lax.broadcasted_iota(jnp.int32, (16, 128), 1) // 32

    def joined(parts):
        result = parts[0]
        for n in range(1, 4):
            result = jnp.where(block == n, parts[n], result)
        return result

    def turn(value, shift):
        return value if shift % 4 == 0 else pltpu.roll(value, 32 * (shift % 4), 1)

    turned[...] = faces.T
    for m in range(BLOCKS):
        for parity in range(2):
            t_faces[16 * m : 16 * m + 16, 128 * parity : 128 * parity + 128] = joined(
                [
                    turn(
                        turned[
                            32 * q + 16 * parity : 32 * q + 16 * parity + 16,
                            128 * (m // 4) : 128 * (m // 4) + 128,
                        ],
                        q - m,
                    )
                    for q in range(4)
                ]
            )
    modes = dot3((zbasis[0], zbasis[1]), halves(t_faces[...]))
    west_end = modes[:, :128] + modes[:, 128:]
    east_end = modes[:, :128] - modes[:, 128:]

    def by_lane(at):
        values = [numbers[at + 128 * n : at + 128 * n + 128] for n in range(3)]
        return jnp.where(stiff < 2.0, values[0], jnp.where(stiff < 8.0, values[1], values[2]))

    face_near, face_far = by_lane(FACE_NEAR), by_lane(FACE_FAR)
    twice = (allowed > 1.0).astype(F32)
    west1, east1 = exchange(west_end, east_end)
    west1, east1 = west1 * twice, east1 * twice
    first = west_end + face_near * west1 + face_far * east1
    last = east_end + face_far * west1 + face_near * east1
    west2, east2 = exchange(first, last)
    moved = (west2 - west1) + (east2 - east1)
    coarse = stiff * jnp.sum(moved * zsum, axis=0, keepdims=True)
    target = jnp.broadcast_to(DAMPING * coarse / diagonal, (16, 128))
    corrections = dot3(halves(target), (passing[0], passing[1]))
    west3 = west2 + zsum * corrections[0:1, :128]
    east3 = east2 + zsum * corrections[0:1, 128:]
    first = west_end + face_near * west3 + face_far * east3
    last = east_end + face_far * west3 + face_near * east3
    west4, east4 = exchange(first, last)
    again = twice > 0.0
    west = jnp.where(again, west4, west3)
    east = jnp.where(again, east4, east3)
    sums = jnp.concatenate((west + east, west - east), axis=1)
    t_faces[...] = dot3((zbasis[2], zbasis[3]), halves(sums))

    for q in range(4):
        for parity in range(2):
            for h in range(2):
                turned[
                    32 * q + 16 * parity : 32 * q + 16 * parity + 16, 128 * h : 128 * h + 128
                ] = joined(
                    [
                        turn(
                            t_faces[
                                64 * h + 16 * m : 64 * h + 16 * m + 16,
                                128 * parity : 128 * parity + 128,
                            ],
                            m - q,
                        )
                        for m in range(4)
                    ]
                )
    faces = turned[...].T
    for m in range(BLOCKS):
        out[pl.ds(3 * m + 2, 32, stride=24), :] = faces[32 * m : 32 * m + 32]
    levelled = [
        jnp.concatenate([link[256 * n : 256 * n + 256, :] for n in range(3)], axis=1)
        for link in links
    ]
    driven = dot3(spread(faces), levelled, NT)
    sides = interfaces(
        [even[m] + driven[32 * m : 32 * m + 32, 0:128] for m in range(BLOCKS)],
        [odd[m] + driven[32 * m : 32 * m + 32, 128:256] for m in range(BLOCKS)],
    )
    for m in range(BLOCKS):
        for kind in range(2):
            out[pl.ds(3 * m + kind, 32, stride=24), :] = sides[m][kind]


def backward_kernel(
    levels, inbox, w_in, tables, kq, out, features, sums, rows_out, sems,
):
    easing = 1.0 / stiffness_scalar(levels[0])
    for kind in range(3):
        features[kind] = inbox[pl.ds(kind, DEVICES, stride=3), :].T
    firsts, lambdas = per_mode(SB[0]), per_mode(LB)
    for q in range(4):
        base = [column + kq[:, 256 * q : 256 * q + 256] * easing for column in lambdas]
        for parity in range(2):
            place = 32 * q + 16 * parity
            side = features[2, place : place + 16, :]
            terms = []
            for a in range(16):
                shift = np.float32(LX[IX[16 * parity + a]])
                face = np.float32(SX[0, IX[16 * parity + a]])
                pair = []
                for half in range(2):
                    row = 16 * a + 8 * half
                    end = features[half, place + a : place + a + 1, :]
                    drive = firsts[half] * end + face * side[8 * half : 8 * half + 8]
                    w = w_in[2 * q + parity, row : row + 8, :]
                    pair.append(w + drive * inverted(base[half] + shift))
                terms.append(halves(jnp.concatenate(pair, axis=0)))
            u = [jnp.concatenate([t[h] for t in terms], axis=0) for h in range(2)]
            sums[q, 256 * parity : 256 * parity + 256, :] = dot3(u, (tables[q], tables[4 + q]), NT)
    copies = []
    for n in range(4):
        cut = slice(256 * n, 256 * n + 256)
        sides = []
        for parity in range(2):
            terms = []
            for k in range(16):
                rows = slice(256 * parity + 16 * k, 256 * parity + 16 * k + 16)
                p0, p2, p1, p5 = (sums[q, rows, :] for q in range(4))
                e = p0 + p2 if n % 2 == 0 else p0 - p2
                half = slice(128 * (n % 2), 128 * (n % 2) + 128)
                turn = (p1 - p5) * ROOT_HALF
                mixed = turn[:, :128] + turn[:, 128:] if n % 2 == 0 else turn[:, 128:] - turn[:, :128]
                f = jnp.concatenate((p1[:, half] + p5[:, half], mixed), axis=1)
                terms.append(halves(e + f if n < 2 else e - f))
            v = [jnp.concatenate([t[h] for t in terms], axis=0) for h in range(2)]
            sides.append(dot3((tables[12 + parity], tables[14 + parity]), v))
        spans = {15: [(0, 32, n)]} if n < 3 else {7: [(0, 8, 3), (24, 8, 4)], 15: [(8, 16, 5)]}
        for k in range(16):
            rows = slice(16 * k, 16 * k + 16)
            rows_out[k, :, cut] = sides[0][rows] + sides[1][rows]
            rows_out[31 - k, :, cut] = sides[0][rows] - sides[1][rows]
            for at, size, sem in spans.get(k, ()):
                place = (pl.ds(at, size), slice(None), pl.ds(256 * n, 256))
                copy = pltpu.make_async_copy(rows_out.at[place], out.at[place], sems.at[sem])
                copy.start()
                copies.append(copy)
    for copy in copies:
        copy.wait()


def whole(shape):
    return pl.BlockSpec(shape, lambda *_: (0,) * len(shape))


SMEM = pl.BlockSpec(memory_space=pltpu.SMEM)
VMEM = pl.BlockSpec(memory_space=pltpu.VMEM)


HBM = pl.BlockSpec(memory_space=pltpu.HBM)
GRANT = pltpu.CompilerParams(vmem_limit_bytes=20 * 2**20)


def constants():
    tables = []
    for table in (T, PLANE, np.swapaxes(PLANE, 1, 2)):
        tables.extend(two_terms(table))
    return jnp.asarray(np.concatenate(tables)), jnp.asarray(KQ[None, :], F32)


def run_forward(levels, neighbours, sweeps, mode, x, **kw):
    return pl.pallas_call(
        forward_kernel,
        in_specs=[SMEM] * 4 + [HBM] * 2 + [VMEM],
        out_specs=[HBM, HBM],
        out_shape=[
            jax.ShapeDtypeStruct((768, 128), F32),
            jax.ShapeDtypeStruct((8, 256, 256), F32),
        ],
        scratch_shapes=[
            pltpu.VMEM((768, 128), F32),
            pltpu.VMEM((BX, ROWS, NY), F32),
            pltpu.VMEM((2, 256, 256), BF16),
            pltpu.VMEM((2, 256, 256), BF16),
            pltpu.VMEM((4, 256, 256), BF16),
            pltpu.VMEM((4, 256, 256), BF16),
            pltpu.VMEM((4, 512, 256), BF16),
            pltpu.VMEM((4, 512, 256), BF16),
            pltpu.VMEM((4, 512, 256), BF16),
            pltpu.VMEM((4, 512, 256), BF16),
            pltpu.VMEM((8, 256, 256), F32),
            pltpu.VMEM((3, 128, 256), F32),
            pltpu.SemaphoreType.DMA((2, 4)),
            pltpu.SemaphoreType.DMA((10,)),
            pltpu.SemaphoreType.DMA((3,)),
        ],
        name="forward",
        **kw,
    )(levels, neighbours, sweeps, mode, x, *constants())


def run_prepare(device, w, **kw):
    zbasis = np.stack([t for table in (ZBASIS, ZBASIS.T) for t in two_terms(table)])
    wide = np.ones((1, 128))
    numbers = np.concatenate(
        (
            LINK_SCALE, LINK_LAMBDA, ZSUM * wide, LZ[:, None] * wide,
            np.tile(LX[IX], 4)[None, :] * np.ones((8, 1)),
        )
    )
    shapes = [((Z_SUM + 128, 128), F32), ((2048, 128), BF16), (w.shape, F32)]
    return pl.pallas_call(
        prepare_kernel,
        grid_spec=pltpu.PrefetchScalarGridSpec(
            num_scalar_prefetch=1,
            grid=(1,),
            in_specs=[
                HBM,
                pl.BlockSpec((1, 1, 128), lambda i, own: (own[0], 0, 0)),
                whole(numbers.shape),
                whole(zbasis.shape),
            ],
            out_specs=[VMEM] * len(shapes),
            scratch_shapes=[pltpu.SemaphoreType.DMA],
        ),
        out_shape=[jax.ShapeDtypeStruct(*shape) for shape in shapes],
        compiler_params=GRANT,
        name="prepare",
        **kw,
    )(device, w, jnp.asarray(KQ_OWN, F32), jnp.asarray(numbers, F32), jnp.asarray(zbasis))


def run_columns(inbox, numbers, terms, **kw):
    return pl.pallas_call(
        column_kernel,
        in_specs=[VMEM] * 3,
        out_specs=VMEM,
        scratch_shapes=[
            pltpu.VMEM((256, 256), F32),
            pltpu.VMEM((128, 256), F32),
            pltpu.VMEM((128, 256), F32),
            pltpu.VMEM((2, 128, 256), BF16),
        ],
        out_shape=jax.ShapeDtypeStruct((768, 128), F32),
        compiler_params=GRANT,
        name="columns",
        **kw,
    )(inbox, numbers, terms)


def run_backward(levels, inbox, w, **kw):
    return pl.pallas_call(
        backward_kernel,
        in_specs=[SMEM] + [VMEM] * 4,
        out_specs=HBM,
        out_shape=jax.ShapeDtypeStruct((BX, ROWS, NY), F32),
        scratch_shapes=[
            pltpu.VMEM((3, 128, 256), F32),
            pltpu.VMEM((4, 512, 256), F32),
            pltpu.VMEM((BX, ROWS, NY), F32),
            pltpu.SemaphoreType.DMA((6,)),
        ],
        compiler_params=GRANT,
        name="backward",
        **kw,
    )(levels, inbox, w, *constants())


def traded(outbox):
    pieces = outbox.reshape(DEVICES, 1, 384)
    pieces = lax.all_to_all(pieces, ("blk", "mode"), split_axis=0, concat_axis=0, tiled=True)
    return pieces.reshape(3 * DEVICES, 128)


def body(divergence, neighbours, levels, sweeps):
    mode = lax.axis_index("mode").astype(jnp.int32)
    device = lax.axis_index("blk").astype(jnp.int32) * BLOCKS + mode
    outbox, w = run_forward(levels, neighbours, sweeps, mode[None], divergence[0])
    numbers, terms, w = run_prepare(device[None], w)
    outbox = run_columns(traded(outbox), numbers, terms)
    return run_backward(levels, traded(outbox), w)[None]


def solution(mesh):
    return jax.shard_map(
        body,
        mesh=mesh,
        in_specs=(P("blk", None, "mode", None), P("blk", None), P("blk"), P()),
        out_specs=P("blk", None, "mode", None),
        check_vma=False,
    )
```

```python
import functools
import math

import jax
import jax.numpy as jnp
import numpy as np
from jax import lax
from jax.experimental import pallas as pl
from jax.experimental.pallas import tpu as pltpu
from jax.sharding import PartitionSpec as P

NY = 1024
BX = 32
NZ = 128
CITERS = 8
DAMPING = 0.8
REACH = 3
BLOCKS = 8
ROWS = NZ // BLOCKS
DEVICES = 256
F32 = jnp.float32
BF16 = jnp.bfloat16


def sine_table(extent):
    ordinal = np.arange(1, extent + 1)
    angles = np.pi * np.outer(ordinal, ordinal) / (extent + 1)
    matrix = np.sqrt(2.0 / (extent + 1)) * np.sin(angles)
    return matrix, 4.0 * np.sin(np.pi * ordinal / (2 * (extent + 1))) ** 2


def two_terms(array):
    high = np.asarray(array, np.float32).astype(BF16)
    low = (np.asarray(array, np.float64) - high.astype(np.float64)).astype(BF16)
    return high, low


def fourier_class(length, cosines, sines):
    y = np.arange(length)
    columns = []
    for waves, function in ((cosines, np.cos), (sines, np.sin)):
        for m in waves:
            weight = (1.0 if m in (0, NY // 2) else 2.0) / NY
            columns.append(math.sqrt(weight) * function(2 * np.pi * ((m * y) % NY) / NY))
    waves = np.concatenate((np.array(cosines), np.array(sines)))
    return np.stack(columns, axis=1), 4.0 * np.sin(np.pi * waves / NY) ** 2


def odd_class(residue):
    y = np.arange(128)
    columns = []
    waves = []
    for function in (0, 1):
        for m in range(residue, NY, 8):
            angle = 2 * np.pi * ((m * y) % NY) / NY
            if function == 0:
                column = np.concatenate((np.cos(angle), -np.sin(angle)))
            else:
                column = np.concatenate((np.sin(angle), np.cos(angle)))
                column = column if m < NY // 2 else -column
            columns.append(math.sqrt(2.0 / NY) * column)
            waves.append(min(m, NY - m))
    return np.stack(columns, axis=1), 4.0 * np.sin(np.pi * np.array(waves) / NY) ** 2


SX, LX = sine_table(BX)
SB, LB = sine_table(ROWS)
SZ, LZ = sine_table(NZ)
IX = np.concatenate((np.arange(0, BX, 2), np.arange(1, BX, 2)))
JB = np.concatenate((np.arange(0, ROWS, 2), np.arange(1, ROWS, 2)))
T0, K0 = fourier_class(256, range(0, 513, 4), range(4, 512, 4))
T2, K2 = fourier_class(256, range(2, 512, 4), range(2, 512, 4))
T1, K1 = odd_class(1)
T5, K5 = odd_class(5)
T = np.stack((T0, T2, T1, T5))
KQ = np.concatenate((K0, K2, K1, K5))
ROOT_HALF = math.sqrt(0.5)


def plane_table(parity):
    ways = SX[IX[16 * parity : 16 * parity + 16], :16]
    return np.einsum("ix,jz->ijxz", ways, SB[JB]).reshape(256, 256)


PLANE = np.stack((plane_table(0), plane_table(1)))
ZBASIS = np.einsum("jmz,kz->jmk", SZ.reshape(NZ, BLOCKS, ROWS), SB[JB]).reshape(NZ, NZ)
ZSUM = SZ.sum(axis=0).reshape(NZ, 1)


def link_tables():
    scale = np.zeros((2, 4, 32, 4, 2, 16))
    lam = np.zeros((2, 4, 32, 4, 2, 16))
    for half in range(2):
        for q in range(4):
            for a in range(32):
                lam[half, q, a] = LX[IX[a]] + LB[JB][None, None, :]
                for b in range(8 * half, 8 * half + 8):
                    scale[half, q, a, q, a // 16, b] = SX[0, IX[a]] * SB[0, JB[b]]
    return scale.reshape(256, 128), lam.reshape(256, 128)


LINK_SCALE, LINK_LAMBDA = link_tables()
KQ_OWN = np.repeat(KQ.reshape(4, DEVICES).T, 32, axis=1).reshape(DEVICES, 1, 128)


def halves(value):
    high = value.astype(BF16)
    return high, (value - high.astype(F32)).astype(BF16)


NN = (((1,), (0,)), ((), ()))
NT = (((1,), (1,)), ((), ()))


def dot3(a, b, dims=NN):
    ah, al = a
    bh, bl = b
    return lax.dot_general(
        jnp.concatenate((ah, al, ah), axis=1),
        jnp.concatenate((bh, bh, bl), axis=dims[0][1][0]),
        dims,
        preferred_element_type=F32,
    )


def inverted(value):
    guess = pl.reciprocal(value, approx=True)
    return guess * (2.0 - value * guess)


def stiffness_scalar(level):
    return lax.shift_left(jnp.int32(1), 2 * level).astype(F32)


def per_mode(values):
    iota = lax.broadcasted_iota(jnp.int32, (8, 256), 0)
    halves_of = []
    for half in range(2):
        column = jnp.zeros((8, 256), F32)
        for b in range(8):
            column = jnp.where(iota == b, np.float32(values[JB[8 * half + b]]), column)
        halves_of.append(column)
    return halves_of


def pieces_of(x, x_buffer, x_sems, step):
    first, second = 2 * step, 30 - 2 * step
    return [
        pltpu.make_async_copy(x.at[pl.ds(at, 2)], x_buffer.at[pl.ds(at, 2)], x_sems.at[n, step])
        for n, at in enumerate((first, second))
    ]


def forward_kernel(
    levels, neighbours, sweeps, mode, x, tables_in, kq,
    out_hbm, w_out, out, x_buffer, p_h, p_l, t_h, t_l, yh, yl, fh, fl, w_buffer, features,
    x_sems, t_sems, w_sems,
):
    tables = [
        pltpu.make_async_copy(source, place, t_sems.at[n])
        for n, (source, place) in enumerate(
            (
                (tables_in.at[pl.ds(0, 4)], t_h), (tables_in.at[pl.ds(4, 4)], t_l),
                (tables_in.at[pl.ds(8, 2)], p_h), (tables_in.at[pl.ds(10, 2)], p_l),
            )
        )
    ]
    for step in range(8):
        for copy in pieces_of(x, x_buffer, x_sems, step):
            copy.start()
    for copy in tables:
        copy.start()

    def fold(step, k):
        for parity in range(2):
            for k in (k,):
                a, b = x_buffer[2 * step + k], x_buffer[31 - 2 * step - k]
                v = a + b if parity == 0 else a - b
                v0, v1, v2, v3 = (v[:, 256 * n : 256 * n + 256] for n in range(4))
                e0, e1 = v0 + v2, v1 + v3
                f, g = v0 - v2, v1 - v3
                f0, f1 = f[:, :128], f[:, 128:] * ROOT_HALF
                g0, g1 = g[:, :128], g[:, 128:] * ROOT_HALF
                turn0, turn1 = f1 - g1, f1 + g1
                parts = (
                    e0 + e1,
                    e0 - e1,
                    jnp.concatenate((f0 + turn0, g0 + turn1), axis=1),
                    jnp.concatenate((f0 - turn0, g0 - turn1), axis=1),
                )
                at = 256 * parity + 16 * (2 * step + k)
                rows = slice(at, at + 16)
                for q in range(4):
                    high, low = halves(parts[q])
                    yh[q, rows, :] = high
                    yl[q, rows, :] = low

    def transform(unit):
        q, parity = divmod(unit, 2)
        rows = slice(256 * parity, 256 * parity + 256)
        high, low = halves(dot3((yh[q, rows, :], yl[q, rows, :]), (t_h[q], t_l[q])))
        fh[q, rows, :] = high
        fl[q, rows, :] = low

    def in_plane(unit):
        q, parity = divmod(unit, 2)
        rows = slice(256 * parity, 256 * parity + 256)
        w_buffer[unit] = dot3((p_h[parity], p_l[parity]), (fh[q, rows, :], fl[q, rows, :]))

    for step in range(8):
        for copy in pieces_of(x, x_buffer, x_sems, step):
            copy.wait()
        if step == 7:
            for copy in tables:
                copy.wait()
        for k in range(2):
            fold(step, k)
    level = levels[0]
    stiffness = stiffness_scalar(level)
    lambdas = [stiffness * column for column in per_mode(LB)]
    firsts = per_mode(SB[0])
    sublane = lax.broadcasted_iota(jnp.int32, (8, 256), 0)
    low_side = {size: sublane % (2 * size) < size for size in (4, 2, 1)}

    def summed(values):
        for size in (4, 2, 1):
            merged = []
            for n in range(size):
                one, other = values[n], values[n + size]
                kept = jnp.where(low_side[size], one, other)
                moved = jnp.where(low_side[size], other, one)
                if size == 4:
                    moved = pltpu.roll(moved, 4, 0)
                else:
                    moved = jnp.where(
                        low_side[size],
                        pltpu.roll(moved, 8 - size, 0),
                        pltpu.roll(moved, size, 0),
                    )
                merged.append(kept + moved)
            values = merged
        return values[0]

    def divide(unit):
        q, parity = divmod(unit, 2)
        base = [column + kq[:, 256 * q : 256 * q + 256] for column in lambdas]
        place = 32 * q + 16 * parity
        totals = [None, None]
        for group in range(2):
            ends = [[], []]
            for a in range(8 * group, 8 * group + 8):
                shift = stiffness * np.float32(LX[IX[16 * parity + a]])
                face = np.float32(SX[0, IX[16 * parity + a]])
                for half in range(2):
                    row = slice(16 * a + 8 * half, 16 * a + 8 * half + 8)
                    w = w_buffer[unit, row, :] * inverted(base[half] + shift)
                    w_buffer[unit, row, :] = w
                    ends[half].append(w * firsts[half])
                    part = face * w
                    totals[half] = part if a == 0 else totals[half] + part
            at = place + 8 * group
            for half in range(2):
                features[half, at : at + 8, :] = summed(ends[half])
        for half in range(2):
            features[2, place + 8 * half : place + 8 * half + 8, :] = totals[half]

    copies = []
    transform(0)
    for unit in range(8):
        if unit < 7:
            transform(unit + 1)
        in_plane(unit)
        divide(unit)
        q, parity = divmod(unit, 2)
        if q >= 2 and parity == 1:
            span = pl.ds(0, 6) if q == 2 else pl.ds(6, 2)
            copy = pltpu.make_async_copy(w_buffer.at[span], w_out.at[span], w_sems.at[q - 2])
            copy.start()
            copies.append(copy)
    last = mode[0] == BLOCKS - 1
    lane = lax.broadcasted_iota(jnp.int32, (8, 128), 1)
    meta = jnp.zeros((8, 128), F32)
    facts = (
        stiffness,
        sweeps[level].astype(F32),
        neighbours[0, 0].astype(F32),
        neighbours[0, 1].astype(F32),
    )
    for n, fact in enumerate(facts):
        meta = jnp.where(lane == n, fact, meta)
    meta = jnp.concatenate([meta] * (DEVICES // 8), axis=0)
    for part in range(2):
        cut = slice(128 * part, 128 * part + 128)
        even, odd, sides = (features[kind, :, cut].T for kind in range(3))
        first = 384 * part
        out[pl.ds(first, 128, stride=3), :] = jnp.where(last, even + odd, even)
        out[pl.ds(first + 1, 128, stride=3), :] = jnp.where(last, meta[cut], odd)
        out[pl.ds(first + 2, 128, stride=3), :] = sides
        span = pl.ds(first, 384)
        copy = pltpu.make_async_copy(out.at[span], out_hbm.at[span], w_sems.at[2 + part])
        copy.start()
        copies.append(copy)
    for copy in copies:
        copy.wait()


def end_responses(shift, extent):
    half = 0.5 * shift
    ratio = 1.0 / (1.0 + half + jnp.sqrt(half * (half + 2.0)))
    square = ratio * ratio
    power = ratio
    for _ in range(extent.bit_length() - 1):
        power = power * power
    rest = power * power
    below = 1.0 / (1.0 - rest * square)
    return ratio * (1.0 - rest) * below, power * (1.0 - square) * below


RATIOS, SCALES, NEAR_FAR, FACE_NEAR, FACE_FAR, Z_SUM = 8, 72, 136, 152, 536, 920


def prepare_kernel(own, w_in, k_own, constants_in, zbasis, numbers, terms, w_out, sem):
    del own
    copy = pltpu.make_async_copy(w_in, w_out, sem)
    copy.start()
    link_scale, link_lambda = constants_in[0:256], constants_in[256:512]
    zsum, lam_z, lam_x = constants_in[512:640], constants_in[640:768], constants_in[768:776]
    k_row = k_own[0]
    numbers[0:8] = jnp.broadcast_to(k_row, (8, 128))
    level = lax.broadcasted_iota(jnp.int32, (8, 128), 0)
    easing = jnp.where(level == 0, 1.0, jnp.where(level == 1, 0.25, 0.0625))
    near, far = end_responses(lam_x + k_row * easing, ROWS)
    numbers[NEAR_FAR : NEAR_FAR + 8] = near
    numbers[NEAR_FAR + 8 : NEAR_FAR + 16] = far
    carry = jnp.zeros((8, 128), F32)
    for m in range(BLOCKS):
        scale = 1.0 / (1.0 - near * carry)
        numbers[RATIOS + 8 * m : RATIOS + 8 * m + 8] = carry
        numbers[SCALES + 8 * m : SCALES + 8 * m + 8] = scale
        carry = near + far * far * carry * scale
    for level in range(3):
        shift = k_row * np.float32(0.25**level)
        face_near, face_far = end_responses(lam_z + shift, BX)
        numbers[FACE_NEAR + 128 * level : FACE_NEAR + 128 * level + 128] = face_near
        numbers[FACE_FAR + 128 * level : FACE_FAR + 128 * level + 128] = face_far
        high, low = halves(link_scale / (link_lambda + shift))
        terms[256 * level : 256 * level + 256] = high
        terms[768 + 256 * level : 768 + 256 * level + 256] = low
    for n in range(4):
        terms[1536 + 128 * n : 1536 + 128 * n + 128] = zbasis[n]
    numbers[Z_SUM : Z_SUM + 128] = zsum
    copy.wait()


def column_kernel(
    inbox, numbers, terms_in, out, x_links, t_faces, turned, passing,
):
    k_row = numbers[0:1]
    links = (terms_in[0:768], terms_in[768:1536])
    zsum = numbers[Z_SUM : Z_SUM + 128]
    zbasis = [terms_in[1536 + 128 * n : 1536 + 128 * n + 128] for n in range(4)]
    meta = inbox[pl.ds(3 * (BLOCKS - 1) + 1, 32, stride=24), :]
    stiff_col = meta[:, 0:1]
    flat = stiff_col < 2.0
    middle = stiff_col < 8.0

    meta_t = meta.T
    facts = jnp.concatenate([meta_t[0:8]] * 4, axis=1)
    stiff, allowed = facts[0:1], facts[1:2]
    west_slot, east_slot = facts[2:3], facts[3:4]
    lane = lax.broadcasted_iota(jnp.int32, (1, 128), 1)
    first_lane = (lane - lane % 32).astype(F32)
    row = lax.broadcasted_iota(jnp.int32, (128, 128), 0).astype(F32)
    west_pick = ((row == first_lane + west_slot) & (west_slot >= 0.0)).astype(F32)
    east_pick = ((row == first_lane + east_slot) & (east_slot >= 0.0)).astype(F32)
    diagonal = stiff * np.float32(2 * NZ + 2 * BX) + np.float32(BX * NZ) * k_row
    coupling = stiff * np.float32(NZ) / diagonal
    column = lax.broadcasted_iota(jnp.int32, (128, 128), 1).astype(F32)
    unit = (row == column).astype(F32)
    step1 = (1.0 - DAMPING) * unit + DAMPING * coupling * (west_pick + east_pick)
    step1_terms = halves(step1)
    step2_terms = halves(dot3(step1_terms, step1_terms))
    step4 = dot3(step2_terms, step2_terms)
    run2 = step1 + unit
    run4 = run2 + dot3(halves(run2), step2_terms)
    run8 = run4 + dot3(halves(run4), halves(step4))
    picks = jnp.concatenate((west_pick, east_pick), axis=1).astype(BF16)
    run_high, run_low = halves(run8)
    sideways = jnp.dot(
        jnp.concatenate((run_high, run_low), axis=1),
        jnp.concatenate((picks, picks), axis=0),
        preferred_element_type=F32,
    )
    passing[0], passing[1] = halves(sideways)
    west_bits = jnp.concatenate([west_pick.astype(BF16)] * 2, axis=0)
    east_bits = jnp.concatenate([east_pick.astype(BF16)] * 2, axis=0)

    def exchange(first, last):
        west = jnp.dot(
            jnp.concatenate(halves(last), axis=1), west_bits, preferred_element_type=F32
        )
        east = jnp.dot(
            jnp.concatenate(halves(first), axis=1), east_bits, preferred_element_type=F32
        )
        return west, east

    def by_level(at):
        values = numbers[at : at + 8]
        return jnp.where(flat, values[0:1], jnp.where(middle, values[1:2], values[2:3]))

    near, far = by_level(NEAR_FAR), by_level(NEAR_FAR + 8)
    held = [(by_level(RATIOS + 8 * m), by_level(SCALES + 8 * m)) for m in range(BLOCKS)]

    def interfaces(even, odd):
        firsts, offsets = [], []
        offset = jnp.zeros((32, 128), F32)
        for m in range(BLOCKS):
            ratio, scale = held[m]
            first, last = even[m] + odd[m], even[m] - odd[m]
            pushed = (first + near * offset) * scale
            offsets.append(offset)
            firsts.append(pushed)
            offset = last + far * (offset + ratio * pushed)
        above = jnp.zeros((32, 128), F32)
        sides = [None] * BLOCKS
        for m in reversed(range(BLOCKS)):
            ratio, scale = held[m]
            head = firsts[m] + far * scale * above
            below = ratio * head + offsets[m]
            sides[m] = (below + above, below - above)
            above = head
        return sides

    def received(kind, m):
        return inbox[pl.ds(3 * m + kind, 32, stride=24), :]

    even = [received(0, m) for m in range(BLOCKS)]
    odd = [received(1, m) for m in range(BLOCKS - 1)] + [jnp.zeros((32, 128), F32)]
    sides = interfaces(even, odd)
    for m in range(BLOCKS):
        x_links[32 * m : 32 * m + 32, 0:128] = sides[m][0]
        x_links[32 * m : 32 * m + 32, 128:256] = sides[m][1]

    stiff_rows = jnp.broadcast_to(jnp.concatenate([stiff_col] * BLOCKS, axis=0), (256, 128))
    hits = [(stiff_rows == np.float32(4.0**level)).astype(BF16) for level in range(3)]

    def spread(value):
        wide = value.shape[1] // 128
        return [
            jnp.concatenate(
                [
                    term[:, 128 * n : 128 * n + 128] * hits[level]
                    for level in range(3)
                    for n in range(wide)
                ],
                axis=1,
            )
            for term in halves(value)
        ]

    faces = jnp.concatenate([received(2, m) for m in range(BLOCKS)], axis=0)
    faces = faces + dot3(spread(x_links[...]), links)

    block = lax.broadcasted_iota(jnp.int32, (16, 128), 1) // 32

    def joined(parts):
        result = parts[0]
        for n in range(1, 4):
            result = jnp.where(block == n, parts[n], result)
        return result

    def turn(value, shift):
        return value if shift % 4 == 0 else pltpu.roll(value, 32 * (shift % 4), 1)

    turned[...] = faces.T
    for m in range(BLOCKS):
        for parity in range(2):
            t_faces[16 * m : 16 * m + 16, 128 * parity : 128 * parity + 128] = joined(
                [
                    turn(
                        turned[
                            32 * q + 16 * parity : 32 * q + 16 * parity + 16,
                            128 * (m // 4) : 128 * (m // 4) + 128,
                        ],
                        q - m,
                    )
                    for q in range(4)
                ]
            )
    modes = dot3((zbasis[0], zbasis[1]), halves(t_faces[...]))
    west_end = modes[:, :128] + modes[:, 128:]
    east_end = modes[:, :128] - modes[:, 128:]

    def by_lane(at):
        values = [numbers[at + 128 * n : at + 128 * n + 128] for n in range(3)]
        return jnp.where(stiff < 2.0, values[0], jnp.where(stiff < 8.0, values[1], values[2]))

    face_near, face_far = by_lane(FACE_NEAR), by_lane(FACE_FAR)
    twice = (allowed > 1.0).astype(F32)
    west1, east1 = exchange(west_end, east_end)
    west1, east1 = west1 * twice, east1 * twice
    first = west_end + face_near * west1 + face_far * east1
    last = east_end + face_far * west1 + face_near * east1
    west2, east2 = exchange(first, last)
    moved = (west2 - west1) + (east2 - east1)
    coarse = stiff * jnp.sum(moved * zsum, axis=0, keepdims=True)
    target = jnp.broadcast_to(DAMPING * coarse / diagonal, (16, 128))
    corrections = dot3(halves(target), (passing[0], passing[1]))
    west3 = west2 + zsum * corrections[0:1, :128]
    east3 = east2 + zsum * corrections[0:1, 128:]
    first = west_end + face_near * west3 + face_far * east3
    last = east_end + face_far * west3 + face_near * east3
    west4, east4 = exchange(first, last)
    again = twice > 0.0
    west = jnp.where(again, west4, west3)
    east = jnp.where(again, east4, east3)
    sums = jnp.concatenate((west + east, west - east), axis=1)
    t_faces[...] = dot3((zbasis[2], zbasis[3]), halves(sums))

    for q in range(4):
        for parity in range(2):
            for h in range(2):
                turned[
                    32 * q + 16 * parity : 32 * q + 16 * parity + 16, 128 * h : 128 * h + 128
                ] = joined(
                    [
                        turn(
                            t_faces[
                                64 * h + 16 * m : 64 * h + 16 * m + 16,
                                128 * parity : 128 * parity + 128,
                            ],
                            m - q,
                        )
                        for m in range(4)
                    ]
                )
    faces = turned[...].T
    for m in range(BLOCKS):
        out[pl.ds(3 * m + 2, 32, stride=24), :] = faces[32 * m : 32 * m + 32]
    levelled = [
        jnp.concatenate([link[256 * n : 256 * n + 256, :] for n in range(3)], axis=1)
        for link in links
    ]
    driven = dot3(spread(faces), levelled, NT)
    sides = interfaces(
        [even[m] + driven[32 * m : 32 * m + 32, 0:128] for m in range(BLOCKS)],
        [odd[m] + driven[32 * m : 32 * m + 32, 128:256] for m in range(BLOCKS)],
    )
    for m in range(BLOCKS):
        for kind in range(2):
            out[pl.ds(3 * m + kind, 32, stride=24), :] = sides[m][kind]


def backward_kernel(
    levels, inbox, w_in, tables, kq, out, features, sums, rows_out, sems,
):
    easing = 1.0 / stiffness_scalar(levels[0])
    for kind in range(3):
        features[kind] = inbox[pl.ds(kind, DEVICES, stride=3), :].T
    firsts, lambdas = per_mode(SB[0]), per_mode(LB)
    for q in range(4):
        base = [column + kq[:, 256 * q : 256 * q + 256] * easing for column in lambdas]
        for parity in range(2):
            place = 32 * q + 16 * parity
            side = features[2, place : place + 16, :]
            terms = []
            for a in range(16):
                shift = np.float32(LX[IX[16 * parity + a]])
                face = np.float32(SX[0, IX[16 * parity + a]])
                pair = []
                for half in range(2):
                    row = 16 * a + 8 * half
                    end = features[half, place + a : place + a + 1, :]
                    drive = firsts[half] * end + face * side[8 * half : 8 * half + 8]
                    w = w_in[2 * q + parity, row : row + 8, :]
                    pair.append(w + drive * inverted(base[half] + shift))
                terms.append(halves(jnp.concatenate(pair, axis=0)))
            u = [jnp.concatenate([t[h] for t in terms], axis=0) for h in range(2)]
            sums[q, 256 * parity : 256 * parity + 256, :] = dot3(u, (tables[q], tables[4 + q]), NT)
    copies = []
    for n in range(4):
        cut = slice(256 * n, 256 * n + 256)
        sides = []
        for parity in range(2):
            terms = []
            for k in range(16):
                rows = slice(256 * parity + 16 * k, 256 * parity + 16 * k + 16)
                p0, p2, p1, p5 = (sums[q, rows, :] for q in range(4))
                e = p0 + p2 if n % 2 == 0 else p0 - p2
                half = slice(128 * (n % 2), 128 * (n % 2) + 128)
                turn = (p1 - p5) * ROOT_HALF
                mixed = turn[:, :128] + turn[:, 128:] if n % 2 == 0 else turn[:, 128:] - turn[:, :128]
                f = jnp.concatenate((p1[:, half] + p5[:, half], mixed), axis=1)
                terms.append(halves(e + f if n < 2 else e - f))
            v = [jnp.concatenate([t[h] for t in terms], axis=0) for h in range(2)]
            sides.append(dot3((tables[12 + parity], tables[14 + parity]), v))
        spans = {15: [(0, 32, n)]} if n < 3 else {7: [(0, 8, 3), (24, 8, 4)], 15: [(8, 16, 5)]}
        for k in range(16):
            rows = slice(16 * k, 16 * k + 16)
            rows_out[k, :, cut] = sides[0][rows] + sides[1][rows]
            rows_out[31 - k, :, cut] = sides[0][rows] - sides[1][rows]
            for at, size, sem in spans.get(k, ()):
                place = (pl.ds(at, size), slice(None), pl.ds(256 * n, 256))
                copy = pltpu.make_async_copy(rows_out.at[place], out.at[place], sems.at[sem])
                copy.start()
                copies.append(copy)
    for copy in copies:
        copy.wait()


def whole(shape):
    return pl.BlockSpec(shape, lambda *_: (0,) * len(shape))


SMEM = pl.BlockSpec(memory_space=pltpu.SMEM)
VMEM = pl.BlockSpec(memory_space=pltpu.VMEM)


HBM = pl.BlockSpec(memory_space=pltpu.HBM)
GRANT = pltpu.CompilerParams(vmem_limit_bytes=20 * 2**20)


def constants():
    tables = []
    for table in (T, PLANE, np.swapaxes(PLANE, 1, 2)):
        tables.extend(two_terms(table))
    return jnp.asarray(np.concatenate(tables)), jnp.asarray(KQ[None, :], F32)


def run_forward(levels, neighbours, sweeps, mode, x, **kw):
    return pl.pallas_call(
        forward_kernel,
        in_specs=[SMEM] * 4 + [HBM] * 2 + [VMEM],
        out_specs=[HBM, HBM],
        out_shape=[
            jax.ShapeDtypeStruct((768, 128), F32),
            jax.ShapeDtypeStruct((8, 256, 256), F32),
        ],
        scratch_shapes=[
            pltpu.VMEM((768, 128), F32),
            pltpu.VMEM((BX, ROWS, NY), F32),
            pltpu.VMEM((2, 256, 256), BF16),
            pltpu.VMEM((2, 256, 256), BF16),
            pltpu.VMEM((4, 256, 256), BF16),
            pltpu.VMEM((4, 256, 256), BF16),
            pltpu.VMEM((4, 512, 256), BF16),
            pltpu.VMEM((4, 512, 256), BF16),
            pltpu.VMEM((4, 512, 256), BF16),
            pltpu.VMEM((4, 512, 256), BF16),
            pltpu.VMEM((8, 256, 256), F32),
            pltpu.VMEM((3, 128, 256), F32),
            pltpu.SemaphoreType.DMA((2, 8)),
            pltpu.SemaphoreType.DMA((4,)),
            pltpu.SemaphoreType.DMA((4,)),
        ],
        name="forward",
        **kw,
    )(levels, neighbours, sweeps, mode, x, *constants())


def run_prepare(device, w, **kw):
    zbasis = np.stack([t for table in (ZBASIS, ZBASIS.T) for t in two_terms(table)])
    wide = np.ones((1, 128))
    numbers = np.concatenate(
        (
            LINK_SCALE, LINK_LAMBDA, ZSUM * wide, LZ[:, None] * wide,
            np.tile(LX[IX], 4)[None, :] * np.ones((8, 1)),
        )
    )
    shapes = [((Z_SUM + 128, 128), F32), ((2048, 128), BF16), (w.shape, F32)]
    return pl.pallas_call(
        prepare_kernel,
        grid_spec=pltpu.PrefetchScalarGridSpec(
            num_scalar_prefetch=1,
            grid=(1,),
            in_specs=[
                HBM,
                pl.BlockSpec((1, 1, 128), lambda i, own: (own[0], 0, 0)),
                whole(numbers.shape),
                whole(zbasis.shape),
            ],
            out_specs=[VMEM] * len(shapes),
            scratch_shapes=[pltpu.SemaphoreType.DMA],
        ),
        out_shape=[jax.ShapeDtypeStruct(*shape) for shape in shapes],
        compiler_params=GRANT,
        name="prepare",
        **kw,
    )(device, w, jnp.asarray(KQ_OWN, F32), jnp.asarray(numbers, F32), jnp.asarray(zbasis))


def run_columns(inbox, numbers, terms, **kw):
    return pl.pallas_call(
        column_kernel,
        in_specs=[VMEM] * 3,
        out_specs=VMEM,
        scratch_shapes=[
            pltpu.VMEM((256, 256), F32),
            pltpu.VMEM((128, 256), F32),
            pltpu.VMEM((128, 256), F32),
            pltpu.VMEM((2, 128, 256), BF16),
        ],
        out_shape=jax.ShapeDtypeStruct((768, 128), F32),
        compiler_params=GRANT,
        name="columns",
        **kw,
    )(inbox, numbers, terms)


def run_backward(levels, inbox, w, **kw):
    return pl.pallas_call(
        backward_kernel,
        in_specs=[SMEM] + [VMEM] * 4,
        out_specs=HBM,
        out_shape=jax.ShapeDtypeStruct((BX, ROWS, NY), F32),
        scratch_shapes=[
            pltpu.VMEM((3, 128, 256), F32),
            pltpu.VMEM((4, 512, 256), F32),
            pltpu.VMEM((BX, ROWS, NY), F32),
            pltpu.SemaphoreType.DMA((6,)),
        ],
        compiler_params=GRANT,
        name="backward",
        **kw,
    )(levels, inbox, w, *constants())


def traded(outbox):
    pieces = outbox.reshape(DEVICES, 1, 384)
    pieces = lax.all_to_all(pieces, ("blk", "mode"), split_axis=0, concat_axis=0, tiled=True)
    return pieces.reshape(3 * DEVICES, 128)


def body(divergence, neighbours, levels, sweeps):
    mode = lax.axis_index("mode").astype(jnp.int32)
    device = lax.axis_index("blk").astype(jnp.int32) * BLOCKS + mode
    outbox, w = run_forward(levels, neighbours, sweeps, mode[None], divergence[0])
    numbers, terms, w = run_prepare(device[None], w)
    outbox = run_columns(traded(outbox), numbers, terms)
    return run_backward(levels, traded(outbox), w)[None]


def solution(mesh):
    return jax.shard_map(
        body,
        mesh=mesh,
        in_specs=(P("blk", None, "mode", None), P("blk", None), P("blk"), P()),
        out_specs=P("blk", None, "mode", None),
        check_vma=False,
    )
```
